32 devices in a mesh: lon: 8 (over y, x, core), depth: 4 (over z).
Axes of the slice: x: 2, y: 2, z: 4, core: 2. Of those that a mesh axis runs over, the one named last changes fastest.
Arguments:
- innovations: float32 [5, 256, 128, 256], P(None, 'depth', 'lon'), may hold values from -6 to 6
- courant: float32 [3, 256, 128, 256], P(None, 'depth', 'lon'), may hold values from -0.3 to 0.3
- diffusivity: float32 [256, 128, 256], P('depth', 'lon'), may hold values from 0.05 to 0.12
- sea_bricks: int32 [256, 8, 128], P('depth', 'lon'), may hold values 0 or 1
- tile_ranks: int32 [8, 8], P('lon'), may hold values from 16 to 128
- row_factors: bfloat16 [8, 8, 4096, 128], P('lon', None, None, 'depth'), may hold values from -0.09375 to 0.09375
- column_factors: bfloat16 [8, 8, 4096, 128], P('lon', None, None, 'depth'), may hold values from -0.25 to 0.25
Outputs:
- initial_adjoint: float32 [256, 128, 256], P('depth', 'lon')
- gradient: float32 [256, 128, 256], P('depth', 'lon')
The draws below stay inside these ranges and needn't reach their ends.
All inputs are finite; a program needn't handle non-finite values. No bound on the sum of `sea_bricks` on one device may be relied on, other than what follows from the above.
Results may differ from the reference program's by a relative error of at most 0.0041.
Values may be sent and summed in bfloat16 or wider, within the bound.
No kernel may reach another device: no remote copies, remote signals or barrier semaphores. Data moves between devices by JAX's collectives and lax.ppermute only.
A program may use at most 64 MiB of HBM per device.

```python
import math
import jax
import jax.numpy as jnp
from jax import lax

TILE = 4096
RMAX = 128
NB = 8
STEPS = 4
NY = 256
CX = 16
NX = 128
NZ = 256
N_LON = 8


def set_ends(array, rng, least, largest):
    shape = array.shape
    index_at = [jax.random.randint(jax.random.fold_in(rng, axis), (), 0, shape[axis]) for axis in range(len(shape))]
    array = array.at[tuple(index_at)].set(least)
    longest = shape.index(max(shape))
    index_at[longest] = (index_at[longest] + 1) % shape[longest]
    return array.at[tuple(index_at)].set(largest)


def levels(key, extent, pieces, smallest, high):
    def one(axis_at, shards_of):
        heights = jax.random.uniform(jax.random.fold_in(jax.random.fold_in(key, 6), axis_at), (shards_of,), jnp.float32, smallest / len(pieces), high / len(pieces))
        return jnp.repeat(jnp.exp(heights), extent[axis_at] // shards_of).reshape((-1,) + (1,) * (len(extent) - axis_at - 1))

    loudness = one(*pieces[0])
    for cut in pieces[1:]:
        loudness = loudness * one(*cut)
    return loudness


def scatter_about(rng, dims, deviation, limit, cuts=(), held_as=jnp.bfloat16):
    factor_of = levels(rng, dims, cuts, -0.22, 0.18) if cuts else 1.0
    array = jax.random.normal(rng, dims, jnp.float32) * deviation * factor_of
    return jnp.minimum(jnp.maximum(array, -limit), limit).astype(held_as)


def setup_inputs(seed: int = 0) -> dict:
    streams_of = jax.random.split(jax.random.key(seed), 8)
    return {
        "innovations": scatter_about(streams_of[0], (STEPS + 1, NZ, NX, NY), 1.0, 6.0, ((1, 4), (2, 8)), jnp.float32),
        "courant": jnp.clip(jax.random.uniform(streams_of[1], (3, NZ, NX, NY), jnp.float32, -0.3, 0.3) * levels(streams_of[1], (3, NZ, NX, NY), ((1, 4), (2, 8)), -0.4, 0.0), -0.3, 0.3),
        "diffusivity": jnp.clip(jnp.exp(math.log(0.12) - 0.8754687 * jax.random.uniform(streams_of[2], (NZ, NX, NY), jnp.float32) ** levels(streams_of[2], (NZ, NX, NY), ((0, 4), (1, 8)), -0.2, 0.2)), 0.05, 0.12),
        "sea_bricks": set_ends((jax.random.randint(streams_of[3], (NZ, N_LON, NY // 2), 0, 4) < 3).astype(jnp.int32), jax.random.fold_in(streams_of[3], 1), 0, 1),
        "tile_ranks": set_ends(jax.random.randint(streams_of[4], (N_LON, NB), 16, 129), jax.random.fold_in(streams_of[4], 1), 16, 128).astype(jnp.int32),
        "row_factors": scatter_about(streams_of[5], (N_LON, NB, TILE, RMAX), TILE ** -0.5, 0.09375, ((0, 8), (3, 4))),
        "column_factors": scatter_about(streams_of[6], (N_LON, NB, TILE, RMAX), (RMAX * NB // 2) ** -0.5, 0.25, ((0, 8), (3, 4))),
    }


def lat_terms(plus_term, minus_term):
    lower = jnp.pad(plus_term[:, :, :-1], ((0, 0), (0, 0), (1, 0)))
    upper = jnp.pad(minus_term[:, :, 1:], ((0, 0), (0, 0), (0, 1)))
    return lower + upper


def adjoint_apply(lam, plus, minus, center):
    plus_term = plus * lam
    minus_term = minus * lam
    out = center * lam
    out = out + jnp.pad(plus_term[0][:-1], ((1, 0), (0, 0), (0, 0)))
    out = out + jnp.pad(minus_term[0][1:], ((0, 1), (0, 0), (0, 0)))
    out = out + jnp.roll(plus_term[1], 1, axis=1) + jnp.roll(minus_term[1], -1, axis=1)
    return out + lat_terms(plus_term[2], minus_term[2])


def row_coeffs(args):
    block, factors, ranks = args
    coeff = jnp.einsum('zt,ktr->kzr', block.astype(jnp.float32), factors.astype(jnp.float32))
    columns = jnp.arange(RMAX, dtype=jnp.int32)
    keep = (columns[None, :] < ranks[:, None]).astype(jnp.float32)
    return (coeff * keep[:, None, :]).astype(jnp.bfloat16)


def column_sum(args):
    received, factors = args
    return jnp.einsum('kzr,ktr->zt', received.astype(jnp.float32), factors.astype(jnp.float32))


def reference(innovations, courant, diffusivity, sea_bricks, tile_ranks, row_factors, column_factors):
    sea = sea_bricks.astype(jnp.float32)
    sea = jnp.broadcast_to(sea[:, :, None, :, None], (NZ, N_LON, CX, NY // 2, 2)).reshape(NZ, NX, NY)
    plus = diffusivity[None] - 0.5 * courant
    minus = diffusivity[None] + 0.5 * courant
    center = 1.0 - 6.0 * diffusivity
    lam = sea * innovations[STEPS]
    for step in reversed(range(STEPS)):
        lam = sea * (adjoint_apply(lam, plus, minus, center) + innovations[step])
    blocks = lam.astype(jnp.bfloat16).reshape(NZ, N_LON, TILE).transpose(1, 0, 2)
    coeff = lax.map(row_coeffs, (blocks, row_factors, tile_ranks))
    received = jnp.stack([jnp.roll(coeff[:, k], k - NB // 2, axis=0) for k in range(NB)], axis=1)
    sums = lax.map(column_sum, (received, column_factors))
    gradient = sums.transpose(1, 0, 2).reshape(NZ, NX, NY)
    return lam, gradient
```

```python
import jax
import jax.numpy as jnp
from jax import lax
from jax.sharding import PartitionSpec as P


def from_behind(value, axis, steps):
    count = lax.axis_size(axis)
    initial, last = (max(0, -steps), min(count, count - steps))
    return lax.ppermute(value, axis, [(source, source + steps) for source in range(initial, last)])


def shifted(block, axis, distance):
    devices = range(lax.axis_size(axis))
    route = [((i - distance) % len(devices), i) for i in devices]
    return lax.ppermute(block, axis, route)


def swapped(block, axis, mask):
    return lax.ppermute(block, axis, [(i, i ^ mask) for i in range(lax.axis_size(axis))])


def lat_terms(plus_term, minus_term):
    lower = jnp.pad(plus_term[:, :, :-1], ((0, 0), (0, 0), (1, 0)))
    upper = jnp.pad(minus_term[:, :, 1:], ((0, 0), (0, 0), (0, 1)))
    return lower + upper


def per_device(
    innovations, courant, diffusivity, sea_bricks, tile_ranks, row_factors, column_factors
):
    levels_here, lon_cells, lat_cells = diffusivity.shape
    tile_cols = lon_cells * lat_cells
    half = tile_cols // 2
    blocks_row = tile_ranks.shape[1]
    count = lax.axis_size("depth")
    me = lax.axis_index("depth")
    side = me % 2
    left = row_factors[0].transpose(0, 2, 1)
    right = column_factors[0].transpose(0, 2, 1)
    width = left.shape[1]

    def split(array, axis):
        mine = lax.dynamic_slice_in_dim(array, side * half, half, axis)
        other = lax.dynamic_slice_in_dim(array, (1 - side) * half, half, axis)
        return mine, other

    left_mine, left_other = split(left, 2)
    right_mine, right_other = split(right, 2)

    sea = sea_bricks.astype(jnp.float32)
    sea = jnp.broadcast_to(sea[:, :, :, None], (levels_here, 1, lat_cells // 2, 2)).reshape(
        levels_here, 1, lat_cells
    )
    plus = diffusivity[None] - 0.5 * courant
    minus = diffusivity[None] + 0.5 * courant
    center = 1.0 - 6.0 * diffusivity
    steps_total = innovations.shape[0] - 1
    lam = sea * innovations[steps_total]
    for step in reversed(range(steps_total)):
        plus_term = plus * lam
        minus_term = minus * lam
        below = from_behind(plus_term[0, -1:], "depth", 1)
        above = from_behind(minus_term[0, :1], "depth", -1)
        west = shifted(plus_term[1][:, -1:], "lon", 1)
        east = shifted(minus_term[1][:, :1], "lon", -1)
        if step == steps_total - 1:
            left_pair = swapped(left_other, "depth", 1)
            right_pair = swapped(right_other, "depth", 1)
        out = center * lam
        out = out + jnp.concatenate([below, plus_term[0, :-1]], 0)
        out = out + jnp.concatenate([minus_term[0, 1:], above], 0)
        out = out + jnp.concatenate([west, plus_term[1][:, :-1]], 1)
        out = out + jnp.concatenate([minus_term[1][:, 1:], east], 1)
        lam = sea * (out + lat_terms(plus_term[2], minus_term[2]) + innovations[step])
    lam_half = lam.astype(jnp.bfloat16).reshape(levels_here, tile_cols)
    lam_mine, lam_other = split(lam_half, 1)
    blocks = [lam_mine]
    for mask in range(1, count):
        blocks.append(swapped(lam_other if mask % 2 else lam_mine, "depth", mask))
    partial = [
        [
            jnp.einsum("zt,krt->krz", block, factor, preferred_element_type=jnp.float32)
            for factor in (left_mine, left_pair)
        ]
        for block in blocks
    ]
    sent = jnp.concatenate(
        [jnp.stack([partial[s ^ 1][1], partial[s ^ 1][0]], 1) for s in range(count)], 3
    ).astype(jnp.bfloat16)
    kept = jnp.concatenate([jnp.stack(partial[s], 1) for s in range(count)], 3)
    coeff = kept + swapped(sent, "depth", 1).astype(jnp.float32)
    ranks = tile_ranks[0]
    owner = jnp.stack([me, me ^ 1])
    columns = owner[:, None] * width + jnp.arange(width, dtype=jnp.int32)[None, :]
    keep = columns[None] < ranks[:, None, None]
    coeff = jnp.where(keep[:, :, :, None], coeff, 0.0).astype(jnp.bfloat16)
    received = jnp.stack(
        [shifted(coeff[k], "lon", k - blocks_row // 2) for k in range(blocks_row)], 0
    )
    sums = [
        jnp.einsum("krz,krt->zt", levels[:, 0], right_mine, preferred_element_type=jnp.float32)
        + jnp.einsum("krz,krt->zt", levels[:, 1], right_pair, preferred_element_type=jnp.float32)
        for levels in jnp.split(received, count, 3)
    ]
    arrived = [
        swapped(sums[mask].astype(jnp.bfloat16), "depth", mask) for mask in range(1, count)
    ]
    grad_mine = sums[0]
    for mask in range(2, count, 2):
        grad_mine = grad_mine + arrived[mask - 1].astype(jnp.float32)
    grad_other = arrived[0].astype(jnp.float32)
    for mask in range(3, count, 2):
        grad_other = grad_other + arrived[mask - 1].astype(jnp.float32)
    low = jnp.where(side == 0, grad_mine, grad_other)
    high = jnp.where(side == 0, grad_other, grad_mine)
    gradient = jnp.concatenate([low, high], 1)
    return (lam, gradient.reshape(levels_here, lon_cells, lat_cells))


def solution(mesh):
    placed = (
        P(None, "depth", "lon", None),
        P(None, "depth", "lon", None),
        P("depth", "lon", None),
        P("depth", "lon", None),
        P("lon", None),
        P("lon", None, None, "depth"),
        P("lon", None, None, "depth"),
    )
    return jax.shard_map(
        per_device,
        mesh=mesh,
        in_specs=placed,
        out_specs=(P("depth", "lon", None), P("depth", "lon", None)),
        check_vma=False,
    )
```

```python
import functools
import jax
import jax.numpy as jnp
from jax import lax
from jax.experimental import pallas as pl
from jax.experimental.pallas import tpu as pltpu
from jax.sharding import PartitionSpec as P

UNROLL = 3
LANES = 128
GRANT = 4 << 20
VMEM = pl.BlockSpec(memory_space=pltpu.VMEM)


def from_behind(value, axis, steps):
    count = lax.axis_size(axis)
    initial, last = (max(0, -steps), min(count, count - steps))
    return lax.ppermute(value, axis, [(source, source + steps) for source in range(initial, last)])


def shifted(block, axis, distance):
    devices = range(lax.axis_size(axis))
    if distance % len(devices) == 0:
        return block
    route = [((i - distance) % len(devices), i) for i in devices]
    return lax.ppermute(block, axis, route)


def swapped(block, axis, mask):
    return lax.ppermute(block, axis, [(i, i ^ mask) for i in range(lax.axis_size(axis))])


def halo_table(depth):
    order, at = {}, 0
    for name, extent in (
        [(("innov", k), k) for k in range(depth, 0, -1)]
        + [("diff", depth), ("c0", depth), ("c1", depth - 1), ("c2", depth - 1)]
    ):
        for distance in range(1, extent + 1):
            order[name, distance] = at
            at += 1
    order["sea"] = at
    return order, at + 1


def pack_kernel(table, innov_lo, innov_hi, cour_lo, cour_hi, diff_lo, diff_hi, sea_lo, sea_hi, down, up):
    depth = diff_lo.shape[0]

    def fill(out, innov, cour, diff, sea, level):
        for key, at in table.items():
            if key == "sea":
                rows = [sea[level(d)] for d in range(1, depth + 1)]
                rows.append(jnp.zeros((out.shape[1] - depth, out.shape[2]), jnp.float32))
                value = jnp.concatenate(rows, 0)
            else:
                name, distance = key
                z = level(distance)
                if name == "diff":
                    value = diff[z]
                elif name == "c0":
                    value = cour[0, z]
                elif name == "c1":
                    value = cour[1, z]
                elif name == "c2":
                    value = cour[2, z]
                else:
                    value = innov[name[1], z]
            out[at] = value.astype(jnp.bfloat16)

    fill(down, innov_hi, cour_hi, diff_hi, sea_hi, lambda d: depth - d)
    fill(up, innov_lo, cour_lo, diff_lo, sea_lo, lambda d: d - 1)


def first_kernel(table, innov, cour, diff, sea, before, after, sea_ext, east_gain, west_gain, to_east, to_west):
    steps = innov.shape[0] - 1
    levels, lon_cells, lat_cells = diff.shape
    last = lon_cells - 1

    def put(at, sea_row, diff_a, diff_b, cour_a, cour_b, innov_a, innov_b):
        sea_ext[at] = sea_row
        low_row, high_row = sea_row * innov_a, sea_row * innov_b
        west = diff_a + 0.5 * cour_a
        east = diff_b - 0.5 * cour_b
        west_gain[at], east_gain[at] = west, east
        to_west[at], to_east[at] = west * low_row, east * high_row

    for halo, where in ((before, lambda d: steps - d), (after, lambda d: steps + levels + d - 1)):
        sea_rows = halo[table["sea"]].astype(jnp.float32)
        for d in range(1, steps + 1):
            sea_row = sea_rows[d - 1 : d]
            at = where(d)
            if d == steps:
                zero = jnp.zeros((1, lat_cells), jnp.float32)
                sea_ext[at] = sea_row
                west_gain[at], east_gain[at], to_west[at], to_east[at] = zero, zero, zero, zero
            else:
                dd = halo[table["diff", d]].astype(jnp.float32)
                cc = halo[table["c1", d]].astype(jnp.float32)
                ii = halo[table[("innov", steps), d]].astype(jnp.float32)
                put(at, sea_row, dd[:1], dd[last:], cc[:1], cc[last:], ii[:1], ii[last:])

    def one(z, carry):
        edge = lambda ref: (ref[z, :1], ref[z, last:])
        put(z + steps, sea[z], *edge(diff), *edge(cour.at[1]), *edge(innov.at[steps]))
        return carry

    lax.fori_loop(0, levels, one, 0, unroll=4)


def step_kernel(table, step, innov, cour, diff, sea_ext, before, after, low, high, *rest):
    steps = innov.shape[0] - 1
    levels, lon_cells, lat_cells = diff.shape
    if step > 1:
        lam, rest = rest[0], rest[1:]
    out, out_low, out_high = rest
    last = lon_cells - 1
    x_at = lax.broadcasted_iota(jnp.int32, (lon_cells, lat_cells), 0)
    y_at = lax.broadcasted_iota(jnp.int32, (lon_cells, lat_cells), 1)
    first_x, last_x = x_at == 0, x_at == last
    first_y, last_y = y_at == 0, y_at == lat_cells - 1
    reach = steps - step

    def halo_level(halo, d, name):
        return halo[table[name, d]].astype(jnp.float32)

    def state(at, innovation):
        if step == 1:
            return sea_ext[at] * innovation
        value = jnp.where(first_x, low[at], lam[at])
        return jnp.where(last_x, high[at], value)

    def finish(at, acc, up_flux):
        value = sea_ext[at] * (acc + up_flux)
        out[at] = value
        out_low[at] = value[:1]
        out_high[at] = value[last:]

    def depth_terms(a, d, c):
        spread, drift = d * a, c * (0.5 * a)
        return spread - drift, spread + drift

    def level(a, d, c0, c1, c2, innovation):
        half = 0.5 * a
        spread = d * a
        drift = c0 * half
        plus0, minus0 = spread - drift, spread + drift
        drift = c1 * half
        plus1, minus1 = spread - drift, spread + drift
        drift = c2 * half
        plus2, minus2 = spread - drift, spread + drift
        acc = a - 6.0 * spread + innovation
        acc = acc + jnp.where(first_x, 0.0, pltpu.roll(plus1, 1, 0))
        acc = acc + jnp.where(last_x, 0.0, pltpu.roll(minus1, lon_cells - 1, 0))
        acc = acc + jnp.where(first_y, 0.0, pltpu.roll(plus2, 1, 1))
        acc = acc + jnp.where(last_y, 0.0, pltpu.roll(minus2, lat_cells - 1, 1))
        return acc, plus0, minus0

    def halo_full(halo, d, at):
        a = state(at, halo_level(halo, d, ("innov", steps)))
        return level(
            a,
            halo_level(halo, d, "diff"),
            halo_level(halo, d, "c0"),
            halo_level(halo, d, "c1"),
            halo_level(halo, d, "c2"),
            halo_level(halo, d, ("innov", steps - step)),
        )

    def halo_edge(halo, d, at):
        a = state(at, halo_level(halo, d, ("innov", steps)))
        return depth_terms(a, halo_level(halo, d, "diff"), halo_level(halo, d, "c0"))

    down_flux, _ = halo_edge(before, reach + 1, steps - reach - 1)
    acc = None
    for d in range(reach, 0, -1):
        at = steps - d
        value, plus0, minus0 = halo_full(before, d, at)
        if acc is not None:
            finish(at - 1, acc, minus0)
        acc, down_flux = value + down_flux, plus0

    def own(z):
        a = state(z + steps, innov[steps, z])
        return level(a, diff[z], cour[0, z], cour[1, z], cour[2, z], innov[steps - step, z])

    value, plus0, minus0 = own(0)
    if acc is not None:
        finish(steps - 1, acc, minus0)
    carry = (value + down_flux, plus0)

    def one(z, carry):
        acc, down_flux = carry
        value, plus0, minus0 = own(z)
        finish(z + steps - 1, acc, minus0)
        return value + down_flux, plus0

    head = (levels - 1) % UNROLL
    for z in range(1, 1 + head):
        carry = one(z, carry)

    def several(i, carry):
        for u in range(UNROLL):
            carry = one(1 + head + i * UNROLL + u, carry)
        return carry

    acc, down_flux = lax.fori_loop(0, (levels - 1) // UNROLL, several, carry)
    at = steps + levels - 1
    for d in range(1, reach + 1):
        value, plus0, minus0 = halo_full(after, d, at + d)
        finish(at + d - 1, acc, minus0)
        acc, down_flux = value + down_flux, plus0
    _, up_flux = halo_edge(after, reach + 1, at + reach + 1)
    finish(at + reach, acc, up_flux)


def last_kernel(side, lam, low, high, out, mine, other, *rows):
    levels, lon_cells, lat_cells = out.shape
    steps = (lam.shape[0] - levels) // 2
    x_at = lax.broadcasted_iota(jnp.int32, (lon_cells, lat_cells), 0)
    first_x, last_x = x_at == 0, x_at == lon_cells - 1

    def one(z, carry):
        value = jnp.where(first_x, low[z + steps], lam[z + steps])
        value = jnp.where(last_x, high[z + steps], value)
        out[z] = value
        for c, lanes in enumerate(rows):
            at = pl.multiple_of(z * lon_cells, lon_cells)
            lanes[pl.ds(at, lon_cells), :] = value[:, c * LANES : (c + 1) * LANES]
        return carry

    lax.fori_loop(0, levels, one, 0, unroll=4)
    half = lon_cells // 2
    for part, start in ((mine, side[0] * half), (other, (1 - side[0]) * half)):
        for x in range(half):
            for c, lanes in enumerate(rows):
                picked = lanes[pl.ds(start + x, levels, stride=lon_cells), :]
                at = x * lat_cells + c * LANES
                part[:, at : at + LANES] = picked.astype(jnp.bfloat16)


def face_kernel(sea_ext, out_low, out_high, west, east, west_gain, east_gain, low, high, to_west, to_east):
    low_rows = out_low[...] + sea_ext[...] * west[...]
    high_rows = out_high[...] + sea_ext[...] * east[...]
    low[...], high[...] = low_rows, high_rows
    to_west[...], to_east[...] = west_gain[...] * low_rows, east_gain[...] * high_rows


def sweep(innovations, courant, diffusivity, sea, side):
    levels, lon_cells, lat_cells = diffusivity.shape
    steps = innovations.shape[0] - 1
    table, layers = halo_table(steps)
    f32, bf16 = jnp.float32, jnp.bfloat16
    end = levels // steps - 1

    def edges(shape, axis):
        block = list(shape)
        block[axis] = steps
        at = lambda index: lambda i: tuple(index if a == axis else 0 for a in range(len(shape)))
        return [pl.BlockSpec(tuple(block), at(index)) for index in (0, end)]

    message = jax.ShapeDtypeStruct((layers, lon_cells, lat_cells), bf16)
    down, up = pl.pallas_call(
        functools.partial(pack_kernel, table),
        grid=(1,),
        in_specs=edges(innovations.shape, 1)
        + edges(courant.shape, 1)
        + edges(diffusivity.shape, 0)
        + edges(sea.shape, 0),
        out_shape=[message, message],
        out_specs=[VMEM, VMEM],
        compiler_params=pltpu.CompilerParams(vmem_limit_bytes=GRANT),
        cost_estimate=pl.CostEstimate(flops=0, bytes_accessed=1 << 20, transcendentals=0),
    )(innovations, innovations, courant, courant, diffusivity, diffusivity, sea, sea)
    before = from_behind(down, "depth", 1)
    after = from_behind(up, "depth", -1)
    row = jax.ShapeDtypeStruct((levels + 2 * steps, 1, lat_cells), f32)
    cells = jax.ShapeDtypeStruct((levels + 2 * steps, lon_cells, lat_cells), f32)
    inputs = (innovations, courant, diffusivity)
    sea_ext, east_gain, west_gain, to_east, to_west = pl.pallas_call(
        functools.partial(first_kernel, table),
        in_specs=[VMEM] * 6,
        out_shape=[row] * 5,
        out_specs=[VMEM] * 5,
        compiler_params=pltpu.CompilerParams(vmem_limit_bytes=GRANT),
        cost_estimate=pl.CostEstimate(flops=0, bytes_accessed=1 << 20, transcendentals=0),
    )(*inputs, sea, before, after)
    lam = ()
    low = high = sea_ext
    for step in range(1, steps + 1):
        west = shifted(to_east, "lon", 1)
        east = shifted(to_west, "lon", -1)
        state = (low, high) + lam
        out, out_low, out_high = pl.pallas_call(
            functools.partial(step_kernel, table, step),
            in_specs=[VMEM] * (6 + len(state)),
            out_shape=[cells, row, row],
            out_specs=[VMEM] * 3,
            compiler_params=pltpu.CompilerParams(vmem_limit_bytes=GRANT),
        cost_estimate=pl.CostEstimate(flops=40 * levels * lon_cells * lat_cells, bytes_accessed=9 << 20, transcendentals=0),
        )(*inputs, sea_ext, before, after, *state)
        low, high, to_west, to_east = pl.pallas_call(
            face_kernel,
            in_specs=[VMEM] * 7,
            out_shape=[row] * 4,
            out_specs=[VMEM] * 4,
            compiler_params=pltpu.CompilerParams(vmem_limit_bytes=GRANT),
            cost_estimate=pl.CostEstimate(flops=0, bytes_accessed=1 << 19, transcendentals=0),
        )(sea_ext, out_low, out_high, west, east, west_gain, east_gain)
        lam = (out,)
    half = jax.ShapeDtypeStruct((levels, lon_cells * lat_cells // 2), bf16)
    return pl.pallas_call(
        last_kernel,
        in_specs=[pl.BlockSpec(memory_space=pltpu.SMEM)] + [VMEM] * 3,
        out_shape=[jax.ShapeDtypeStruct((levels, lon_cells, lat_cells), f32), half, half],
        out_specs=[VMEM] * 3,
        scratch_shapes=[pltpu.VMEM((levels * lon_cells, LANES), f32)] * (lat_cells // LANES),
        compiler_params=pltpu.CompilerParams(vmem_limit_bytes=GRANT),
        cost_estimate=pl.CostEstimate(flops=0, bytes_accessed=3 << 20, transcendentals=0),
    )(side.reshape(1), out, low, high)


def per_device(
    innovations, courant, diffusivity, sea_bricks, tile_ranks, row_factors, column_factors
):
    levels_here, lon_cells, lat_cells = diffusivity.shape
    tile_cols = lon_cells * lat_cells
    half = tile_cols // 2
    blocks_row = tile_ranks.shape[1]
    count = lax.axis_size("depth")
    me = lax.axis_index("depth")
    side = me % 2
    left = row_factors[0].transpose(0, 2, 1)
    right = column_factors[0].transpose(0, 2, 1)
    width = left.shape[1]

    def split(array, axis):
        mine = lax.dynamic_slice_in_dim(array, side * half, half, axis)
        other = lax.dynamic_slice_in_dim(array, (1 - side) * half, half, axis)
        return mine, other

    left_mine, left_other = split(left, 2)
    right_mine, right_other = split(right, 2)

    sea = sea_bricks.astype(jnp.float32)
    sea = jnp.broadcast_to(sea[:, :, :, None], (levels_here, 1, lat_cells // 2, 2)).reshape(
        levels_here, 1, lat_cells
    )
    lam, lam_mine, lam_other = sweep(innovations, courant, diffusivity, sea, side)
    left_pair = swapped(left_other, "depth", 1)
    right_pair = swapped(right_other, "depth", 1)
    blocks = [lam_mine]
    for mask in range(1, count):
        blocks.append(swapped(lam_other if mask % 2 else lam_mine, "depth", mask))
    partial = [
        [
            jnp.einsum("zt,krt->krz", block, factor, preferred_element_type=jnp.float32)
            for factor in (left_mine, left_pair)
        ]
        for block in blocks
    ]
    sent = jnp.concatenate(
        [jnp.stack([partial[s ^ 1][1], partial[s ^ 1][0]], 1) for s in range(count)], 3
    ).astype(jnp.bfloat16)
    kept = jnp.concatenate([jnp.stack(partial[s], 1) for s in range(count)], 3)
    coeff = kept + swapped(sent, "depth", 1).astype(jnp.float32)
    ranks = tile_ranks[0]
    owner = jnp.stack([me, me ^ 1])
    columns = owner[:, None] * width + jnp.arange(width, dtype=jnp.int32)[None, :]
    keep = columns[None] < ranks[:, None, None]
    coeff = jnp.where(keep[:, :, :, None], coeff, 0.0).astype(jnp.bfloat16)
    received = jnp.stack(
        [shifted(coeff[k], "lon", k - blocks_row // 2) for k in range(blocks_row)], 0
    )
    sums = [
        jnp.einsum("krz,krt->zt", levels[:, 0], right_mine, preferred_element_type=jnp.float32)
        + jnp.einsum("krz,krt->zt", levels[:, 1], right_pair, preferred_element_type=jnp.float32)
        for levels in jnp.split(received, count, 3)
    ]
    arrived = [
        swapped(sums[mask].astype(jnp.bfloat16), "depth", mask) for mask in range(1, count)
    ]
    grad_mine = sums[0]
    for mask in range(2, count, 2):
        grad_mine = grad_mine + arrived[mask - 1].astype(jnp.float32)
    grad_other = arrived[0].astype(jnp.float32)
    for mask in range(3, count, 2):
        grad_other = grad_other + arrived[mask - 1].astype(jnp.float32)
    low = jnp.where(side == 0, grad_mine, grad_other)
    high = jnp.where(side == 0, grad_other, grad_mine)
    gradient = jnp.concatenate([low, high], 1)
    return (lam, gradient.reshape(levels_here, lon_cells, lat_cells))


def solution(mesh):
    placed = (
        P(None, "depth", "lon", None),
        P(None, "depth", "lon", None),
        P("depth", "lon", None),
        P("depth", "lon", None),
        P("lon", None),
        P("lon", None, None, "depth"),
        P("lon", None, None, "depth"),
    )
    return jax.shard_map(
        per_device,
        mesh=mesh,
        in_specs=placed,
        out_specs=(P("depth", "lon", None), P("depth", "lon", None)),
        check_vma=False,
    )
```

```python
import functools
import jax
import jax.numpy as jnp
from jax import lax
from jax.experimental import pallas as pl
from jax.experimental.pallas import tpu as pltpu
from jax.sharding import PartitionSpec as P

UNROLL = 3
LANES = 128
GRANT = 4 << 20
VMEM = pl.BlockSpec(memory_space=pltpu.VMEM)
SMEM = pl.BlockSpec(memory_space=pltpu.SMEM)
ANY = pl.BlockSpec(memory_space=pl.ANY)


def from_behind(value, axis, steps):
    count = lax.axis_size(axis)
    initial, last = (max(0, -steps), min(count, count - steps))
    return lax.ppermute(value, axis, [(source, source + steps) for source in range(initial, last)])


def shifted(block, axis, distance):
    devices = range(lax.axis_size(axis))
    if distance % len(devices) == 0:
        return block
    route = [((i - distance) % len(devices), i) for i in devices]
    return lax.ppermute(block, axis, route)


def swapped(block, axis, mask):
    return lax.ppermute(block, axis, [(i, i ^ mask) for i in range(lax.axis_size(axis))])


def halo_table(depth):
    order, at = {}, 0
    for name, extent in (
        [(("innov", k), k) for k in range(depth, 0, -1)]
        + [("diff", depth), ("c0", depth), ("c1", depth - 1), ("c2", depth - 1)]
    ):
        for distance in range(1, extent + 1):
            order[name, distance] = at
            at += 1
    order["sea"] = at
    return order, at + 1


def pack_kernel(table, place, innov_lo, innov_hi, cour_lo, cour_hi, diff_lo, diff_hi, sea_lo, sea_hi, down, up, placed):
    for n in range(place.shape[0]):
        placed[n] = place[n]
    depth = diff_lo.shape[0]

    def fill(out, innov, cour, diff, sea, level):
        for key, at in table.items():
            if key == "sea":
                rows = [sea[level(d)] for d in range(1, depth + 1)]
                rows.append(jnp.zeros((out.shape[1] - depth, out.shape[2]), jnp.float32))
                value = jnp.concatenate(rows, 0)
            else:
                name, distance = key
                z = level(distance)
                if name == "diff":
                    value = diff[z]
                elif name == "c0":
                    value = cour[0, z]
                elif name == "c1":
                    value = cour[1, z]
                elif name == "c2":
                    value = cour[2, z]
                else:
                    value = innov[name[1], z]
            out[at] = value.astype(jnp.bfloat16)

    fill(down, innov_hi, cour_hi, diff_hi, sea_hi, lambda d: depth - d)
    fill(up, innov_lo, cour_lo, diff_lo, sea_lo, lambda d: d - 1)


def first_kernel(table, innov, cour, diff, sea, before, after, sea_ext, east_gain, west_gain, to_east, to_west):
    steps = innov.shape[0] - 1
    levels, lon_cells, lat_cells = diff.shape
    last = lon_cells - 1

    def put(at, sea_row, diff_a, diff_b, cour_a, cour_b, innov_a, innov_b):
        sea_ext[at] = sea_row
        low_row, high_row = sea_row * innov_a, sea_row * innov_b
        west = diff_a + 0.5 * cour_a
        east = diff_b - 0.5 * cour_b
        west_gain[at], east_gain[at] = west, east
        to_west[at], to_east[at] = west * low_row, east * high_row

    for halo, where in ((before, lambda d: steps - d), (after, lambda d: steps + levels + d - 1)):
        sea_rows = halo[table["sea"]].astype(jnp.float32)
        for d in range(1, steps + 1):
            sea_row = sea_rows[d - 1 : d]
            at = where(d)
            if d == steps:
                zero = jnp.zeros((1, lat_cells), jnp.float32)
                sea_ext[at] = sea_row
                west_gain[at], east_gain[at], to_west[at], to_east[at] = zero, zero, zero, zero
            else:
                dd = halo[table["diff", d]].astype(jnp.float32)
                cc = halo[table["c1", d]].astype(jnp.float32)
                ii = halo[table[("innov", steps), d]].astype(jnp.float32)
                put(at, sea_row, dd[:1], dd[last:], cc[:1], cc[last:], ii[:1], ii[last:])

    def one(z, carry):
        edge = lambda ref: (ref[z, :1], ref[z, last:])
        put(z + steps, sea[z], *edge(diff), *edge(cour.at[1]), *edge(innov.at[steps]))
        return carry

    lax.fori_loop(0, levels, one, 0, unroll=4)


def step_kernel(table, step, innov, cour, diff, sea_ext, before, after, low, high, *rest):
    steps = innov.shape[0] - 1
    levels, lon_cells, lat_cells = diff.shape
    if step > 1:
        lam, rest = rest[0], rest[1:]
    out, out_low, out_high = rest
    last = lon_cells - 1
    x_at = lax.broadcasted_iota(jnp.int32, (lon_cells, lat_cells), 0)
    y_at = lax.broadcasted_iota(jnp.int32, (lon_cells, lat_cells), 1)
    first_x, last_x = x_at == 0, x_at == last
    first_y, last_y = y_at == 0, y_at == lat_cells - 1
    reach = steps - step

    def halo_level(halo, d, name):
        return halo[table[name, d]].astype(jnp.float32)

    def state(at, innovation):
        if step == 1:
            return sea_ext[at] * innovation
        value = jnp.where(first_x, low[at], lam[at])
        return jnp.where(last_x, high[at], value)

    def finish(at, acc, up_flux):
        value = sea_ext[at] * (acc + up_flux)
        out[at] = value
        out_low[at] = value[:1]
        out_high[at] = value[last:]

    def depth_terms(a, d, c):
        spread, drift = d * a, c * (0.5 * a)
        return spread - drift, spread + drift

    def level(a, d, c0, c1, c2, innovation):
        half = 0.5 * a
        spread = d * a
        drift = c0 * half
        plus0, minus0 = spread - drift, spread + drift
        drift = c1 * half
        plus1, minus1 = spread - drift, spread + drift
        drift = c2 * half
        plus2, minus2 = spread - drift, spread + drift
        acc = a - 6.0 * spread + innovation
        acc = acc + jnp.where(first_x, 0.0, pltpu.roll(plus1, 1, 0))
        acc = acc + jnp.where(last_x, 0.0, pltpu.roll(minus1, lon_cells - 1, 0))
        acc = acc + jnp.where(first_y, 0.0, pltpu.roll(plus2, 1, 1))
        acc = acc + jnp.where(last_y, 0.0, pltpu.roll(minus2, lat_cells - 1, 1))
        return acc, plus0, minus0

    def halo_full(halo, d, at):
        a = state(at, halo_level(halo, d, ("innov", steps)))
        return level(
            a,
            halo_level(halo, d, "diff"),
            halo_level(halo, d, "c0"),
            halo_level(halo, d, "c1"),
            halo_level(halo, d, "c2"),
            halo_level(halo, d, ("innov", steps - step)),
        )

    def halo_edge(halo, d, at):
        a = state(at, halo_level(halo, d, ("innov", steps)))
        return depth_terms(a, halo_level(halo, d, "diff"), halo_level(halo, d, "c0"))

    down_flux, _ = halo_edge(before, reach + 1, steps - reach - 1)
    acc = None
    for d in range(reach, 0, -1):
        at = steps - d
        value, plus0, minus0 = halo_full(before, d, at)
        if acc is not None:
            finish(at - 1, acc, minus0)
        acc, down_flux = value + down_flux, plus0

    def own(z):
        a = state(z + steps, innov[steps, z])
        return level(a, diff[z], cour[0, z], cour[1, z], cour[2, z], innov[steps - step, z])

    value, plus0, minus0 = own(0)
    if acc is not None:
        finish(steps - 1, acc, minus0)
    carry = (value + down_flux, plus0)

    def one(z, carry):
        acc, down_flux = carry
        value, plus0, minus0 = own(z)
        finish(z + steps - 1, acc, minus0)
        return value + down_flux, plus0

    head = (levels - 1) % UNROLL
    for z in range(1, 1 + head):
        carry = one(z, carry)

    def several(i, carry):
        for u in range(UNROLL):
            carry = one(1 + head + i * UNROLL + u, carry)
        return carry

    acc, down_flux = lax.fori_loop(0, (levels - 1) // UNROLL, several, carry)
    at = steps + levels - 1
    for d in range(1, reach + 1):
        value, plus0, minus0 = halo_full(after, d, at + d)
        finish(at + d - 1, acc, minus0)
        acc, down_flux = value + down_flux, plus0
    _, up_flux = halo_edge(after, reach + 1, at + reach + 1)
    finish(at + reach, acc, up_flux)


def last_kernel(place, lam, low, high, out, mine, other, *rows):
    levels, lon_cells, lat_cells = out.shape
    steps = (lam.shape[0] - levels) // 2
    x_at = lax.broadcasted_iota(jnp.int32, (lon_cells, lat_cells), 0)
    first_x, last_x = x_at == 0, x_at == lon_cells - 1

    def one(z, carry):
        value = jnp.where(first_x, low[z + steps], lam[z + steps])
        value = jnp.where(last_x, high[z + steps], value)
        out[z] = value
        for c, lanes in enumerate(rows):
            at = pl.multiple_of(z * lon_cells, lon_cells)
            lanes[pl.ds(at, lon_cells), :] = value[:, c * LANES : (c + 1) * LANES]
        return carry

    lax.fori_loop(0, levels, one, 0, unroll=4)
    half = lon_cells // 2
    for part, start in ((mine, place[1] * half), (other, (1 - place[1]) * half)):
        for x in range(half):
            for c, lanes in enumerate(rows):
                picked = lanes[pl.ds(start + x, levels, stride=lon_cells), :]
                at = x * lat_cells + c * LANES
                part[:, at : at + LANES] = picked.astype(jnp.bfloat16)


def face_kernel(sea_ext, out_low, out_high, west, east, west_gain, east_gain, low, high, to_west, to_east):
    low_rows = out_low[...] + sea_ext[...] * west[...]
    high_rows = out_high[...] + sea_ext[...] * east[...]
    low[...], high[...] = low_rows, high_rows
    to_west[...], to_east[...] = west_gain[...] * low_rows, east_gain[...] * high_rows


def pack(innovations, courant, diffusivity, sea, place):
    levels, lon_cells, lat_cells = diffusivity.shape
    steps = innovations.shape[0] - 1
    table, layers = halo_table(steps)
    bf16 = jnp.bfloat16
    end = levels // steps - 1

    def edges(shape, axis):
        block = list(shape)
        block[axis] = steps
        at = lambda index: lambda i: tuple(index if a == axis else 0 for a in range(len(shape)))
        return [pl.BlockSpec(tuple(block), at(index)) for index in (0, end)]

    message = jax.ShapeDtypeStruct((layers, lon_cells, lat_cells), bf16)
    down, up, place = pl.pallas_call(
        functools.partial(pack_kernel, table),
        grid=(1,),
        in_specs=[SMEM]
        + edges(innovations.shape, 1)
        + edges(courant.shape, 1)
        + edges(diffusivity.shape, 0)
        + edges(sea.shape, 0),
        out_shape=[message, message, jax.ShapeDtypeStruct(place.shape, place.dtype)],
        out_specs=[VMEM, VMEM, SMEM],
        compiler_params=pltpu.CompilerParams(vmem_limit_bytes=GRANT),
        cost_estimate=pl.CostEstimate(flops=0, bytes_accessed=1 << 20, transcendentals=0),
    )(place, innovations, innovations, courant, courant, diffusivity, diffusivity, sea, sea)
    return down, up, place


def sweep(innovations, courant, diffusivity, sea, down, up, place):
    levels, lon_cells, lat_cells = diffusivity.shape
    steps = innovations.shape[0] - 1
    table, _ = halo_table(steps)
    f32, bf16 = jnp.float32, jnp.bfloat16
    before = from_behind(down, "depth", 1)
    after = from_behind(up, "depth", -1)
    row = jax.ShapeDtypeStruct((levels + 2 * steps, 1, lat_cells), f32)
    cells = jax.ShapeDtypeStruct((levels + 2 * steps, lon_cells, lat_cells), f32)
    inputs = (innovations, courant, diffusivity)
    sea_ext, east_gain, west_gain, to_east, to_west = pl.pallas_call(
        functools.partial(first_kernel, table),
        in_specs=[VMEM] * 6,
        out_shape=[row] * 5,
        out_specs=[VMEM] * 5,
        compiler_params=pltpu.CompilerParams(vmem_limit_bytes=GRANT),
        cost_estimate=pl.CostEstimate(flops=0, bytes_accessed=1 << 20, transcendentals=0),
    )(*inputs, sea, before, after)
    lam = ()
    low = high = sea_ext
    for step in range(1, steps + 1):
        west = shifted(to_east, "lon", 1)
        east = shifted(to_west, "lon", -1)
        state = (low, high) + lam
        out, out_low, out_high = pl.pallas_call(
            functools.partial(step_kernel, table, step),
            in_specs=[VMEM] * (6 + len(state)),
            out_shape=[cells, row, row],
            out_specs=[VMEM] * 3,
            compiler_params=pltpu.CompilerParams(vmem_limit_bytes=GRANT),
        cost_estimate=pl.CostEstimate(flops=40 * levels * lon_cells * lat_cells, bytes_accessed=9 << 20, transcendentals=0),
        )(*inputs, sea_ext, before, after, *state)
        low, high, to_west, to_east = pl.pallas_call(
            face_kernel,
            in_specs=[VMEM] * 7,
            out_shape=[row] * 4,
            out_specs=[VMEM] * 4,
            compiler_params=pltpu.CompilerParams(vmem_limit_bytes=GRANT),
            cost_estimate=pl.CostEstimate(flops=0, bytes_accessed=1 << 19, transcendentals=0),
        )(sea_ext, out_low, out_high, west, east, west_gain, east_gain)
        lam = (out,)
    half = jax.ShapeDtypeStruct((levels, lon_cells * lat_cells // 2), bf16)
    return pl.pallas_call(
        last_kernel,
        in_specs=[SMEM] + [VMEM] * 3,
        out_shape=[jax.ShapeDtypeStruct((levels, lon_cells, lat_cells), f32), half, half],
        out_specs=[VMEM] * 3,
        scratch_shapes=[pltpu.VMEM((levels * lon_cells, LANES), f32)] * (lat_cells // LANES),
        compiler_params=pltpu.CompilerParams(vmem_limit_bytes=GRANT),
        cost_estimate=pl.CostEstimate(flops=0, bytes_accessed=3 << 20, transcendentals=0),
    )(place, out, low, high)


def halves_kernel(place, left, right, left_mine, left_other, right_mine, right_other, *scratch):
    half = left_mine.shape[2]
    side = place[1]
    vmem, sems = scratch
    jobs = []
    for source, mine, other in ((left, left_mine, left_other), (right, right_mine, right_other)):
        jobs.append((source, other, 1 - side))
        jobs.append((source, mine, side))
    loads, stores = [], []
    for n, (source, target, which) in enumerate(jobs):
        window = source.at[0, :, :, pl.ds(pl.multiple_of(which * half, half), half)]
        loads.append(pltpu.make_async_copy(window, vmem.at[n], sems.at[n]))
        loads[-1].start()
        stores.append(pltpu.make_async_copy(vmem.at[n], target, sems.at[len(jobs) + n]))
    for load, store in zip(loads, stores):
        load.wait()
        store.start()
    for store in stores:
        store.wait()


def against(a, b):
    return lax.dot_general(a, b, (((1,), (1,)), ((), ())), preferred_element_type=jnp.float32)


def rows_kernel(left_mine, left_pair, first, second, kept, sent):
    for c, factor in enumerate((left_mine, left_pair)):
        parts = [against(factor[...], block[...]) for block in (first, second)]
        kept[c] = jnp.concatenate(parts, 1)
        sent[1 - c] = jnp.concatenate(parts[::-1], 1).astype(jnp.bfloat16)


def mask_kernel(slots, place, ranks, kept, arrived, *out):
    rows = kept.shape[1] // slots
    for c in range(2):
        owner = place[0] if c == 0 else place[0] + 1 - 2 * place[1]
        for k in range(slots):
            at = slice(k * rows, (k + 1) * rows)
            value = kept[c, at, :] + arrived[c, at, :].astype(jnp.float32)
            row = lax.broadcasted_iota(jnp.int32, value.shape, 0) + owner * rows
            value = jnp.where(row < ranks[0, k], value, 0.0).astype(jnp.bfloat16)
            if len(out) > 1:
                out[k][c] = value
            else:
                count = out[0].shape[0]
                out[0][lax.rem(place[2] + (k - slots // 2 + count), count), c] = value


def columns_kernel(slots, wide, place, right_mine, right_pair, *rest):
    received, out = rest[:-2], rest[-2:]
    count = received[0].shape[0]
    total = None
    for c, factor in enumerate((right_mine, right_pair)):
        for k in range(slots):
            if len(received) > 1:
                coeff = received[k][c]
            else:
                coeff = received[0][lax.rem(place[2] + (count + slots // 2 - k), count), c]
            coeffs = [coeff] if k == 0 and c == 0 else coeffs + [coeff]
    stacked = jnp.concatenate(coeffs, 0)
    rows = right_mine.shape[0]
    lead = (((0,), (0,)), ((), ()))
    for at in range(0, right_mine.shape[1], wide):
        lanes = slice(at, at + wide)
        total = lax.dot_general(stacked[:rows], right_mine[:, lanes], lead, preferred_element_type=jnp.float32)
        total = total + lax.dot_general(stacked[rows:], right_pair[:, lanes], lead, preferred_element_type=jnp.float32)
        levels = out[0].shape[0]
        out[0][:, lanes] = total[:levels].astype(out[0].dtype)
        out[1][:, lanes] = total[levels:].astype(out[1].dtype)


def join_kernel(place, own, arrived1, arrived2, arrived3, out, *rows):
    levels, lon_cells, lat_cells = out.shape
    half = lon_cells // 2
    f32 = jnp.float32
    for x in range(half):
        for c, lanes in enumerate(rows):
            at = x * lat_cells + c * LANES
            cols = slice(at, at + LANES)
            mine = own[:, cols] + arrived2[:, cols].astype(f32)
            other = arrived1[:, cols].astype(f32) + arrived3[:, cols].astype(f32)
            lanes[pl.ds(place[1] * half + x, levels, stride=lon_cells), :] = mine
            lanes[pl.ds((1 - place[1]) * half + x, levels, stride=lon_cells), :] = other

    def one(z, carry):
        at = pl.multiple_of(z * lon_cells, lon_cells)
        for c, lanes in enumerate(rows):
            out[z, :, c * LANES : (c + 1) * LANES] = lanes[pl.ds(at, lon_cells), :]
        return carry

    lax.fori_loop(0, levels, one, 0, unroll=4)


def call(kernel, operands, in_specs, outs, grant=GRANT, flops=0, moved=1 << 20, scratch=()):
    return pl.pallas_call(
        kernel,
        in_specs=in_specs,
        out_shape=[jax.ShapeDtypeStruct(*o[:2]) for o in outs],
        out_specs=[o[2] if len(o) > 2 else VMEM for o in outs],
        scratch_shapes=list(scratch),
        compiler_params=pltpu.CompilerParams(vmem_limit_bytes=grant),
        cost_estimate=pl.CostEstimate(flops=flops, bytes_accessed=moved, transcendentals=0),
    )(*operands)


def per_device(
    innovations, courant, diffusivity, sea_bricks, tile_ranks, row_factors, column_factors
):
    levels, lon_cells, lat_cells = diffusivity.shape
    tile_cols = lon_cells * lat_cells
    half = tile_cols // 2
    slots = tile_ranks.shape[1]
    count = lax.axis_size("depth")
    lon_count = lax.axis_size("lon")
    f32, bf16 = jnp.float32, jnp.bfloat16
    me = lax.axis_index("depth")
    place = jnp.stack([me, me % 2, lax.axis_index("lon")]).astype(jnp.int32)
    left = row_factors.transpose(0, 1, 3, 2)
    right = column_factors.transpose(0, 1, 3, 2)
    width = left.shape[2]
    rows = slots * width

    sea = sea_bricks.astype(f32)
    sea = jnp.broadcast_to(sea[:, :, :, None], (levels, 1, lat_cells // 2, 2)).reshape(levels, 1, lat_cells)
    down, up, place = pack(innovations, courant, diffusivity, sea, place)
    part = (slots, width, half)
    left_mine, left_other, right_mine, right_other = call(
        halves_kernel,
        (place, left, right),
        [SMEM, ANY, ANY],
        [(part, bf16, ANY)] * 4,
        grant=8 << 20,
        moved=8 << 20,
        scratch=[pltpu.VMEM((4, slots, width, half), bf16), pltpu.SemaphoreType.DMA((8,))],
    )
    left_pair = swapped(left_other, "depth", 1)
    right_pair = swapped(right_other, "depth", 1)
    lam, lam_mine, lam_other = sweep(innovations, courant, diffusivity, sea, down, up, place)
    left_mine, left_pair, right_mine, right_pair = (
        a.reshape(rows, half) for a in (left_mine, left_pair, right_mine, right_pair)
    )
    blocks = {0: lam_mine}
    for mask in [1] + list(range(count - 1, 1, -1)):
        blocks[mask] = swapped(lam_other if mask % 2 else lam_mine, "depth", mask)
    arrived, own = {}, None
    for stage in range(0, count, 2):
        pair = (2, rows, 2 * levels)
        kept, sent = call(
            rows_kernel,
            (left_mine, left_pair, blocks[stage], blocks[stage + 1]),
            [VMEM] * 4,
            [(pair, f32), (pair, bf16)],
            flops=8 * rows * half * levels,
            moved=3 << 20,
        )
        other = swapped(sent, "depth", 1)
        grouped = lon_count == slots
        slot = (2, width, 2 * levels)
        outs = [((lon_count,) + slot, bf16)] if grouped else [(slot, bf16)] * slots
        coeff = call(
            functools.partial(mask_kernel, slots),
            (place, tile_ranks, kept, other),
            [SMEM, SMEM, VMEM, VMEM],
            outs,
        )
        if grouped:
            received = [lax.all_to_all(coeff[0], "lon", 0, 0, tiled=True)]
        else:
            received = [shifted(coeff[k], "lon", k - slots // 2) for k in range(slots)]
        block = (levels, half)
        first, second = call(
            functools.partial(columns_kernel, slots, 4 * LANES),
            (place, right_mine, right_pair, *received),
            [SMEM] + [VMEM] * (2 + len(received)),
            [(block, bf16 if stage else f32), (block, bf16)],
            flops=8 * rows * half * levels,
            moved=3 << 20,
        )
        if stage:
            arrived[stage] = swapped(first, "depth", stage)
        else:
            own = first
        arrived[stage + 1] = swapped(second, "depth", stage + 1)
    (gradient,) = call(
        join_kernel,
        (place, own, *(arrived[mask] for mask in range(1, count))),
        [SMEM] + [VMEM] * count,
        [((levels, lon_cells, lat_cells), f32)],
        scratch=[pltpu.VMEM((levels * lon_cells, LANES), f32)] * (lat_cells // LANES),
        moved=4 << 20,
    )
    return (lam, gradient)


def solution(mesh):
    placed = (
        P(None, "depth", "lon", None),
        P(None, "depth", "lon", None),
        P("depth", "lon", None),
        P("depth", "lon", None),
        P("lon", None),
        P("lon", None, None, "depth"),
        P("lon", None, None, "depth"),
    )
    return jax.shard_map(
        per_device,
        mesh=mesh,
        in_specs=placed,
        out_specs=(P("depth", "lon", None), P("depth", "lon", None)),
        check_vma=False,
    )
```

```python
import functools
import jax
import jax.numpy as jnp
from jax import lax
from jax.experimental import pallas as pl
from jax.experimental.pallas import tpu as pltpu
from jax.sharding import PartitionSpec as P

UNROLL = 3
LANES = 128
PARTS = 4
GRANT = 4 << 20
VMEM = pl.BlockSpec(memory_space=pltpu.VMEM)
SMEM = pl.BlockSpec(memory_space=pltpu.SMEM)
ANY = pl.BlockSpec(memory_space=pl.ANY)


def from_behind(value, axis, steps):
    count = lax.axis_size(axis)
    initial, last = (max(0, -steps), min(count, count - steps))
    return lax.ppermute(value, axis, [(source, source + steps) for source in range(initial, last)])


def shifted(block, axis, distance):
    devices = range(lax.axis_size(axis))
    if distance % len(devices) == 0:
        return block
    route = [((i - distance) % len(devices), i) for i in devices]
    return lax.ppermute(block, axis, route)


def swapped(block, axis, mask):
    return lax.ppermute(block, axis, [(i, i ^ mask) for i in range(lax.axis_size(axis))])


def halo_table(depth):
    order, at = {}, 0
    for name, extent in (
        [(("innov", k), k) for k in range(depth, 0, -1)]
        + [("diff", depth), ("c0", depth), ("c1", depth - 1), ("c2", depth - 1)]
    ):
        for distance in range(1, extent + 1):
            order[name, distance] = at
            at += 1
    order["sea"] = at
    return order, at + 1


def pack_kernel(table, place, bricks, innov_lo, innov_hi, cour_lo, cour_hi, diff_lo, diff_hi, down, up, sea, placed, rows):
    for n in range(place.shape[0]):
        placed[n] = place[n]
    depth = diff_lo.shape[0]
    levels, _, count = bricks.shape
    lat_cells = sea.shape[2]
    for z in range(levels):
        rows[z : z + 1] = bricks[z].astype(jnp.float32)
    brick_at = lax.broadcasted_iota(jnp.int32, (count, lat_cells), 0)
    cell_at = lax.broadcasted_iota(jnp.int32, (count, lat_cells), 1)
    inside = (brick_at == cell_at // (lat_cells // count)).astype(jnp.bfloat16)
    wide = jnp.dot(rows[...].astype(jnp.bfloat16), inside, preferred_element_type=jnp.float32)
    for z in range(levels):
        sea[z] = wide[z : z + 1]
    sea_lo, sea_hi = sea, sea.at[pl.ds(levels - depth, depth)]

    def fill(out, innov, cour, diff, sea, level):
        for key, at in table.items():
            if key == "sea":
                rows = [sea[level(d)] for d in range(1, depth + 1)]
                rows.append(jnp.zeros((out.shape[1] - depth, out.shape[2]), jnp.float32))
                value = jnp.concatenate(rows, 0)
            else:
                name, distance = key
                z = level(distance)
                if name == "diff":
                    value = diff[z]
                elif name == "c0":
                    value = cour[0, z]
                elif name == "c1":
                    value = cour[1, z]
                elif name == "c2":
                    value = cour[2, z]
                else:
                    value = innov[name[1], z]
            out[at] = value.astype(jnp.bfloat16)

    fill(down, innov_hi, cour_hi, diff_hi, sea_hi, lambda d: depth - d)
    fill(up, innov_lo, cour_lo, diff_lo, sea_lo, lambda d: d - 1)


def first_kernel(table, innov, cour, diff, sea, before, after, sea_ext, east_gain, west_gain, to_east, to_west):
    steps = innov.shape[0] - 1
    levels, lon_cells, lat_cells = diff.shape
    last = lon_cells - 1

    def put(at, sea_row, diff_a, diff_b, cour_a, cour_b, innov_a, innov_b):
        sea_ext[at] = sea_row
        low_row, high_row = sea_row * innov_a, sea_row * innov_b
        west = diff_a + 0.5 * cour_a
        east = diff_b - 0.5 * cour_b
        west_gain[at], east_gain[at] = west, east
        to_west[at], to_east[at] = west * low_row, east * high_row

    for halo, where in ((before, lambda d: steps - d), (after, lambda d: steps + levels + d - 1)):
        sea_rows = halo[table["sea"]].astype(jnp.float32)
        for d in range(1, steps + 1):
            sea_row = sea_rows[d - 1 : d]
            at = where(d)
            if d == steps:
                zero = jnp.zeros((1, lat_cells), jnp.float32)
                sea_ext[at] = sea_row
                west_gain[at], east_gain[at], to_west[at], to_east[at] = zero, zero, zero, zero
            else:
                dd = halo[table["diff", d]].astype(jnp.float32)
                cc = halo[table["c1", d]].astype(jnp.float32)
                ii = halo[table[("innov", steps), d]].astype(jnp.float32)
                put(at, sea_row, dd[:1], dd[last:], cc[:1], cc[last:], ii[:1], ii[last:])

    def one(z, carry):
        edge = lambda ref: (ref[z, :1], ref[z, last:])
        put(z + steps, sea[z], *edge(diff), *edge(cour.at[1]), *edge(innov.at[steps]))
        return carry

    lax.fori_loop(0, levels, one, 0, unroll=4)


def step_kernel(table, step, innov, cour, diff, sea_ext, before, after, low, high, *rest):
    steps = innov.shape[0] - 1
    levels, lon_cells, lat_cells = diff.shape
    if step > 1:
        lam, rest = rest[0], rest[1:]
    out, out_low, out_high = rest
    last = lon_cells - 1
    x_at = lax.broadcasted_iota(jnp.int32, (lon_cells, lat_cells), 0)
    y_at = lax.broadcasted_iota(jnp.int32, (lon_cells, lat_cells), 1)
    first_x, last_x = x_at == 0, x_at == last
    first_y, last_y = y_at == 0, y_at == lat_cells - 1
    reach = steps - step

    def halo_level(halo, d, name):
        return halo[table[name, d]].astype(jnp.float32)

    def state(at, innovation):
        if step == 1:
            return sea_ext[at] * innovation
        value = jnp.where(first_x, low[at], lam[at])
        return jnp.where(last_x, high[at], value)

    def finish(at, acc, up_flux):
        value = sea_ext[at] * (acc + up_flux)
        out[at] = value
        out_low[at] = value[:1]
        out_high[at] = value[last:]

    def depth_terms(a, d, c):
        spread, drift = d * a, c * (0.5 * a)
        return spread - drift, spread + drift

    def level(a, d, c0, c1, c2, innovation):
        half = 0.5 * a
        spread = d * a
        drift = c0 * half
        plus0, minus0 = spread - drift, spread + drift
        drift = c1 * half
        plus1, minus1 = spread - drift, spread + drift
        drift = c2 * half
        plus2, minus2 = spread - drift, spread + drift
        acc = a - 6.0 * spread + innovation
        acc = acc + jnp.where(first_x, 0.0, pltpu.roll(plus1, 1, 0))
        acc = acc + jnp.where(last_x, 0.0, pltpu.roll(minus1, lon_cells - 1, 0))
        acc = acc + jnp.where(first_y, 0.0, pltpu.roll(plus2, 1, 1))
        acc = acc + jnp.where(last_y, 0.0, pltpu.roll(minus2, lat_cells - 1, 1))
        return acc, plus0, minus0

    def halo_full(halo, d, at):
        a = state(at, halo_level(halo, d, ("innov", steps)))
        return level(
            a,
            halo_level(halo, d, "diff"),
            halo_level(halo, d, "c0"),
            halo_level(halo, d, "c1"),
            halo_level(halo, d, "c2"),
            halo_level(halo, d, ("innov", steps - step)),
        )

    def halo_edge(halo, d, at):
        a = state(at, halo_level(halo, d, ("innov", steps)))
        return depth_terms(a, halo_level(halo, d, "diff"), halo_level(halo, d, "c0"))

    down_flux, _ = halo_edge(before, reach + 1, steps - reach - 1)
    acc = None
    for d in range(reach, 0, -1):
        at = steps - d
        value, plus0, minus0 = halo_full(before, d, at)
        if acc is not None:
            finish(at - 1, acc, minus0)
        acc, down_flux = value + down_flux, plus0

    def own(z):
        a = state(z + steps, innov[steps, z])
        return level(a, diff[z], cour[0, z], cour[1, z], cour[2, z], innov[steps - step, z])

    value, plus0, minus0 = own(0)
    if acc is not None:
        finish(steps - 1, acc, minus0)
    carry = (value + down_flux, plus0)

    def one(z, carry):
        acc, down_flux = carry
        value, plus0, minus0 = own(z)
        finish(z + steps - 1, acc, minus0)
        return value + down_flux, plus0

    head = (levels - 1) % UNROLL
    for z in range(1, 1 + head):
        carry = one(z, carry)

    def several(i, carry):
        for u in range(UNROLL):
            carry = one(1 + head + i * UNROLL + u, carry)
        return carry

    acc, down_flux = lax.fori_loop(0, (levels - 1) // UNROLL, several, carry)
    at = steps + levels - 1
    for d in range(1, reach + 1):
        value, plus0, minus0 = halo_full(after, d, at + d)
        finish(at + d - 1, acc, minus0)
        acc, down_flux = value + down_flux, plus0
    _, up_flux = halo_edge(after, reach + 1, at + reach + 1)
    finish(at + reach, acc, up_flux)


def last_kernel(place, lam, sea_ext, out_low, out_high, west, east, out, mine, other, *rows):
    levels, lon_cells, lat_cells = out.shape
    steps = (lam.shape[0] - levels) // 2
    x_at = lax.broadcasted_iota(jnp.int32, (lon_cells, lat_cells), 0)
    first_x, last_x = x_at == 0, x_at == lon_cells - 1

    def one(z, carry):
        at = z + steps
        low = out_low[at] + sea_ext[at] * west[at]
        high = out_high[at] + sea_ext[at] * east[at]
        value = jnp.where(last_x, high, jnp.where(first_x, low, lam[at]))
        out[z] = value
        for c, lanes in enumerate(rows):
            at = pl.multiple_of(z * lon_cells, lon_cells)
            lanes[pl.ds(at, lon_cells), :] = value[:, c * LANES : (c + 1) * LANES]
        return carry

    lax.fori_loop(0, levels, one, 0, unroll=4)
    half = lon_cells // 2
    for part, start in ((mine, place[1] * half), (other, (1 - place[1]) * half)):
        for x in range(half):
            for c, lanes in enumerate(rows):
                picked = lanes[pl.ds(start + x, levels, stride=lon_cells), :]
                at = x * lat_cells + c * LANES
                part[:, at : at + LANES] = picked.astype(jnp.bfloat16)


def face_kernel(sea_ext, out_low, out_high, west, east, west_gain, east_gain, low, high, to_west, to_east):
    low_rows = out_low[...] + sea_ext[...] * west[...]
    high_rows = out_high[...] + sea_ext[...] * east[...]
    low[...], high[...] = low_rows, high_rows
    to_west[...], to_east[...] = west_gain[...] * low_rows, east_gain[...] * high_rows


def pack(innovations, courant, diffusivity, bricks, place):
    levels, lon_cells, lat_cells = diffusivity.shape
    steps = innovations.shape[0] - 1
    table, layers = halo_table(steps)
    f32, bf16 = jnp.float32, jnp.bfloat16
    end = levels // steps - 1

    def edges(shape, axis):
        block = list(shape)
        block[axis] = steps
        at = lambda index: lambda i: tuple(index if a == axis else 0 for a in range(len(shape)))
        return [pl.BlockSpec(tuple(block), at(index)) for index in (0, end)]

    message = jax.ShapeDtypeStruct((layers, lon_cells, lat_cells), bf16)
    down, up, sea, place = pl.pallas_call(
        functools.partial(pack_kernel, table),
        grid=(1,),
        in_specs=[SMEM, VMEM]
        + edges(innovations.shape, 1)
        + edges(courant.shape, 1)
        + edges(diffusivity.shape, 0),
        out_shape=[message, message, jax.ShapeDtypeStruct((levels, 1, lat_cells), f32), jax.ShapeDtypeStruct(place.shape, place.dtype)],
        out_specs=[VMEM, VMEM, VMEM, SMEM],
        scratch_shapes=[pltpu.VMEM((levels, bricks.shape[2]), f32)],
        cost_estimate=pl.CostEstimate(flops=0, bytes_accessed=1 << 20, transcendentals=0),
    )(place, bricks, innovations, innovations, courant, courant, diffusivity, diffusivity)
    return down, up, sea, place


def sweep(innovations, courant, diffusivity, sea, down, up, place):
    levels, lon_cells, lat_cells = diffusivity.shape
    steps = innovations.shape[0] - 1
    table, _ = halo_table(steps)
    f32, bf16 = jnp.float32, jnp.bfloat16
    before = from_behind(down, "depth", 1)
    after = from_behind(up, "depth", -1)
    row = jax.ShapeDtypeStruct((levels + 2 * steps, 1, lat_cells), f32)
    cells = jax.ShapeDtypeStruct((levels + 2 * steps, lon_cells, lat_cells), f32)
    inputs = (innovations, courant, diffusivity)
    sea_ext, east_gain, west_gain, to_east, to_west = pl.pallas_call(
        functools.partial(first_kernel, table),
        in_specs=[VMEM] * 6,
        out_shape=[row] * 5,
        out_specs=[VMEM] * 5,
        compiler_params=pltpu.CompilerParams(vmem_limit_bytes=GRANT),
        cost_estimate=pl.CostEstimate(flops=0, bytes_accessed=1 << 20, transcendentals=0),
    )(*inputs, sea, before, after)
    lam = ()
    low = high = sea_ext
    for step in range(1, steps + 1):
        west = shifted(to_east, "lon", 1)
        east = shifted(to_west, "lon", -1)
        state = (low, high) + lam
        out, out_low, out_high = pl.pallas_call(
            functools.partial(step_kernel, table, step),
            in_specs=[VMEM] * (6 + len(state)),
            out_shape=[cells, row, row],
            out_specs=[VMEM] * 3,
            compiler_params=pltpu.CompilerParams(vmem_limit_bytes=GRANT),
            cost_estimate=pl.CostEstimate(flops=40 * levels * lon_cells * lat_cells, bytes_accessed=9 << 20, transcendentals=0),
        )(*inputs, sea_ext, before, after, *state)
        if step == steps:
            break
        low, high, to_west, to_east = pl.pallas_call(
            face_kernel,
            in_specs=[VMEM] * 7,
            out_shape=[row] * 4,
            out_specs=[VMEM] * 4,
            compiler_params=pltpu.CompilerParams(vmem_limit_bytes=GRANT),
            cost_estimate=pl.CostEstimate(flops=0, bytes_accessed=1 << 19, transcendentals=0),
        )(sea_ext, out_low, out_high, west, east, west_gain, east_gain)
        lam = (out,)
    half = jax.ShapeDtypeStruct((levels, lon_cells * lat_cells // 2), bf16)
    return pl.pallas_call(
        last_kernel,
        in_specs=[SMEM] + [VMEM] * 6,
        out_shape=[jax.ShapeDtypeStruct((levels, lon_cells, lat_cells), f32), half, half],
        out_specs=[VMEM] * 3,
        scratch_shapes=[pltpu.VMEM((levels * lon_cells, LANES), f32)] * (lat_cells // LANES),
        compiler_params=pltpu.CompilerParams(vmem_limit_bytes=GRANT),
        cost_estimate=pl.CostEstimate(flops=0, bytes_accessed=3 << 20, transcendentals=0),
    )(place, out, sea_ext, out_low, out_high, west, east)


def halves_kernel(place, left, right, left_mine, right_mine, left_other, *rest):
    right_other, (vmem, sems) = rest[:-2], rest[-2:]
    half = left_mine.shape[2]
    side = place[1]
    jobs = [
        (left, 1 - side, [left_other]),
        (right, 1 - side, right_other),
        (left, side, [left_mine]),
        (right, side, [right_mine]),
    ]
    loads, stores = [], []
    for n, (source, which, targets) in enumerate(jobs):
        window = source.at[0, :, :, pl.ds(pl.multiple_of(which * half, half), half)]
        loads.append(pltpu.make_async_copy(window, vmem.at[n], sems.at[n]))
        loads[-1].start()
    for n, (source, which, targets) in enumerate(jobs):
        loads[n].wait()
        size = vmem.shape[1] // len(targets)
        for q, target in enumerate(targets):
            piece = vmem.at[n, pl.ds(q * size, size)]
            stores.append(pltpu.make_async_copy(piece, target, sems.at[len(jobs) + len(stores)]))
            stores[-1].start()
    for store in stores:
        store.wait()


def against(a, b):
    return lax.dot_general(a, b, (((1,), (1,)), ((), ())), preferred_element_type=jnp.float32)


def rows_kernel(left_mine, left_pair, first, second, kept, sent):
    for c, factor in enumerate((left_mine, left_pair)):
        parts = [against(factor[...], block[...]) for block in (first, second)]
        kept[c] = jnp.concatenate(parts, 1)
        sent[1 - c] = jnp.concatenate(parts[::-1], 1).astype(jnp.bfloat16)


def mask_kernel(slots, place, ranks, kept, arrived, *out):
    rows = kept.shape[1] // slots
    for c in range(2):
        owner = place[0] if c == 0 else place[0] + 1 - 2 * place[1]
        for k in range(slots):
            at = slice(k * rows, (k + 1) * rows)
            value = kept[c, at, :] + arrived[c, at, :].astype(jnp.float32)
            row = lax.broadcasted_iota(jnp.int32, value.shape, 0) + owner * rows
            value = jnp.where(row < ranks[0, k], value, 0.0).astype(jnp.bfloat16)
            if len(out) > 1:
                out[k][c] = value
            else:
                count = out[0].shape[0]
                out[0][lax.rem(place[2] + (k - slots // 2 + count), count), c] = value


def columns_kernel(slots, wide, place, right_mine, *rest):
    right_pair, received, out = rest[:PARTS], rest[PARTS:-2], rest[-2:]
    count = received[0].shape[0]
    total = None
    for c in range(2):
        for k in range(slots):
            if len(received) > 1:
                coeff = received[k][c]
            else:
                coeff = received[0][lax.rem(place[2] + (count + slots // 2 - k), count), c]
            coeffs = [coeff] if k == 0 and c == 0 else coeffs + [coeff]
    stacked = jnp.concatenate(coeffs, 0)
    rows = right_mine.shape[0]
    lead = (((0,), (0,)), ((), ()))
    for at in range(0, right_mine.shape[1], wide):
        lanes = slice(at, at + wide)
        total = lax.dot_general(stacked[:rows], right_mine[:, lanes], lead, preferred_element_type=jnp.float32)
        pair = jnp.concatenate([piece[:, lanes] for piece in right_pair], 0)
        total = total + lax.dot_general(stacked[rows:], pair, lead, preferred_element_type=jnp.float32)
        levels = out[0].shape[0]
        out[0][:, lanes] = total[:levels].astype(out[0].dtype)
        out[1][:, lanes] = total[levels:].astype(out[1].dtype)


def join_kernel(place, own, arrived1, arrived2, arrived3, out, *rows):
    levels, lon_cells, lat_cells = out.shape
    half = lon_cells // 2
    f32 = jnp.float32
    for x in range(half):
        for c, lanes in enumerate(rows):
            at = x * lat_cells + c * LANES
            cols = slice(at, at + LANES)
            mine = own[:, cols] + arrived2[:, cols].astype(f32)
            other = arrived1[:, cols].astype(f32) + arrived3[:, cols].astype(f32)
            lanes[pl.ds(place[1] * half + x, levels, stride=lon_cells), :] = mine
            lanes[pl.ds((1 - place[1]) * half + x, levels, stride=lon_cells), :] = other

    def one(z, carry):
        at = pl.multiple_of(z * lon_cells, lon_cells)
        for c, lanes in enumerate(rows):
            out[z, :, c * LANES : (c + 1) * LANES] = lanes[pl.ds(at, lon_cells), :]
        return carry

    lax.fori_loop(0, levels, one, 0, unroll=4)


def call(kernel, operands, in_specs, outs, grant=GRANT, flops=0, moved=1 << 20, scratch=()):
    return pl.pallas_call(
        kernel,
        in_specs=in_specs,
        out_shape=[jax.ShapeDtypeStruct(*o[:2]) for o in outs],
        out_specs=[o[2] if len(o) > 2 else VMEM for o in outs],
        scratch_shapes=list(scratch),
        compiler_params=pltpu.CompilerParams(vmem_limit_bytes=grant),
        cost_estimate=pl.CostEstimate(flops=flops, bytes_accessed=moved, transcendentals=0),
    )(*operands)


def per_device(
    innovations, courant, diffusivity, sea_bricks, tile_ranks, row_factors, column_factors
):
    levels, lon_cells, lat_cells = diffusivity.shape
    tile_cols = lon_cells * lat_cells
    half = tile_cols // 2
    slots = tile_ranks.shape[1]
    count = lax.axis_size("depth")
    lon_count = lax.axis_size("lon")
    f32, bf16 = jnp.float32, jnp.bfloat16
    me = lax.axis_index("depth")
    place = jnp.stack([me, me % 2, lax.axis_index("lon")]).astype(jnp.int32)
    left = row_factors.transpose(0, 1, 3, 2)
    right = column_factors.transpose(0, 1, 3, 2)
    width = left.shape[2]
    rows = slots * width

    down, up, sea, place = pack(innovations, courant, diffusivity, sea_bricks, place)
    part = (slots, width, half)
    piece = (slots // PARTS, width, half)
    left_mine, right_mine, left_other, *right_other = call(
        halves_kernel,
        (place, left, right),
        [SMEM, ANY, ANY],
        [(part, bf16, ANY)] * 3 + [(piece, bf16, ANY)] * PARTS,
        grant=8 << 20,
        moved=8 << 20,
        scratch=[pltpu.VMEM((4, slots, width, half), bf16), pltpu.SemaphoreType.DMA((7 + PARTS,))],
    )
    left_pair = swapped(left_other, "depth", 1)
    right_pair = []
    for part in range(PARTS):
        right_pair.append(swapped(right_other[part], "depth", 1).reshape(rows // PARTS, half))
    lam, lam_mine, lam_other = sweep(innovations, courant, diffusivity, sea, down, up, place)
    left_mine, left_pair, right_mine = (a.reshape(rows, half) for a in (left_mine, left_pair, right_mine))
    blocks = {0: lam_mine}
    for mask in [1] + list(range(count - 1, 1, -1)):
        blocks[mask] = swapped(lam_other if mask % 2 else lam_mine, "depth", mask)
    arrived, own = {}, None
    for stage in range(0, count, 2):
        pair = (2, rows, 2 * levels)
        kept, sent = call(
            rows_kernel,
            (left_mine, left_pair, blocks[stage], blocks[stage + 1]),
            [VMEM] * 4,
            [(pair, f32), (pair, bf16)],
            flops=8 * rows * half * levels,
            moved=3 << 20,
        )
        other = swapped(sent, "depth", 1)
        grouped = lon_count == slots
        slot = (2, width, 2 * levels)
        outs = [((lon_count,) + slot, bf16)] if grouped else [(slot, bf16)] * slots
        coeff = call(
            functools.partial(mask_kernel, slots),
            (place, tile_ranks, kept, other),
            [SMEM, SMEM, VMEM, VMEM],
            outs,
        )
        if grouped:
            received = [lax.all_to_all(coeff[0], "lon", 0, 0, tiled=True)]
        else:
            received = [shifted(coeff[k], "lon", k - slots // 2) for k in range(slots)]
        block = (levels, half)
        first, second = call(
            functools.partial(columns_kernel, slots, 4 * LANES),
            (place, right_mine, *right_pair, *received),
            [SMEM] + [VMEM] * (1 + PARTS + len(received)),
            [(block, bf16 if stage else f32), (block, bf16)],
            flops=8 * rows * half * levels,
            moved=3 << 20,
        )
        if stage:
            arrived[stage] = swapped(first, "depth", stage)
        else:
            own = first
        arrived[stage + 1] = swapped(second, "depth", stage + 1)
    (gradient,) = call(
        join_kernel,
        (place, own, *(arrived[mask] for mask in range(1, count))),
        [SMEM] + [VMEM] * count,
        [((levels, lon_cells, lat_cells), f32)],
        scratch=[pltpu.VMEM((levels * lon_cells, LANES), f32)] * (lat_cells // LANES),
        moved=4 << 20,
    )
    return (lam, gradient)


def solution(mesh):
    placed = (
        P(None, "depth", "lon", None),
        P(None, "depth", "lon", None),
        P("depth", "lon", None),
        P("depth", "lon", None),
        P("lon", None),
        P("lon", None, None, "depth"),
        P("lon", None, None, "depth"),
    )
    return jax.shard_map(
        per_device,
        mesh=mesh,
        in_specs=placed,
        out_specs=(P("depth", "lon", None), P("depth", "lon", None)),
        check_vma=False,
    )
```

```python
import functools
import jax
import jax.numpy as jnp
from jax import lax
from jax.experimental import pallas as pl
from jax.experimental.pallas import tpu as pltpu
from jax.sharding import PartitionSpec as P

UNROLL = 3
LANES = 128
PARTS = 4
STAGES = 2
GRANT = 4 << 20
VMEM = pl.BlockSpec(memory_space=pltpu.VMEM)
SMEM = pl.BlockSpec(memory_space=pltpu.SMEM)
ANY = pl.BlockSpec(memory_space=pl.ANY)


def from_behind(value, axis, steps):
    count = lax.axis_size(axis)
    initial, last = (max(0, -steps), min(count, count - steps))
    return lax.ppermute(value, axis, [(source, source + steps) for source in range(initial, last)])


def shifted(block, axis, distance):
    devices = range(lax.axis_size(axis))
    if distance % len(devices) == 0:
        return block
    route = [((i - distance) % len(devices), i) for i in devices]
    return lax.ppermute(block, axis, route)


def swapped(block, axis, mask):
    return lax.ppermute(block, axis, [(i, i ^ mask) for i in range(lax.axis_size(axis))])


def halo_table(depth):
    order, at = {}, 0
    for name, extent in (
        [(("innov", k), k) for k in range(depth, 0, -1)]
        + [("diff", depth), ("c0", depth), ("c1", depth - 1), ("c2", depth - 1)]
    ):
        for distance in range(1, extent + 1):
            order[name, distance] = at
            at += 1
    order["sea"] = at
    return order, at + 1


def pack_kernel(table, axes, bricks, innov_lo, innov_hi, cour_lo, cour_hi, diff_lo, diff_hi, left, right, *rest):
    down, up, sea, place, left_other, *right_other = rest[:-3]
    rows, vmem, sems = rest[-3:]
    me = lax.axis_index(axes[1])
    side = lax.rem(me, 2)
    place[0], place[1], place[2] = me, side, lax.axis_index(axes[0])
    half = left_other.shape[2]
    start = pl.multiple_of((1 - side) * half, half)
    loads, stores = [], []
    for n, source in enumerate((left, right)):
        window = source.at[0, :, :, pl.ds(start, half)]
        loads.append(pltpu.make_async_copy(window, vmem.at[n], sems.at[n]))
        loads[-1].start()
    depth = diff_lo.shape[0]
    levels, _, count = bricks.shape
    lat_cells = sea.shape[2]
    for z in range(levels):
        rows[z : z + 1] = bricks[z].astype(jnp.float32)
    brick_at = lax.broadcasted_iota(jnp.int32, (count, lat_cells), 0)
    cell_at = lax.broadcasted_iota(jnp.int32, (count, lat_cells), 1)
    inside = (brick_at == cell_at // (lat_cells // count)).astype(jnp.bfloat16)
    wide = jnp.dot(rows[...].astype(jnp.bfloat16), inside, preferred_element_type=jnp.float32)
    for z in range(levels):
        sea[z] = wide[z : z + 1]
    sea_lo, sea_hi = sea, sea.at[pl.ds(levels - depth, depth)]

    def fill(out, innov, cour, diff, sea, level):
        for key, at in table.items():
            if key == "sea":
                rows = [sea[level(d)] for d in range(1, depth + 1)]
                rows.append(jnp.zeros((out.shape[1] - depth, out.shape[2]), jnp.float32))
                value = jnp.concatenate(rows, 0)
            else:
                name, distance = key
                z = level(distance)
                if name == "diff":
                    value = diff[z]
                elif name == "c0":
                    value = cour[0, z]
                elif name == "c1":
                    value = cour[1, z]
                elif name == "c2":
                    value = cour[2, z]
                else:
                    value = innov[name[1], z]
            out[at] = value.astype(jnp.bfloat16)

    fill(down, innov_hi, cour_hi, diff_hi, sea_hi, lambda d: depth - d)
    fill(up, innov_lo, cour_lo, diff_lo, sea_lo, lambda d: d - 1)
    for n, targets in enumerate(([left_other], right_other)):
        loads[n].wait()
        size = vmem.shape[1] // len(targets)
        for q, target in enumerate(targets):
            piece = vmem.at[n, pl.ds(q * size, size)]
            stores.append(pltpu.make_async_copy(piece, target, sems.at[2 + len(stores)]))
            stores[-1].start()
    for store in stores:
        store.wait()


def load_kernel(*refs):
    count = len(refs) // 2
    copies = [pltpu.make_async_copy(refs[n], refs[count + n], refs[-1].at[n]) for n in range(count)]
    for copy in copies:
        copy.start()
    for copy in copies:
        copy.wait()


def first_kernel(table, innov, cour, diff, sea, before, after, sea_ext, east_gain, west_gain, to_east, to_west):
    steps = innov.shape[0] - 1
    levels, lon_cells, lat_cells = diff.shape
    last = lon_cells - 1

    def put(at, sea_row, diff_a, diff_b, cour_a, cour_b, innov_a, innov_b):
        sea_ext[at] = sea_row
        low_row, high_row = sea_row * innov_a, sea_row * innov_b
        west = diff_a + 0.5 * cour_a
        east = diff_b - 0.5 * cour_b
        west_gain[at], east_gain[at] = west, east
        to_west[at], to_east[at] = west * low_row, east * high_row

    for halo, where in ((before, lambda d: steps - d), (after, lambda d: steps + levels + d - 1)):
        sea_rows = halo[table["sea"]].astype(jnp.float32)
        for d in range(1, steps + 1):
            sea_row = sea_rows[d - 1 : d]
            at = where(d)
            if d == steps:
                zero = jnp.zeros((1, lat_cells), jnp.float32)
                sea_ext[at] = sea_row
                west_gain[at], east_gain[at], to_west[at], to_east[at] = zero, zero, zero, zero
            else:
                dd = halo[table["diff", d]].astype(jnp.float32)
                cc = halo[table["c1", d]].astype(jnp.float32)
                ii = halo[table[("innov", steps), d]].astype(jnp.float32)
                put(at, sea_row, dd[:1], dd[last:], cc[:1], cc[last:], ii[:1], ii[last:])

    def one(z, carry):
        edge = lambda ref: (ref[z, :1], ref[z, last:])
        put(z + steps, sea[z], *edge(diff), *edge(cour.at[1]), *edge(innov.at[steps]))
        return carry

    lax.fori_loop(0, levels, one, 0, unroll=4)


def step_kernel(table, step, innov, cour, diff, sea_ext, before, after, low, high, *rest):
    steps = innov.shape[0] - 1
    levels, lon_cells, lat_cells = diff.shape
    if step > 1:
        lam, rest = rest[0], rest[1:]
    out, out_low, out_high = rest
    last = lon_cells - 1
    x_at = lax.broadcasted_iota(jnp.int32, (lon_cells, lat_cells), 0)
    y_at = lax.broadcasted_iota(jnp.int32, (lon_cells, lat_cells), 1)
    first_x, last_x = x_at == 0, x_at == last
    first_y, last_y = y_at == 0, y_at == lat_cells - 1
    reach = steps - step

    def halo_level(halo, d, name):
        return halo[table[name, d]].astype(jnp.float32)

    def state(at, innovation):
        if step == 1:
            return sea_ext[at] * innovation
        value = jnp.where(first_x, low[at], lam[at])
        return jnp.where(last_x, high[at], value)

    def finish(at, acc, up_flux):
        value = sea_ext[at] * (acc + up_flux)
        out[at] = value
        out_low[at] = value[:1]
        out_high[at] = value[last:]

    def depth_terms(a, d, c):
        spread, drift = d * a, c * (0.5 * a)
        return spread - drift, spread + drift

    def level(a, d, c0, c1, c2, innovation):
        half = 0.5 * a
        spread = d * a
        drift = c0 * half
        plus0, minus0 = spread - drift, spread + drift
        drift = c1 * half
        plus1, minus1 = spread - drift, spread + drift
        drift = c2 * half
        plus2, minus2 = spread - drift, spread + drift
        acc = a - 6.0 * spread + innovation
        acc = acc + jnp.where(first_x, 0.0, pltpu.roll(plus1, 1, 0))
        acc = acc + jnp.where(last_x, 0.0, pltpu.roll(minus1, lon_cells - 1, 0))
        acc = acc + jnp.where(first_y, 0.0, pltpu.roll(plus2, 1, 1))
        acc = acc + jnp.where(last_y, 0.0, pltpu.roll(minus2, lat_cells - 1, 1))
        return acc, plus0, minus0

    def halo_full(halo, d, at):
        a = state(at, halo_level(halo, d, ("innov", steps)))
        return level(
            a,
            halo_level(halo, d, "diff"),
            halo_level(halo, d, "c0"),
            halo_level(halo, d, "c1"),
            halo_level(halo, d, "c2"),
            halo_level(halo, d, ("innov", steps - step)),
        )

    def halo_edge(halo, d, at):
        a = state(at, halo_level(halo, d, ("innov", steps)))
        return depth_terms(a, halo_level(halo, d, "diff"), halo_level(halo, d, "c0"))

    down_flux, _ = halo_edge(before, reach + 1, steps - reach - 1)
    acc = None
    for d in range(reach, 0, -1):
        at = steps - d
        value, plus0, minus0 = halo_full(before, d, at)
        if acc is not None:
            finish(at - 1, acc, minus0)
        acc, down_flux = value + down_flux, plus0

    def own(z):
        a = state(z + steps, innov[steps, z])
        return level(a, diff[z], cour[0, z], cour[1, z], cour[2, z], innov[steps - step, z])

    value, plus0, minus0 = own(0)
    if acc is not None:
        finish(steps - 1, acc, minus0)
    carry = (value + down_flux, plus0)

    def one(z, carry):
        acc, down_flux = carry
        value, plus0, minus0 = own(z)
        finish(z + steps - 1, acc, minus0)
        return value + down_flux, plus0

    head = (levels - 1) % UNROLL
    for z in range(1, 1 + head):
        carry = one(z, carry)

    def several(i, carry):
        for u in range(UNROLL):
            carry = one(1 + head + i * UNROLL + u, carry)
        return carry

    acc, down_flux = lax.fori_loop(0, (levels - 1) // UNROLL, several, carry)
    at = steps + levels - 1
    for d in range(1, reach + 1):
        value, plus0, minus0 = halo_full(after, d, at + d)
        finish(at + d - 1, acc, minus0)
        acc, down_flux = value + down_flux, plus0
    _, up_flux = halo_edge(after, reach + 1, at + reach + 1)
    finish(at + reach, acc, up_flux)


def lay_kernel(place, lam, mine, other, *rows):
    levels = mine.shape[0]
    total, lon_cells, lat_cells = lam.shape
    steps = (total - levels) // 2

    def one(z, carry):
        value = lam[z + steps]
        for c, lanes in enumerate(rows):
            at = pl.multiple_of(z * lon_cells, lon_cells)
            lanes[pl.ds(at, lon_cells), :] = value[:, c * LANES : (c + 1) * LANES]
        return carry

    lax.fori_loop(0, levels, one, 0, unroll=4)
    half = lon_cells // 2
    for part, start in ((mine, place[1] * half), (other, (1 - place[1]) * half)):
        for x in range(half):
            for c, lanes in enumerate(rows):
                picked = lanes[pl.ds(start + x, levels, stride=lon_cells), :]
                at = x * lat_cells + c * LANES
                part[:, at : at + LANES] = picked.astype(jnp.bfloat16)


def fix_kernel(place, sea_ext, out_low, out_high, west, east, mine_in, other_in, mine, other, low_rows, high_rows):
    levels, half = mine.shape
    lat_cells = low_rows.shape[1]
    steps = (sea_ext.shape[0] - levels) // 2
    for z in range(levels):
        at = z + steps
        low_rows[z : z + 1] = out_low[at] + sea_ext[at] * west[at]
        high_rows[z : z + 1] = out_high[at] + sea_ext[at] * east[at]
    low = low_rows[...].astype(jnp.bfloat16)
    high = high_rows[...].astype(jnp.bfloat16)

    @pl.when(place[1] == 0)
    def _():
        mine[:, :lat_cells] = low
        other[:, half - lat_cells :] = high

    @pl.when(place[1] != 0)
    def _():
        other[:, :lat_cells] = low
        mine[:, half - lat_cells :] = high


def emit_kernel(lam, sea_ext, out_low, out_high, west, east, out):
    levels, lon_cells, lat_cells = out.shape
    steps = (lam.shape[0] - levels) // 2
    x_at = lax.broadcasted_iota(jnp.int32, (lon_cells, lat_cells), 0)
    first_x, last_x = x_at == 0, x_at == lon_cells - 1

    def one(z, carry):
        at = z + steps
        low = out_low[at] + sea_ext[at] * west[at]
        high = out_high[at] + sea_ext[at] * east[at]
        out[z] = jnp.where(last_x, high, jnp.where(first_x, low, lam[at]))
        return carry

    lax.fori_loop(0, levels, one, 0, unroll=4)


def face_kernel(sea_ext, out_low, out_high, west, east, west_gain, east_gain, low, high, to_west, to_east):
    low_rows = out_low[...] + sea_ext[...] * west[...]
    high_rows = out_high[...] + sea_ext[...] * east[...]
    low[...], high[...] = low_rows, high_rows
    to_west[...], to_east[...] = west_gain[...] * low_rows, east_gain[...] * high_rows


def pack(innovations, courant, diffusivity, bricks, left, right):
    levels, lon_cells, lat_cells = diffusivity.shape
    steps = innovations.shape[0] - 1
    table, layers = halo_table(steps)
    f32, bf16 = jnp.float32, jnp.bfloat16
    end = levels // steps - 1

    def edges(shape, axis):
        block = list(shape)
        block[axis] = steps
        at = lambda index: lambda i: tuple(index if a == axis else 0 for a in range(len(shape)))
        return [pl.BlockSpec(tuple(block), at(index)) for index in (0, end)]

    message = jax.ShapeDtypeStruct((layers, lon_cells, lat_cells), bf16)
    _, slots, width, cols = left.shape
    other = jax.ShapeDtypeStruct((slots, width, cols // 2), bf16)
    piece = jax.ShapeDtypeStruct((slots // PARTS, width, cols // 2), bf16)
    return pl.pallas_call(
        functools.partial(pack_kernel, table, ("lon", "depth")),
        grid=(1,),
        in_specs=[VMEM]
        + edges(innovations.shape, 1)
        + edges(courant.shape, 1)
        + edges(diffusivity.shape, 0)
        + [ANY, ANY],
        out_shape=[
            message,
            message,
            jax.ShapeDtypeStruct((levels, 1, lat_cells), f32),
            jax.ShapeDtypeStruct((3,), jnp.int32),
            other,
        ]
        + [piece] * PARTS,
        out_specs=[VMEM, VMEM, VMEM, SMEM] + [ANY] * (1 + PARTS),
        scratch_shapes=[
            pltpu.VMEM((levels, bricks.shape[2]), f32),
            pltpu.VMEM((2, slots, width, cols // 2), bf16),
            pltpu.SemaphoreType.DMA((3 + PARTS,)),
        ],
        cost_estimate=pl.CostEstimate(flops=0, bytes_accessed=1 << 20, transcendentals=0),
    )(bricks, innovations, innovations, courant, courant, diffusivity, diffusivity, left, right)


def sweep(innovations, courant, diffusivity, sea, down, up, place):
    levels, lon_cells, lat_cells = diffusivity.shape
    steps = innovations.shape[0] - 1
    table, _ = halo_table(steps)
    f32, bf16 = jnp.float32, jnp.bfloat16
    before = from_behind(down, "depth", 1)
    after = from_behind(up, "depth", -1)
    row = jax.ShapeDtypeStruct((levels + 2 * steps, 1, lat_cells), f32)
    cells = jax.ShapeDtypeStruct((levels + 2 * steps, lon_cells, lat_cells), f32)
    inputs = (innovations, courant, diffusivity)
    inputs = call(
        load_kernel,
        inputs,
        [ANY] * 3,
        [(a.shape, a.dtype) for a in inputs],
        grant=40 << 20,
        moved=18 << 20,
        scratch=[pltpu.SemaphoreType.DMA((3,))],
    )
    sea_ext, east_gain, west_gain, to_east, to_west = pl.pallas_call(
        functools.partial(first_kernel, table),
        in_specs=[VMEM] * 6,
        out_shape=[row] * 5,
        out_specs=[VMEM] * 5,
        compiler_params=pltpu.CompilerParams(vmem_limit_bytes=GRANT),
        cost_estimate=pl.CostEstimate(flops=0, bytes_accessed=1 << 20, transcendentals=0),
    )(*inputs, sea, before, after)
    lam = ()
    low = high = sea_ext
    for step in range(1, steps + 1):
        west = shifted(to_east, "lon", 1)
        east = shifted(to_west, "lon", -1)
        state = (low, high) + lam
        out, out_low, out_high = pl.pallas_call(
            functools.partial(step_kernel, table, step),
            in_specs=[VMEM] * (6 + len(state)),
            out_shape=[cells, row, row],
            out_specs=[VMEM] * 3,
            compiler_params=pltpu.CompilerParams(vmem_limit_bytes=GRANT),
            cost_estimate=pl.CostEstimate(flops=40 * levels * lon_cells * lat_cells, bytes_accessed=9 << 20, transcendentals=0),
        )(*inputs, sea_ext, before, after, *state)
        if step == steps:
            break
        low, high, to_west, to_east = pl.pallas_call(
            face_kernel,
            in_specs=[VMEM] * 7,
            out_shape=[row] * 4,
            out_specs=[VMEM] * 4,
            compiler_params=pltpu.CompilerParams(vmem_limit_bytes=GRANT),
            cost_estimate=pl.CostEstimate(flops=0, bytes_accessed=1 << 19, transcendentals=0),
        )(sea_ext, out_low, out_high, west, east, west_gain, east_gain)
        lam = (out,)
    half = (levels, lon_cells * lat_cells // 2)
    mine, other = call(
        lay_kernel,
        (place, out),
        [SMEM, VMEM],
        [(half, bf16)] * 2,
        scratch=[pltpu.VMEM((levels * lon_cells, LANES), f32)] * (lat_cells // LANES),
        moved=3 << 20,
    )
    edge = (sea_ext, out_low, out_high, west, east)
    mine, other = call(
        fix_kernel,
        (place, *edge, mine, other),
        [SMEM] + [VMEM] * 7,
        [(half, bf16)] * 2,
        scratch=[pltpu.VMEM((levels, lat_cells), f32)] * 2,
        aliases={6: 0, 7: 1},
    )
    (lam,) = call(
        emit_kernel,
        (out, *edge),
        [VMEM] * 6,
        [((levels, lon_cells, lat_cells), f32)],
        moved=3 << 20,
    )
    return lam, mine, other


def against(a, b):
    return lax.dot_general(a, b, (((1,), (1,)), ((), ())), preferred_element_type=jnp.float32)


def rows_kernel(place, left, left_pair, first, second, kept, sent):
    half = left_pair.shape[1]
    mine = left[:, pl.ds(pl.multiple_of(place[1] * half, half), half)]
    for c, factor in enumerate((mine, left_pair[...])):
        parts = [against(factor, block[...]) for block in (first, second)]
        kept[c] = jnp.concatenate(parts, 1)
        sent[1 - c] = jnp.concatenate(parts[::-1], 1).astype(jnp.bfloat16)


def mask_kernel(slots, place, ranks, *rest):
    stages = [rest[n : n + 2] for n in range(0, STAGES * 2, 2)]
    out = rest[STAGES * 2 :]
    rows = stages[0][0].shape[1] // slots
    for c in range(2):
        owner = place[0] if c == 0 else place[0] + 1 - 2 * place[1]
        for k in range(slots):
            at = slice(k * rows, (k + 1) * rows)
            value = jnp.concatenate(
                [kept[c, at, :] + arrived[c, at, :].astype(jnp.float32) for kept, arrived in stages], 1
            )
            row = lax.broadcasted_iota(jnp.int32, value.shape, 0) + owner * rows
            value = jnp.where(row < ranks[0, k], value, 0.0).astype(jnp.bfloat16)
            if len(out) > 1:
                out[k][c] = value
            else:
                count = out[0].shape[0]
                out[0][lax.rem(place[2] + (k - slots // 2 + count), count), c] = value


def columns_kernel(slots, wide, stage, place, right, *rest):
    right_pair, received, out = rest[:PARTS], rest[PARTS:-2], rest[-2:]
    count = received[0].shape[0]
    levels, half = out[0].shape
    picked = slice(stage * levels, (stage + 2) * levels)
    coeffs = []
    for c in range(2):
        for k in range(slots):
            if len(received) > 1:
                coeffs.append(received[k][c, :, picked])
            else:
                source = lax.rem(place[2] + (count + slots // 2 - k), count)
                coeffs.append(received[0][source, c, :, picked])
    stacked = jnp.concatenate(coeffs, 0)
    rows = right.shape[0]
    lead = (((0,), (0,)), ((), ()))
    for at in range(0, half, wide):
        lanes = slice(at, at + wide)
        mine = right[:, pl.ds(pl.multiple_of(place[1] * half + at, LANES), wide)]
        total = lax.dot_general(stacked[:rows], mine, lead, preferred_element_type=jnp.float32)
        pair = jnp.concatenate([piece[:, lanes] for piece in right_pair], 0)
        total = total + lax.dot_general(stacked[rows:], pair, lead, preferred_element_type=jnp.float32)
        out[0][:, lanes] = total[:levels].astype(out[0].dtype)
        out[1][:, lanes] = total[levels:].astype(out[1].dtype)


def join_kernel(place, own, arrived1, arrived2, arrived3, out, *rows):
    levels, lon_cells, lat_cells = out.shape
    half = lon_cells // 2
    f32 = jnp.float32
    for x in range(half):
        for c, lanes in enumerate(rows):
            at = x * lat_cells + c * LANES
            cols = slice(at, at + LANES)
            mine = own[:, cols] + arrived2[:, cols].astype(f32)
            other = arrived1[:, cols].astype(f32) + arrived3[:, cols].astype(f32)
            lanes[pl.ds(place[1] * half + x, levels, stride=lon_cells), :] = mine
            lanes[pl.ds((1 - place[1]) * half + x, levels, stride=lon_cells), :] = other

    def one(z, carry):
        at = pl.multiple_of(z * lon_cells, lon_cells)
        for c, lanes in enumerate(rows):
            out[z, :, c * LANES : (c + 1) * LANES] = lanes[pl.ds(at, lon_cells), :]
        return carry

    lax.fori_loop(0, levels, one, 0, unroll=4)


def call(kernel, operands, in_specs, outs, grant=GRANT, flops=0, moved=1 << 20, scratch=(), aliases=None):
    return pl.pallas_call(
        kernel,
        in_specs=in_specs,
        out_shape=[jax.ShapeDtypeStruct(*o[:2]) for o in outs],
        out_specs=[o[2] if len(o) > 2 else VMEM for o in outs],
        scratch_shapes=list(scratch),
        input_output_aliases=aliases or {},
        compiler_params=pltpu.CompilerParams(vmem_limit_bytes=grant),
        cost_estimate=pl.CostEstimate(flops=flops, bytes_accessed=moved, transcendentals=0),
    )(*operands)


def per_device(
    innovations, courant, diffusivity, sea_bricks, tile_ranks, row_factors, column_factors
):
    levels, lon_cells, lat_cells = diffusivity.shape
    tile_cols = lon_cells * lat_cells
    half = tile_cols // 2
    slots = tile_ranks.shape[1]
    count = lax.axis_size("depth")
    lon_count = lax.axis_size("lon")
    f32, bf16 = jnp.float32, jnp.bfloat16
    left = row_factors.transpose(0, 1, 3, 2)
    right = column_factors.transpose(0, 1, 3, 2)
    width = left.shape[2]
    rows = slots * width

    down, up, sea, place, left_other, *right_other = pack(
        innovations, courant, diffusivity, sea_bricks, left, right
    )
    left_pair = swapped(left_other, "depth", 1)
    right_pair = []
    for part in range(PARTS):
        right_pair.append(swapped(right_other[part], "depth", 1).reshape(rows // PARTS, half))
    lam, lam_mine, lam_other = sweep(innovations, courant, diffusivity, sea, down, up, place)
    left_pair = left_pair.reshape(rows, half)
    left, right = left.reshape(rows, tile_cols), right.reshape(rows, tile_cols)
    blocks = {0: lam_mine}
    for mask in [1] + list(range(count - 1, 1, -1)):
        blocks[mask] = swapped(lam_other if mask % 2 else lam_mine, "depth", mask)
    sums = []
    for stage in range(0, count, 2):
        pair = (2, rows, 2 * levels)
        kept, sent = call(
            rows_kernel,
            (place, left, left_pair, blocks[stage], blocks[stage + 1]),
            [SMEM] + [VMEM] * 4,
            [(pair, f32), (pair, bf16)],
            flops=8 * rows * half * levels,
            moved=3 << 20,
        )
        sums += [kept, swapped(sent, "depth", 1)]
    grouped = lon_count == slots
    slot = (2, width, count * levels)
    coeff = call(
        functools.partial(mask_kernel, slots),
        (place, tile_ranks, *sums),
        [SMEM, SMEM] + [VMEM] * len(sums),
        [((lon_count,) + slot, bf16)] if grouped else [(slot, bf16)] * slots,
    )
    if grouped:
        received = [lax.all_to_all(coeff[0], "lon", 0, 0, tiled=True)]
    else:
        received = [shifted(coeff[k], "lon", k - slots // 2) for k in range(slots)]
    arrived, own = {}, None
    block = (levels, half)
    for stage in range(count - 2, -1, -2):
        first, second = call(
            functools.partial(columns_kernel, slots, 4 * LANES, stage),
            (place, right, *right_pair, *received),
            [SMEM] + [VMEM] * (1 + PARTS + len(received)),
            [(block, bf16 if stage else f32), (block, bf16)],
            flops=8 * rows * half * levels,
            moved=3 << 20,
        )
        arrived[stage + 1] = swapped(second, "depth", stage + 1)
        if stage:
            arrived[stage] = swapped(first, "depth", stage)
        else:
            own = first
    (gradient,) = call(
        join_kernel,
        (place, own, *(arrived[mask] for mask in range(1, count))),
        [SMEM] + [VMEM] * count,
        [((levels, lon_cells, lat_cells), f32)],
        scratch=[pltpu.VMEM((levels * lon_cells, LANES), f32)] * (lat_cells // LANES),
        moved=4 << 20,
    )
    return (lam, gradient)


def solution(mesh):
    placed = (
        P(None, "depth", "lon", None),
        P(None, "depth", "lon", None),
        P("depth", "lon", None),
        P("depth", "lon", None),
        P("lon", None),
        P("lon", None, None, "depth"),
        P("lon", None, None, "depth"),
    )
    return jax.shard_map(
        per_device,
        mesh=mesh,
        in_specs=placed,
        out_specs=(P("depth", "lon", None), P("depth", "lon", None)),
        check_vma=False,
    )
```

```python
import functools
import jax
import jax.numpy as jnp
from jax import lax
from jax.experimental import pallas as pl
from jax.experimental.pallas import tpu as pltpu
from jax.sharding import PartitionSpec as P

UNROLL = 9
LANES = 128
PARTS = 4
STAGES = 2
LANE_TILES = 2
HALVES = 2
GRANT = 4 << 20
VMEM = pl.BlockSpec(memory_space=pltpu.VMEM)
SMEM = pl.BlockSpec(memory_space=pltpu.SMEM)
ANY = pl.BlockSpec(memory_space=pl.ANY)


def from_behind(value, axis, steps):
    count = lax.axis_size(axis)
    initial, last = (max(0, -steps), min(count, count - steps))
    return lax.ppermute(value, axis, [(source, source + steps) for source in range(initial, last)])


def shifted(block, axis, distance):
    devices = range(lax.axis_size(axis))
    if distance % len(devices) == 0:
        return block
    route = [((i - distance) % len(devices), i) for i in devices]
    return lax.ppermute(block, axis, route)


def swapped(block, axis, mask):
    return lax.ppermute(block, axis, [(i, i ^ mask) for i in range(lax.axis_size(axis))])


def halo_table(depth):
    order, at = {}, 0
    for name, extent in (
        [(("innov", k), k) for k in range(depth, 0, -1)]
        + [("diff", depth), ("c0", depth), ("c1", depth - 1), ("c2", depth - 1)]
    ):
        for distance in range(1, extent + 1):
            order[name, distance] = at
            at += 1
    order["sea"] = at
    return order, at + 1


def pack_kernel(table, axes, bricks, innov_lo, innov_hi, cour_lo, cour_hi, diff_lo, diff_hi, left, down, up, sea, place, left_other, rows, vmem, sems):
    me = lax.axis_index(axes[1])
    side = lax.rem(me, 2)
    place[0], place[1], place[2] = me, side, lax.axis_index(axes[0])
    half = left_other.shape[2]
    start = pl.multiple_of((1 - side) * half, half)
    load = pltpu.make_async_copy(left.at[0, :, :, pl.ds(start, half)], vmem, sems.at[0])
    load.start()
    depth = diff_lo.shape[0]
    levels, _, count = bricks.shape
    lat_cells = sea.shape[2]
    for z in range(levels):
        rows[z : z + 1] = bricks[z].astype(jnp.float32)
    brick_at = lax.broadcasted_iota(jnp.int32, (count, lat_cells), 0)
    cell_at = lax.broadcasted_iota(jnp.int32, (count, lat_cells), 1)
    inside = (brick_at == cell_at // (lat_cells // count)).astype(jnp.bfloat16)
    wide = jnp.dot(rows[...].astype(jnp.bfloat16), inside, preferred_element_type=jnp.float32)
    for z in range(levels):
        sea[z] = wide[z : z + 1]
    sea_lo, sea_hi = sea, sea.at[pl.ds(levels - depth, depth)]

    def fill(out, innov, cour, diff, sea, level):
        for key, at in table.items():
            if key == "sea":
                rows = [sea[level(d)] for d in range(1, depth + 1)]
                rows.append(jnp.zeros((out.shape[1] - depth, out.shape[2]), jnp.float32))
                value = jnp.concatenate(rows, 0)
            else:
                name, distance = key
                z = level(distance)
                if name == "diff":
                    value = diff[z]
                elif name == "c0":
                    value = cour[0, z]
                elif name == "c1":
                    value = cour[1, z]
                elif name == "c2":
                    value = cour[2, z]
                else:
                    value = innov[name[1], z]
            out[at] = value.astype(jnp.bfloat16)

    load.wait()
    store = pltpu.make_async_copy(vmem, left_other, sems.at[1])
    store.start()
    fill(down, innov_hi, cour_hi, diff_hi, sea_hi, lambda d: depth - d)
    fill(up, innov_lo, cour_lo, diff_lo, sea_lo, lambda d: d - 1)
    store.wait()


def halves_kernel(place, right, *rest):
    targets, (vmem, sems) = rest[:-2], rest[-2:]
    wide = targets[0].shape[2]
    start = (1 - place[1]) * wide * len(targets)
    loads, stores = [], []
    for n, target in enumerate(targets):
        window = pl.ds(pl.multiple_of(start + n * wide, wide), wide)
        loads.append(pltpu.make_async_copy(right.at[0, :, :, window], vmem.at[n], sems.at[n]))
        loads[-1].start()
        stores.append(pltpu.make_async_copy(vmem.at[n], target, sems.at[len(targets) + n]))
    for load, store in zip(loads, stores):
        load.wait()
        store.start()
    for store in stores:
        store.wait()


def load_kernel(*refs):
    count = len(refs) // 2
    copies = [pltpu.make_async_copy(refs[n], refs[count + n], refs[-1].at[n]) for n in range(count)]
    for copy in copies:
        copy.start()
    for copy in copies:
        copy.wait()


def first_kernel(table, innov, cour, diff, sea, before, after, sea_ext, east_gain, west_gain, to_east, to_west):
    steps = innov.shape[0] - 1
    levels, lon_cells, lat_cells = diff.shape
    last = lon_cells - 1

    def put(at, sea_row, diff_a, diff_b, cour_a, cour_b, innov_a, innov_b):
        sea_ext[at] = sea_row
        low_row, high_row = sea_row * innov_a, sea_row * innov_b
        west = diff_a + 0.5 * cour_a
        east = diff_b - 0.5 * cour_b
        west_gain[at], east_gain[at] = west, east
        to_west[at], to_east[at] = west * low_row, east * high_row

    for halo, where in ((before, lambda d: steps - d), (after, lambda d: steps + levels + d - 1)):
        sea_rows = halo[table["sea"]].astype(jnp.float32)
        for d in range(1, steps + 1):
            sea_row = sea_rows[d - 1 : d]
            at = where(d)
            if d == steps:
                zero = jnp.zeros((1, lat_cells), jnp.float32)
                sea_ext[at] = sea_row
                west_gain[at], east_gain[at], to_west[at], to_east[at] = zero, zero, zero, zero
            else:
                dd = halo[table["diff", d]].astype(jnp.float32)
                cc = halo[table["c1", d]].astype(jnp.float32)
                ii = halo[table[("innov", steps), d]].astype(jnp.float32)
                put(at, sea_row, dd[:1], dd[last:], cc[:1], cc[last:], ii[:1], ii[last:])

    def one(z, carry):
        edge = lambda ref: (ref[z, :1], ref[z, last:])
        put(z + steps, sea[z], *edge(diff), *edge(cour.at[1]), *edge(innov.at[steps]))
        return carry

    lax.fori_loop(0, levels, one, 0, unroll=4)


def step_kernel(table, step, innov, cour, diff, sea_ext, before, after, low, high, *rest):
    steps = innov.shape[0] - 1
    levels, lon_cells, lat_cells = diff.shape
    if step > 1:
        lam, rest = rest[0], rest[1:]
    out, out_low, out_high = rest
    last = lon_cells - 1
    x_at = lax.broadcasted_iota(jnp.int32, (lon_cells, lat_cells), 0)
    y_at = lax.broadcasted_iota(jnp.int32, (lon_cells, lat_cells), 1)
    first_x, last_x = x_at == 0, x_at == last
    first_y, last_y = y_at == 0, y_at == lat_cells - 1
    reach = steps - step

    def halo_level(halo, d, name):
        return halo[table[name, d]].astype(jnp.float32)

    def state(at, innovation):
        if step == 1:
            return sea_ext[at] * innovation
        value = jnp.where(first_x, low[at], lam[at])
        return jnp.where(last_x, high[at], value)

    def finish(at, acc, up_flux):
        value = sea_ext[at] * (acc + up_flux)
        out[at] = value
        out_low[at] = value[:1]
        out_high[at] = value[last:]

    def depth_terms(a, d, c):
        spread, drift = d * a, c * (0.5 * a)
        return spread - drift, spread + drift

    def level(a, d, c0, c1, c2, innovation):
        half = 0.5 * a
        spread = d * a
        drift = c0 * half
        plus0, minus0 = spread - drift, spread + drift
        drift = c1 * half
        plus1, minus1 = spread - drift, spread + drift
        drift = c2 * half
        plus2, minus2 = spread - drift, spread + drift
        acc = a - 6.0 * spread + innovation
        acc = acc + jnp.where(first_x, 0.0, pltpu.roll(plus1, 1, 0))
        acc = acc + jnp.where(last_x, 0.0, pltpu.roll(minus1, lon_cells - 1, 0))
        acc = acc + jnp.where(first_y, 0.0, pltpu.roll(plus2, 1, 1))
        acc = acc + jnp.where(last_y, 0.0, pltpu.roll(minus2, lat_cells - 1, 1))
        return acc, plus0, minus0

    def halo_full(halo, d, at):
        a = state(at, halo_level(halo, d, ("innov", steps)))
        return level(
            a,
            halo_level(halo, d, "diff"),
            halo_level(halo, d, "c0"),
            halo_level(halo, d, "c1"),
            halo_level(halo, d, "c2"),
            halo_level(halo, d, ("innov", steps - step)),
        )

    def halo_edge(halo, d, at):
        a = state(at, halo_level(halo, d, ("innov", steps)))
        return depth_terms(a, halo_level(halo, d, "diff"), halo_level(halo, d, "c0"))

    down_flux, _ = halo_edge(before, reach + 1, steps - reach - 1)
    acc = None
    for d in range(reach, 0, -1):
        at = steps - d
        value, plus0, minus0 = halo_full(before, d, at)
        if acc is not None:
            finish(at - 1, acc, minus0)
        acc, down_flux = value + down_flux, plus0

    def own(z):
        a = state(z + steps, innov[steps, z])
        return level(a, diff[z], cour[0, z], cour[1, z], cour[2, z], innov[steps - step, z])

    value, plus0, minus0 = own(0)
    if acc is not None:
        finish(steps - 1, acc, minus0)
    carry = (value + down_flux, plus0)

    def one(z, carry):
        acc, down_flux = carry
        value, plus0, minus0 = own(z)
        finish(z + steps - 1, acc, minus0)
        return value + down_flux, plus0

    head = (levels - 1) % UNROLL
    for z in range(1, 1 + head):
        carry = one(z, carry)

    def several(i, carry):
        for u in range(UNROLL):
            carry = one(1 + head + i * UNROLL + u, carry)
        return carry

    acc, down_flux = lax.fori_loop(0, (levels - 1) // UNROLL, several, carry)
    at = steps + levels - 1
    for d in range(1, reach + 1):
        value, plus0, minus0 = halo_full(after, d, at + d)
        finish(at + d - 1, acc, minus0)
        acc, down_flux = value + down_flux, plus0
    _, up_flux = halo_edge(after, reach + 1, at + reach + 1)
    finish(at + reach, acc, up_flux)


def lay_kernel(place, lam, mine, other, *rows):
    levels = mine.shape[0]
    total, lon_cells, lat_cells = lam.shape
    steps = (total - levels) // 2

    def one(z, carry):
        value = lam[z + steps]
        for c, lanes in enumerate(rows):
            at = pl.multiple_of(z * lon_cells, lon_cells)
            lanes[pl.ds(at, lon_cells), :] = value[:, c * LANES : (c + 1) * LANES]
        return carry

    lax.fori_loop(0, levels, one, 0, unroll=4)
    half = lon_cells // 2
    for part, start in ((mine, place[1] * half), (other, (1 - place[1]) * half)):
        for x in range(half):
            for c, lanes in enumerate(rows):
                picked = lanes[pl.ds(start + x, levels, stride=lon_cells), :]
                at = x * lat_cells + c * LANES
                part[:, at : at + LANES] = picked.astype(jnp.bfloat16)


def fix_kernel(place, sea_ext, out_low, out_high, west, east, mine_in, other_in, mine, other, low_rows, high_rows):
    levels, half = mine.shape
    lat_cells = low_rows.shape[1]
    steps = (sea_ext.shape[0] - levels) // 2
    for z in range(levels):
        at = z + steps
        low_rows[z : z + 1] = out_low[at] + sea_ext[at] * west[at]
        high_rows[z : z + 1] = out_high[at] + sea_ext[at] * east[at]
    low = low_rows[...].astype(jnp.bfloat16)
    high = high_rows[...].astype(jnp.bfloat16)

    @pl.when(place[1] == 0)
    def _():
        mine[:, :lat_cells] = low
        other[:, half - lat_cells :] = high

    @pl.when(place[1] != 0)
    def _():
        other[:, :lat_cells] = low
        mine[:, half - lat_cells :] = high


def emit_kernel(lam, sea_ext, out_low, out_high, west, east, out):
    levels, lon_cells, lat_cells = out.shape
    steps = (lam.shape[0] - levels) // 2
    x_at = lax.broadcasted_iota(jnp.int32, (lon_cells, lat_cells), 0)
    first_x, last_x = x_at == 0, x_at == lon_cells - 1

    def one(z, carry):
        at = z + steps
        low = out_low[at] + sea_ext[at] * west[at]
        high = out_high[at] + sea_ext[at] * east[at]
        out[z] = jnp.where(last_x, high, jnp.where(first_x, low, lam[at]))
        return carry

    lax.fori_loop(0, levels, one, 0, unroll=4)


def face_kernel(sea_ext, out_low, out_high, west, east, west_gain, east_gain, low, high, to_west, to_east):
    low_rows = out_low[...] + sea_ext[...] * west[...]
    high_rows = out_high[...] + sea_ext[...] * east[...]
    low[...], high[...] = low_rows, high_rows
    to_west[...], to_east[...] = west_gain[...] * low_rows, east_gain[...] * high_rows


def pack(innovations, courant, diffusivity, bricks, left):
    levels, lon_cells, lat_cells = diffusivity.shape
    steps = innovations.shape[0] - 1
    table, layers = halo_table(steps)
    f32, bf16 = jnp.float32, jnp.bfloat16
    end = levels // steps - 1

    def edges(shape, axis):
        block = list(shape)
        block[axis] = steps
        at = lambda index: lambda i: tuple(index if a == axis else 0 for a in range(len(shape)))
        return [pl.BlockSpec(tuple(block), at(index)) for index in (0, end)]

    message = jax.ShapeDtypeStruct((layers, lon_cells, lat_cells), bf16)
    _, slots, width, cols = left.shape
    other = jax.ShapeDtypeStruct((slots, width, cols // 2), bf16)
    return pl.pallas_call(
        functools.partial(pack_kernel, table, ("lon", "depth")),
        grid=(1,),
        in_specs=[VMEM]
        + edges(innovations.shape, 1)
        + edges(courant.shape, 1)
        + edges(diffusivity.shape, 0)
        + [ANY],
        out_shape=[
            message,
            message,
            jax.ShapeDtypeStruct((levels, 1, lat_cells), f32),
            jax.ShapeDtypeStruct((3,), jnp.int32),
            other,
        ],
        out_specs=[VMEM, VMEM, VMEM, SMEM, ANY],
        scratch_shapes=[
            pltpu.VMEM((levels, bricks.shape[2]), f32),
            pltpu.VMEM((slots, width, cols // 2), bf16),
            pltpu.SemaphoreType.DMA((2,)),
        ],
        cost_estimate=pl.CostEstimate(flops=0, bytes_accessed=1 << 20, transcendentals=0),
    )(bricks, innovations, innovations, courant, courant, diffusivity, diffusivity, left)


def sweep(innovations, courant, diffusivity, sea, down, up, place):
    levels, lon_cells, lat_cells = diffusivity.shape
    steps = innovations.shape[0] - 1
    table, _ = halo_table(steps)
    f32, bf16 = jnp.float32, jnp.bfloat16
    before = from_behind(down, "depth", 1)
    after = from_behind(up, "depth", -1)
    row = jax.ShapeDtypeStruct((levels + 2 * steps, 1, lat_cells), f32)
    cells = jax.ShapeDtypeStruct((levels + 2 * steps, lon_cells, lat_cells), f32)
    inputs = (innovations, courant, diffusivity)
    inputs = call(
        load_kernel,
        inputs,
        [ANY] * 3,
        [(a.shape, a.dtype) for a in inputs],
        grant=40 << 20,
        moved=18 << 20,
        scratch=[pltpu.SemaphoreType.DMA((3,))],
    )
    sea_ext, east_gain, west_gain, to_east, to_west = pl.pallas_call(
        functools.partial(first_kernel, table),
        in_specs=[VMEM] * 6,
        out_shape=[row] * 5,
        out_specs=[VMEM] * 5,
        compiler_params=pltpu.CompilerParams(vmem_limit_bytes=GRANT),
        cost_estimate=pl.CostEstimate(flops=0, bytes_accessed=1 << 20, transcendentals=0),
    )(*inputs, sea, before, after)
    lam = ()
    low = high = sea_ext
    for step in range(1, steps + 1):
        west = shifted(to_east, "lon", 1)
        east = shifted(to_west, "lon", -1)
        state = (low, high) + lam
        out, out_low, out_high = pl.pallas_call(
            functools.partial(step_kernel, table, step),
            in_specs=[VMEM] * (6 + len(state)),
            out_shape=[cells, row, row],
            out_specs=[VMEM] * 3,
            compiler_params=pltpu.CompilerParams(vmem_limit_bytes=GRANT),
            cost_estimate=pl.CostEstimate(flops=40 * levels * lon_cells * lat_cells, bytes_accessed=9 << 20, transcendentals=0),
        )(*inputs, sea_ext, before, after, *state)
        if step == steps:
            break
        low, high, to_west, to_east = pl.pallas_call(
            face_kernel,
            in_specs=[VMEM] * 7,
            out_shape=[row] * 4,
            out_specs=[VMEM] * 4,
            compiler_params=pltpu.CompilerParams(vmem_limit_bytes=GRANT),
            cost_estimate=pl.CostEstimate(flops=0, bytes_accessed=1 << 19, transcendentals=0),
        )(sea_ext, out_low, out_high, west, east, west_gain, east_gain)
        lam = (out,)
    half = (levels, lon_cells * lat_cells // 2)
    mine, other = call(
        lay_kernel,
        (place, out),
        [SMEM, VMEM],
        [(half, bf16)] * 2,
        scratch=[pltpu.VMEM((levels * lon_cells, LANES), f32)] * (lat_cells // LANES),
        moved=3 << 20,
    )
    edge = (sea_ext, out_low, out_high, west, east)
    mine, other = call(
        fix_kernel,
        (place, *edge, mine, other),
        [SMEM] + [VMEM] * 7,
        [(half, bf16)] * 2,
        scratch=[pltpu.VMEM((levels, lat_cells), f32)] * 2,
        aliases={6: 0, 7: 1},
    )
    (lam,) = call(
        emit_kernel,
        (out, *edge),
        [VMEM] * 6,
        [((levels, lon_cells, lat_cells), f32)],
        moved=3 << 20,
    )
    return lam, mine, other


def against(a, b):
    return lax.dot_general(a, b, (((1,), (1,)), ((), ())), preferred_element_type=jnp.float32)


def rows_kernel(wide, place, left, left_pair, first, second, kept, sent):
    half = left_pair.shape[1]
    levels = first.shape[0]
    sums = [None, None]
    for at in range(0, half, wide):
        lanes = slice(at, at + wide)
        mine = left[:, pl.ds(pl.multiple_of(place[1] * half + at, LANES), wide)]
        both = jnp.concatenate([first[:, lanes], second[:, lanes]], 0)
        for c, factor in enumerate((mine, left_pair[:, lanes])):
            term = against(factor, both)
            sums[c] = term if at == 0 else sums[c] + term
    for c in range(2):
        kept[c] = sums[c]
        other_order = [sums[c][:, levels:], sums[c][:, :levels]]
        sent[1 - c] = jnp.concatenate(other_order, 1).astype(jnp.bfloat16)


def mask_kernel(slots, place, ranks, *rest):
    stages = [rest[n : n + 2] for n in range(0, STAGES * 2, 2)]
    out = rest[STAGES * 2 :]
    rows = stages[0][0].shape[1] // slots
    for c in range(2):
        owner = place[0] if c == 0 else place[0] + 1 - 2 * place[1]
        for k in range(slots):
            at = slice(k * rows, (k + 1) * rows)
            value = jnp.concatenate(
                [kept[c, at, :] + arrived[c, at, :].astype(jnp.float32) for kept, arrived in stages], 1
            )
            row = lax.broadcasted_iota(jnp.int32, value.shape, 0) + owner * rows
            value = jnp.where(row < ranks[0, k], value, 0.0).astype(jnp.bfloat16)
            if len(out) > 1:
                out[k][c] = value
            else:
                count = out[0].shape[0]
                out[0][lax.rem(place[2] + (k - slots // 2 + count), count), c] = value


def columns_kernel(slots, stage, start, place, right, *rest):
    pieces = PARTS // HALVES
    right_pair, received, out = rest[:pieces], rest[pieces:-2], rest[-2:]
    count = received[0].shape[0]
    levels = out[0].shape[0]
    wide = right_pair[0].shape[1]
    half = wide * PARTS
    picked = slice(stage * levels, (stage + 2) * levels)
    coeffs = []
    for c in range(2):
        for k in range(slots):
            if len(received) > 1:
                coeffs.append(received[k][c, :, picked])
            else:
                source = lax.rem(place[2] + (count + slots // 2 - k), count)
                coeffs.append(received[0][source, c, :, picked])
    stacked = jnp.concatenate(coeffs, 0)
    rows = right.shape[0]
    lead = (((0,), (0,)), ((), ()))
    for n, piece in enumerate(right_pair):
        lanes = slice(n * wide, (n + 1) * wide)
        mine = right[:, pl.ds(pl.multiple_of(place[1] * half + start + n * wide, LANES), wide)]
        total = lax.dot_general(stacked[:rows], mine, lead, preferred_element_type=jnp.float32)
        total = total + lax.dot_general(stacked[rows:], piece[...], lead, preferred_element_type=jnp.float32)
        out[0][:, lanes] = total[:levels].astype(out[0].dtype)
        out[1][:, lanes] = total[levels:].astype(out[1].dtype)


def join_kernel(flip, place, *rest):
    ones, twos = rest[:HALVES], rest[HALVES : 2 * HALVES]
    out, slab, sem, *rows = rest[-(3 + LANE_TILES) :]
    levels, half, lat_cells = slab.shape
    f32 = jnp.float32
    each = half // HALVES
    for x in range(half):
        for c, lanes in enumerate(rows):
            at = (x % each) * lat_cells + c * LANES
            cols = slice(at, at + LANES)
            value = ones[x // each][:, cols].astype(f32) + twos[x // each][:, cols].astype(f32)
            lanes[pl.ds(x, levels, stride=half), :] = value
    side = 1 - place[1] if flip else place[1]
    start = pl.multiple_of(side * half, half)
    parts = 4
    size = levels // parts
    copies = []
    for part in range(parts):
        for z in range(part * size, (part + 1) * size):
            for c, lanes in enumerate(rows):
                slab[z, :, c * LANES : (c + 1) * LANES] = lanes[z * half : (z + 1) * half, :]
        here = pl.ds(part * size, size)
        target = out.at[here, pl.ds(start, half)]
        copies.append(pltpu.make_async_copy(slab.at[here], target, sem.at[part]))
        copies[-1].start()
    for copy in copies:
        copy.wait()


def call(kernel, operands, in_specs, outs, grant=GRANT, flops=0, moved=1 << 20, scratch=(), aliases=None):
    return pl.pallas_call(
        kernel,
        in_specs=in_specs,
        out_shape=[jax.ShapeDtypeStruct(*o[:2]) for o in outs],
        out_specs=[o[2] if len(o) > 2 else VMEM for o in outs],
        scratch_shapes=list(scratch),
        input_output_aliases=aliases or {},
        compiler_params=pltpu.CompilerParams(vmem_limit_bytes=grant),
        cost_estimate=pl.CostEstimate(flops=flops, bytes_accessed=moved, transcendentals=0),
    )(*operands)


def per_device(
    innovations, courant, diffusivity, sea_bricks, tile_ranks, row_factors, column_factors
):
    levels, lon_cells, lat_cells = diffusivity.shape
    tile_cols = lon_cells * lat_cells
    half = tile_cols // 2
    slots = tile_ranks.shape[1]
    count = lax.axis_size("depth")
    lon_count = lax.axis_size("lon")
    f32, bf16 = jnp.float32, jnp.bfloat16
    left = row_factors.transpose(0, 1, 3, 2)
    right = column_factors.transpose(0, 1, 3, 2)
    width = left.shape[2]
    rows = slots * width

    down, up, sea, place, left_other = pack(innovations, courant, diffusivity, sea_bricks, left)
    right_other = call(
        halves_kernel,
        (place, right),
        [SMEM, ANY],
        [((slots, width, half // PARTS), bf16, ANY)] * PARTS,
        moved=4 << 20,
        scratch=[pltpu.VMEM((PARTS, slots, width, half // PARTS), bf16), pltpu.SemaphoreType.DMA((2 * PARTS,))],
    )
    left_pair = swapped(left_other, "depth", 1)
    right_pair = []
    for part in range(PARTS):
        right_pair.append(swapped(right_other[part], "depth", 1).reshape(rows, half // PARTS))
    lam, lam_mine, lam_other = sweep(innovations, courant, diffusivity, sea, down, up, place)
    left_pair = left_pair.reshape(rows, half)
    left, right = left.reshape(rows, tile_cols), right.reshape(rows, tile_cols)
    blocks = {0: lam_mine}
    for mask in range(count - 1, 0, -1):
        blocks[mask] = swapped(lam_other if mask % 2 else lam_mine, "depth", mask)
    sums = []
    for stage in range(0, count, 2):
        pair = (2, rows, 2 * levels)
        kept, sent = call(
            functools.partial(rows_kernel, 4 * LANES),
            (place, left, left_pair, blocks[stage], blocks[stage + 1]),
            [SMEM] + [VMEM] * 4,
            [(pair, f32), (pair, bf16)],
            flops=8 * rows * half * levels,
            moved=3 << 20,
        )
        sums += [kept, swapped(sent, "depth", 1)]
    grouped = lon_count == slots
    slot = (2, width, count * levels)
    coeff = call(
        functools.partial(mask_kernel, slots),
        (place, tile_ranks, *sums),
        [SMEM, SMEM] + [VMEM] * len(sums),
        [((lon_count,) + slot, bf16)] if grouped else [(slot, bf16)] * slots,
    )
    if grouped:
        received = [lax.all_to_all(coeff[0], "lon", 0, 0, tiled=True)]
    else:
        received = [shifted(coeff[k], "lon", k - slots // 2) for k in range(slots)]
    arrived = {mask: [] for mask in range(count)}
    block = (levels, half // HALVES)
    pieces = PARTS // HALVES
    for part in range(HALVES):
        for stage in range(count - 2, -1, -2):
            first, second = call(
                functools.partial(columns_kernel, slots, stage, part * (half // HALVES)),
                (place, right, *right_pair[part * pieces : (part + 1) * pieces], *received),
                [SMEM] + [VMEM] * (1 + pieces + len(received)),
                [(block, bf16 if stage else f32), (block, bf16)],
                flops=8 * rows * half * levels // HALVES,
                moved=2 << 20,
            )
            arrived[stage + 1].append(swapped(second, "depth", stage + 1))
            if stage:
                first = swapped(first, "depth", stage)
            arrived[stage].append(first)
    scratch = [
        pltpu.VMEM((levels, lon_cells // 2, lat_cells), f32),
        pltpu.SemaphoreType.DMA((4,)),
    ] + [pltpu.VMEM((levels * lon_cells // 2, LANES), f32)] * LANE_TILES
    whole = [((levels, lon_cells, lat_cells), f32, ANY)]
    (gradient,) = call(
        functools.partial(join_kernel, True),
        (place, *arrived[1], *arrived[3]),
        [SMEM] + [VMEM] * (2 * HALVES),
        whole,
        scratch=scratch,
        moved=2 << 20,
    )
    (gradient,) = call(
        functools.partial(join_kernel, False),
        (place, *arrived[0], *arrived[2], gradient),
        [SMEM] + [VMEM] * (2 * HALVES) + [ANY],
        whole,
        scratch=scratch,
        moved=2 << 20,
        aliases={1 + 2 * HALVES: 0},
    )
    return (lam, gradient)


def solution(mesh):
    placed = (
        P(None, "depth", "lon", None),
        P(None, "depth", "lon", None),
        P("depth", "lon", None),
        P("depth", "lon", None),
        P("lon", None),
        P("lon", None, None, "depth"),
        P("lon", None, None, "depth"),
    )
    return jax.shard_map(
        per_device,
        mesh=mesh,
        in_specs=placed,
        out_specs=(P("depth", "lon", None), P("depth", "lon", None)),
        check_vma=False,
    )
```

```python
import functools
import jax
import jax.numpy as jnp
from jax import lax
from jax.experimental import pallas as pl
from jax.experimental.pallas import tpu as pltpu
from jax.sharding import PartitionSpec as P

UNROLL = 9
LANES = 128
PARTS = 4
LOAD_GRANT = 40 << 20
STAGES = 2
LANE_TILES = 2
HALVES = 2
GRANT = 4 << 20
VMEM = pl.BlockSpec(memory_space=pltpu.VMEM)
SMEM = pl.BlockSpec(memory_space=pltpu.SMEM)
ANY = pl.BlockSpec(memory_space=pl.ANY)


def from_behind(value, axis, steps):
    count = lax.axis_size(axis)
    initial, last = (max(0, -steps), min(count, count - steps))
    return lax.ppermute(value, axis, [(source, source + steps) for source in range(initial, last)])


def shifted(block, axis, distance):
    devices = range(lax.axis_size(axis))
    if distance % len(devices) == 0:
        return block
    route = [((i - distance) % len(devices), i) for i in devices]
    return lax.ppermute(block, axis, route)


def swapped(block, axis, mask):
    return lax.ppermute(block, axis, [(i, i ^ mask) for i in range(lax.axis_size(axis))])


def halo_table(depth):
    order, at = {}, 0
    for name, extent in (
        [(("innov", k), min(k, depth - 1)) for k in range(depth, 0, -1)]
        + [("diff", depth - 1), ("c0", depth - 1), ("c1", depth - 1), ("c2", depth - 1)]
    ):
        for distance in range(1, extent + 1):
            order[name, distance] = at
            at += 1
    order["sea"], order["flux"] = at, at + 1
    return order, at + 2


def row(ref, at):
    return ref[pl.ds(at, 1), :]


def pack_kernel(table, axes, bricks, innov_lo, innov_hi, cour_lo, cour_hi, diff_lo, diff_hi, left, down, up, sea, place, left_other, rows, vmem, sems):
    me = lax.axis_index(axes[1])
    side = lax.rem(me, 2)
    place[0], place[1], place[2] = me, side, lax.axis_index(axes[0])
    half = left_other.shape[2]
    window = pl.ds(pl.multiple_of((1 - side) * half, half), half)
    load = pltpu.make_async_copy(left.at[0, :, :, window], vmem, sems.at[0])
    load.start()
    depth = diff_lo.shape[0]
    levels, _, count = bricks.shape
    lat_cells = sea.shape[1]
    for z in range(levels):
        rows[z : z + 1] = bricks[z].astype(jnp.float32)
    brick_at = lax.broadcasted_iota(jnp.int32, (count, lat_cells), 0)
    cell_at = lax.broadcasted_iota(jnp.int32, (count, lat_cells), 1)
    inside = (brick_at == cell_at // (lat_cells // count)).astype(jnp.bfloat16)
    wide = jnp.dot(rows[...].astype(jnp.bfloat16), inside, preferred_element_type=jnp.float32)
    sea[...] = wide
    sea_lo, sea_hi = wide[:depth], wide[levels - depth :]

    def fill(out, innov, cour, diff, sea, level, sign):
        for key, at in table.items():
            if key == "sea":
                rows = [sea[level(d) : level(d) + 1] for d in range(1, depth + 1)]
                rows.append(jnp.zeros((out.shape[1] - depth, out.shape[2]), jnp.float32))
                value = jnp.concatenate(rows, 0)
            elif key == "flux":
                z = level(depth)
                gain = diff[z] + (0.5 * sign) * cour[0, z]
                value = gain * (sea[z : z + 1] * innov[innov.shape[0] - 1, z])
            else:
                name, distance = key
                z = level(distance)
                if name == "diff":
                    value = diff[z]
                elif name == "c0":
                    value = cour[0, z]
                elif name == "c1":
                    value = cour[1, z]
                elif name == "c2":
                    value = cour[2, z]
                else:
                    value = innov[name[1], z]
            out[at] = value.astype(jnp.bfloat16)

    fill(down, innov_hi, cour_hi, diff_hi, sea_hi, lambda d: depth - d, -1.0)
    load.wait()
    store = pltpu.make_async_copy(vmem, left_other, sems.at[1])
    store.start()
    fill(up, innov_lo, cour_lo, diff_lo, sea_lo, lambda d: d - 1, 1.0)
    store.wait()


def load_kernel(*refs):
    count = len(refs) // 2
    copies = [pltpu.make_async_copy(refs[n], refs[count + n], refs[-1].at[n]) for n in range(count)]
    for copy in copies:
        copy.start()
    for copy in copies:
        copy.wait()


def halves_kernel(place, right, *rest):
    targets, (vmem, sems) = rest[:-2], rest[-2:]
    wide = targets[0].shape[2]
    start = (1 - place[1]) * wide * len(targets)
    loads, stores = [], []
    for n, target in enumerate(targets):
        window = pl.ds(pl.multiple_of(start + n * wide, wide), wide)
        loads.append(pltpu.make_async_copy(right.at[0, :, :, window], vmem.at[n], sems.at[n]))
        loads[-1].start()
        stores.append(pltpu.make_async_copy(vmem.at[n], target, sems.at[len(targets) + n]))
    for load, store in zip(loads, stores):
        load.wait()
        store.start()
    for store in stores:
        store.wait()


def first_kernel(table, innov, cour, diff, sea, before, after, sea_ext, east_gain, west_gain, to_east, to_west, east_rows, west_rows):
    steps = innov.shape[0] - 1
    levels, lon_cells, lat_cells = diff.shape
    last = lon_cells - 1

    def put(at, sea_row, diff_a, diff_b, cour_a, cour_b, innov_a, innov_b):
        here = pl.ds(at, 1)
        sea_ext[here, :] = sea_row
        low_row, high_row = sea_row * innov_a, sea_row * innov_b
        west = diff_a + 0.5 * cour_a
        east = diff_b - 0.5 * cour_b
        west_gain[here, :], east_gain[here, :] = west, east
        west_rows[here, :], east_rows[here, :] = west * low_row, east * high_row

    for halo, where in ((before, lambda d: steps - d), (after, lambda d: steps + levels + d - 1)):
        sea_rows = halo[table["sea"]].astype(jnp.float32)
        for d in range(1, steps + 1):
            sea_row = sea_rows[d - 1 : d]
            at = where(d)
            if d == steps:
                zero = jnp.zeros((1, lat_cells), jnp.float32)
                for ref in (sea_ext, west_gain, east_gain, west_rows, east_rows):
                    ref[pl.ds(at, 1), :] = zero
            else:
                dd = halo[table["diff", d]].astype(jnp.float32)
                cc = halo[table["c1", d]].astype(jnp.float32)
                ii = halo[table[("innov", steps), d]].astype(jnp.float32)
                put(at, sea_row, dd[:1], dd[last:], cc[:1], cc[last:], ii[:1], ii[last:])

    def one(z, carry):
        edge = lambda ref: (ref[z, :1], ref[z, last:])
        put(z + steps, row(sea, z), *edge(diff), *edge(cour.at[1]), *edge(innov.at[steps]))
        return carry

    lax.fori_loop(0, levels, one, 0, unroll=4)
    to_west[...] = west_rows[...].astype(jnp.bfloat16)
    to_east[...] = east_rows[...].astype(jnp.bfloat16)


def step_kernel(table, step, innov, cour, diff, sea_ext, before, after, low, high, *rest):
    steps = innov.shape[0] - 1
    levels, lon_cells, lat_cells = diff.shape
    if step > 1:
        lam, rest = rest[0], rest[1:]
    out, out_low, out_high = rest
    last = lon_cells - 1
    x_at = lax.broadcasted_iota(jnp.int32, (lon_cells, lat_cells), 0)
    y_at = lax.broadcasted_iota(jnp.int32, (lon_cells, lat_cells), 1)
    first_x, last_x = x_at == 0, x_at == last
    first_y, last_y = y_at == 0, y_at == lat_cells - 1
    reach = steps - step

    def halo_level(halo, d, name):
        return halo[table[name, d]].astype(jnp.float32)

    def state(at, innovation):
        if step == 1:
            return row(sea_ext, at) * innovation
        value = jnp.where(first_x, row(low, at), lam[at])
        return jnp.where(last_x, row(high, at), value)

    def finish(at, acc, up_flux):
        value = row(sea_ext, at) * (acc + up_flux)
        out[at] = value
        out_low[pl.ds(at, 1), :] = value[:1]
        out_high[pl.ds(at, 1), :] = value[last:]

    def depth_terms(a, d, c):
        spread, drift = d * a, c * (0.5 * a)
        return spread - drift, spread + drift

    def level(a, d, c0, c1, c2, innovation):
        half = 0.5 * a
        spread = d * a
        drift = c0 * half
        plus0, minus0 = spread - drift, spread + drift
        drift = c1 * half
        plus1, minus1 = spread - drift, spread + drift
        drift = c2 * half
        plus2, minus2 = spread - drift, spread + drift
        acc = a - 6.0 * spread + innovation
        acc = acc + jnp.where(first_x, 0.0, pltpu.roll(plus1, 1, 0))
        acc = acc + jnp.where(last_x, 0.0, pltpu.roll(minus1, lon_cells - 1, 0))
        acc = acc + jnp.where(first_y, 0.0, pltpu.roll(plus2, 1, 1))
        acc = acc + jnp.where(last_y, 0.0, pltpu.roll(minus2, lat_cells - 1, 1))
        return acc, plus0, minus0

    def halo_start(halo, d, at):
        return state(at, halo_level(halo, d, ("innov", steps)) if step == 1 else None)

    def halo_full(halo, d, at):
        a = halo_start(halo, d, at)
        return level(
            a,
            halo_level(halo, d, "diff"),
            halo_level(halo, d, "c0"),
            halo_level(halo, d, "c1"),
            halo_level(halo, d, "c2"),
            halo_level(halo, d, ("innov", steps - step)),
        )

    def halo_edge(halo, d, at):
        if step == 1:
            flux = halo[table["flux"]].astype(jnp.float32)
            return flux, flux
        a = halo_start(halo, d, at)
        return depth_terms(a, halo_level(halo, d, "diff"), halo_level(halo, d, "c0"))

    down_flux, _ = halo_edge(before, reach + 1, steps - reach - 1)
    acc = None
    for d in range(reach, 0, -1):
        at = steps - d
        value, plus0, minus0 = halo_full(before, d, at)
        if acc is not None:
            finish(at - 1, acc, minus0)
        acc, down_flux = value + down_flux, plus0

    def own(z):
        a = state(z + steps, innov[steps, z] if step == 1 else None)
        return level(a, diff[z], cour[0, z], cour[1, z], cour[2, z], innov[steps - step, z])

    value, plus0, minus0 = own(0)
    if acc is not None:
        finish(steps - 1, acc, minus0)
    carry = (value + down_flux, plus0)

    def one(z, carry):
        acc, down_flux = carry
        value, plus0, minus0 = own(z)
        finish(z + steps - 1, acc, minus0)
        return value + down_flux, plus0

    head = (levels - 1) % UNROLL
    for z in range(1, 1 + head):
        carry = one(z, carry)

    def several(i, carry):
        for u in range(UNROLL):
            carry = one(1 + head + i * UNROLL + u, carry)
        return carry

    acc, down_flux = lax.fori_loop(0, (levels - 1) // UNROLL, several, carry)
    at = steps + levels - 1
    for d in range(1, reach + 1):
        value, plus0, minus0 = halo_full(after, d, at + d)
        finish(at + d - 1, acc, minus0)
        acc, down_flux = value + down_flux, plus0
    _, up_flux = halo_edge(after, reach + 1, at + reach + 1)
    finish(at + reach, acc, up_flux)


def lay_kernel(place, lam, mine, other, *rows):
    levels = mine.shape[0]
    total, lon_cells, lat_cells = lam.shape
    steps = (total - levels) // 2

    def one(z, carry):
        value = lam[z + steps]
        for c, lanes in enumerate(rows):
            at = pl.multiple_of(z * lon_cells, lon_cells)
            lanes[pl.ds(at, lon_cells), :] = value[:, c * LANES : (c + 1) * LANES]
        return carry

    lax.fori_loop(0, levels, one, 0, unroll=4)
    half = lon_cells // 2
    for part, start in ((mine, place[1] * half), (other, (1 - place[1]) * half)):
        for x in range(half):
            for c, lanes in enumerate(rows):
                picked = lanes[pl.ds(start + x, levels, stride=lon_cells), :]
                at = x * lat_cells + c * LANES
                part[:, at : at + LANES] = picked.astype(jnp.bfloat16)


def fix_kernel(place, sea_ext, out_low, out_high, west, east, mine_in, other_in, mine, other, low, high):
    levels, half = mine.shape
    lat_cells = low.shape[1]
    steps = (sea_ext.shape[0] - levels) // 2
    low[...] = out_low[...] + sea_ext[...] * west[...].astype(jnp.float32)
    high[...] = out_high[...] + sea_ext[...] * east[...].astype(jnp.float32)
    low_rows = low[steps : steps + levels, :].astype(jnp.bfloat16)
    high_rows = high[steps : steps + levels, :].astype(jnp.bfloat16)

    @pl.when(place[1] == 0)
    def _():
        mine[:, :lat_cells] = low_rows
        other[:, half - lat_cells :] = high_rows

    @pl.when(place[1] != 0)
    def _():
        other[:, :lat_cells] = low_rows
        mine[:, half - lat_cells :] = high_rows


def emit_kernel(lam, low, high, out):
    levels, lon_cells, lat_cells = out.shape
    steps = (lam.shape[0] - levels) // 2
    x_at = lax.broadcasted_iota(jnp.int32, (lon_cells, lat_cells), 0)
    first_x, last_x = x_at == 0, x_at == lon_cells - 1

    def one(z, carry):
        at = z + steps
        out[z] = jnp.where(last_x, row(high, at), jnp.where(first_x, row(low, at), lam[at]))
        return carry

    lax.fori_loop(0, levels, one, 0, unroll=4)


def face_kernel(sea_ext, out_low, out_high, west, east, west_gain, east_gain, low, high, to_west, to_east):
    low_rows = out_low[...] + sea_ext[...] * west[...].astype(jnp.float32)
    high_rows = out_high[...] + sea_ext[...] * east[...].astype(jnp.float32)
    low[...], high[...] = low_rows, high_rows
    to_west[...] = (west_gain[...] * low_rows).astype(jnp.bfloat16)
    to_east[...] = (east_gain[...] * high_rows).astype(jnp.bfloat16)


def pack(innovations, courant, diffusivity, bricks, left):
    levels, lon_cells, lat_cells = diffusivity.shape
    steps = innovations.shape[0] - 1
    table, layers = halo_table(steps)
    f32, bf16 = jnp.float32, jnp.bfloat16
    end = levels // steps - 1

    def edges(shape, axis):
        block = list(shape)
        block[axis] = steps
        at = lambda index: lambda i: tuple(index if a == axis else 0 for a in range(len(shape)))
        return [pl.BlockSpec(tuple(block), at(index)) for index in (0, end)]

    message = jax.ShapeDtypeStruct((layers, lon_cells, lat_cells), bf16)
    _, slots, width, cols = left.shape
    other = jax.ShapeDtypeStruct((slots, width, cols // 2), bf16)
    return pl.pallas_call(
        functools.partial(pack_kernel, table, ("lon", "depth")),
        grid=(1,),
        in_specs=[VMEM]
        + edges(innovations.shape, 1)
        + edges(courant.shape, 1)
        + edges(diffusivity.shape, 0)
        + [ANY],
        out_shape=[
            message,
            message,
            jax.ShapeDtypeStruct((levels, lat_cells), f32),
            jax.ShapeDtypeStruct((3,), jnp.int32),
            other,
        ],
        out_specs=[VMEM, VMEM, VMEM, SMEM, ANY],
        scratch_shapes=[
            pltpu.VMEM((levels, bricks.shape[2]), f32),
            pltpu.VMEM((slots, width, cols // 2), bf16),
            pltpu.SemaphoreType.DMA((2,)),
        ],
        cost_estimate=pl.CostEstimate(flops=0, bytes_accessed=1 << 20, transcendentals=0),
    )(bricks, innovations, innovations, courant, courant, diffusivity, diffusivity, left)


def sweep(inputs, sea, before, after, place):
    levels, lon_cells, lat_cells = inputs[2].shape
    steps = inputs[0].shape[0] - 1
    table, _ = halo_table(steps)
    f32, bf16 = jnp.float32, jnp.bfloat16
    extended = (levels + 2 * steps, lat_cells)
    row_of = jax.ShapeDtypeStruct(extended, f32)
    sent_row = jax.ShapeDtypeStruct(extended, bf16)
    cells = jax.ShapeDtypeStruct((levels + 2 * steps, lon_cells, lat_cells), f32)
    sea_ext, east_gain, west_gain, to_east, to_west = pl.pallas_call(
        functools.partial(first_kernel, table),
        in_specs=[VMEM] * 6,
        out_shape=[row_of] * 3 + [sent_row] * 2,
        out_specs=[VMEM] * 5,
        scratch_shapes=[pltpu.VMEM(extended, f32)] * 2,
        compiler_params=pltpu.CompilerParams(vmem_limit_bytes=GRANT),
        cost_estimate=pl.CostEstimate(flops=0, bytes_accessed=1 << 20, transcendentals=0),
    )(*inputs, sea, before, after)
    lam = ()
    low = high = sea_ext
    for step in range(1, steps + 1):
        west = shifted(to_east, "lon", 1)
        east = shifted(to_west, "lon", -1)
        state = (low, high) + lam
        out, out_low, out_high = pl.pallas_call(
            functools.partial(step_kernel, table, step),
            in_specs=[VMEM] * (6 + len(state)),
            out_shape=[cells, row_of, row_of],
            out_specs=[VMEM] * 3,
            compiler_params=pltpu.CompilerParams(vmem_limit_bytes=GRANT),
            cost_estimate=pl.CostEstimate(flops=40 * levels * lon_cells * lat_cells, bytes_accessed=9 << 20, transcendentals=0),
        )(*inputs, sea_ext, before, after, *state)
        if step == steps:
            break
        low, high, to_west, to_east = pl.pallas_call(
            face_kernel,
            in_specs=[VMEM] * 7,
            out_shape=[row_of] * 2 + [sent_row] * 2,
            out_specs=[VMEM] * 4,
            compiler_params=pltpu.CompilerParams(vmem_limit_bytes=GRANT),
            cost_estimate=pl.CostEstimate(flops=0, bytes_accessed=1 << 19, transcendentals=0),
        )(sea_ext, out_low, out_high, west, east, west_gain, east_gain)
        lam = (out,)
    half = (levels, lon_cells * lat_cells // 2)
    mine, other = call(
        lay_kernel,
        (place, out),
        [SMEM, VMEM],
        [(half, bf16)] * 2,
        scratch=[pltpu.VMEM((levels * lon_cells, LANES), f32)] * (lat_cells // LANES),
        moved=3 << 20,
    )
    edge = (sea_ext, out_low, out_high, west, east)
    mine, other, low, high = call(
        fix_kernel,
        (place, *edge, mine, other),
        [SMEM] + [VMEM] * 7,
        [(half, bf16)] * 2 + [(extended, f32)] * 2,
        aliases={6: 0, 7: 1},
    )
    (lam,) = call(
        emit_kernel,
        (out, low, high),
        [VMEM] * 3,
        [((levels, lon_cells, lat_cells), f32)],
        moved=3 << 20,
    )
    return lam, mine, other


def against(a, b):
    return lax.dot_general(a, b, (((1,), (1,)), ((), ())), preferred_element_type=jnp.float32)


def rows_kernel(wide, place, left, left_pair, first, second, kept, sent):
    half = left_pair.shape[1]
    levels = first.shape[0]
    sums = [None, None]
    for at in range(0, half, wide):
        lanes = slice(at, at + wide)
        mine = left[:, pl.ds(pl.multiple_of(place[1] * half + at, LANES), wide)]
        both = jnp.concatenate([first[:, lanes], second[:, lanes]], 0)
        for c, factor in enumerate((mine, left_pair[:, lanes])):
            term = against(factor, both)
            sums[c] = term if at == 0 else sums[c] + term
    for c in range(2):
        kept[c] = sums[c]
        other_order = [sums[c][:, levels:], sums[c][:, :levels]]
        sent[1 - c] = jnp.concatenate(other_order, 1).astype(jnp.bfloat16)


def mask_kernel(slots, place, ranks, *rest):
    stages = [rest[n : n + 2] for n in range(0, STAGES * 2, 2)]
    out = rest[STAGES * 2 :]
    rows = stages[0][0].shape[1] // slots
    for c in range(2):
        owner = place[0] if c == 0 else place[0] + 1 - 2 * place[1]
        for k in range(slots):
            at = slice(k * rows, (k + 1) * rows)
            value = jnp.concatenate(
                [kept[c, at, :] + arrived[c, at, :].astype(jnp.float32) for kept, arrived in stages], 1
            )
            row = lax.broadcasted_iota(jnp.int32, value.shape, 0) + owner * rows
            value = jnp.where(row < ranks[0, k], value, 0.0).astype(jnp.bfloat16)
            if len(out) > 1:
                out[k][c] = value
            else:
                count = out[0].shape[0]
                out[0][lax.rem(place[2] + (k - slots // 2 + count), count), c] = value


def columns_kernel(slots, stage, start, place, right, *rest):
    pieces = PARTS // HALVES
    right_pair, received, out = rest[:pieces], rest[pieces:-2], rest[-2:]
    count = received[0].shape[0]
    levels = out[0].shape[0]
    wide = right_pair[0].shape[1]
    half = wide * PARTS
    picked = slice(stage * levels, (stage + 2) * levels)
    coeffs = []
    for c in range(2):
        for k in range(slots):
            if len(received) > 1:
                coeffs.append(received[k][c, :, picked])
            else:
                source = lax.rem(place[2] + (count + slots // 2 - k), count)
                coeffs.append(received[0][source, c, :, picked])
    stacked = jnp.concatenate(coeffs, 0)
    rows = right.shape[0]
    lead = (((0,), (0,)), ((), ()))
    for n, piece in enumerate(right_pair):
        lanes = slice(n * wide, (n + 1) * wide)
        mine = right[:, pl.ds(pl.multiple_of(place[1] * half + start + n * wide, LANES), wide)]
        total = lax.dot_general(stacked[:rows], mine, lead, preferred_element_type=jnp.float32)
        total = total + lax.dot_general(stacked[rows:], piece[...], lead, preferred_element_type=jnp.float32)
        out[0][:, lanes] = total[:levels].astype(out[0].dtype)
        out[1][:, lanes] = total[levels:].astype(out[1].dtype)


def join_kernel(flip, place, *rest):
    ones, twos = rest[:HALVES], rest[HALVES : 2 * HALVES]
    out, slab, sem, *rows = rest[-(3 + LANE_TILES) :]
    levels, half, lat_cells = slab.shape
    f32 = jnp.float32
    each = half // HALVES
    for x in range(half):
        for c, lanes in enumerate(rows):
            at = (x % each) * lat_cells + c * LANES
            cols = slice(at, at + LANES)
            value = ones[x // each][:, cols].astype(f32) + twos[x // each][:, cols].astype(f32)
            lanes[pl.ds(x, levels, stride=half), :] = value
    side = 1 - place[1] if flip else place[1]
    start = pl.multiple_of(side * half, half)
    parts = 4
    size = levels // parts
    copies = []
    for part in range(parts):
        for z in range(part * size, (part + 1) * size):
            for c, lanes in enumerate(rows):
                slab[z, :, c * LANES : (c + 1) * LANES] = lanes[z * half : (z + 1) * half, :]
        here = pl.ds(part * size, size)
        target = out.at[here, pl.ds(start, half)]
        copies.append(pltpu.make_async_copy(slab.at[here], target, sem.at[part]))
        copies[-1].start()
    for copy in copies:
        copy.wait()


def call(kernel, operands, in_specs, outs, grant=GRANT, flops=0, moved=1 << 20, scratch=(), aliases=None):
    return pl.pallas_call(
        kernel,
        in_specs=in_specs,
        out_shape=[jax.ShapeDtypeStruct(*o[:2]) for o in outs],
        out_specs=[o[2] if len(o) > 2 else VMEM for o in outs],
        scratch_shapes=list(scratch),
        input_output_aliases=aliases or {},
        compiler_params=pltpu.CompilerParams(vmem_limit_bytes=grant),
        cost_estimate=pl.CostEstimate(flops=flops, bytes_accessed=moved, transcendentals=0),
    )(*operands)


def per_device(
    innovations, courant, diffusivity, sea_bricks, tile_ranks, row_factors, column_factors
):
    levels, lon_cells, lat_cells = diffusivity.shape
    tile_cols = lon_cells * lat_cells
    half = tile_cols // 2
    slots = tile_ranks.shape[1]
    count = lax.axis_size("depth")
    lon_count = lax.axis_size("lon")
    f32, bf16 = jnp.float32, jnp.bfloat16
    left = row_factors.transpose(0, 1, 3, 2)
    right = column_factors.transpose(0, 1, 3, 2)
    width = left.shape[2]
    rows = slots * width

    down, up, sea, place, left_other = pack(innovations, courant, diffusivity, sea_bricks, left)
    before = from_behind(down, "depth", 1)
    after = from_behind(up, "depth", -1)
    inputs = (innovations, courant, diffusivity)
    inputs = call(
        load_kernel,
        inputs,
        [ANY] * 3,
        [(a.shape, a.dtype) for a in inputs],
        grant=LOAD_GRANT,
        moved=18 << 20,
        scratch=[pltpu.SemaphoreType.DMA((3,))],
    )
    right_other = call(
        halves_kernel,
        (place, right),
        [SMEM, ANY],
        [((slots, width, half // PARTS), bf16, ANY)] * PARTS,
        moved=4 << 20,
        scratch=[pltpu.VMEM((PARTS, slots, width, half // PARTS), bf16), pltpu.SemaphoreType.DMA((2 * PARTS,))],
    )
    left_pair = swapped(left_other, "depth", 1)
    right_pair = []
    for part in range(PARTS):
        right_pair.append(swapped(right_other[part], "depth", 1).reshape(rows, half // PARTS))
    lam, lam_mine, lam_other = sweep(inputs, sea, before, after, place)
    left_pair = left_pair.reshape(rows, half)
    left, right = left.reshape(rows, tile_cols), right.reshape(rows, tile_cols)
    blocks = {0: lam_mine}
    for mask in range(count - 1, 0, -1):
        blocks[mask] = swapped(lam_other if mask % 2 else lam_mine, "depth", mask)
    sums = []
    for stage in range(0, count, 2):
        pair = (2, rows, 2 * levels)
        kept, sent = call(
            functools.partial(rows_kernel, 4 * LANES),
            (place, left, left_pair, blocks[stage], blocks[stage + 1]),
            [SMEM] + [VMEM] * 4,
            [(pair, f32), (pair, bf16)],
            flops=8 * rows * half * levels,
            moved=3 << 20,
        )
        sums += [kept, swapped(sent, "depth", 1)]
    grouped = lon_count == slots
    slot = (2, width, count * levels)
    coeff = call(
        functools.partial(mask_kernel, slots),
        (place, tile_ranks, *sums),
        [SMEM, SMEM] + [VMEM] * len(sums),
        [((lon_count,) + slot, bf16)] if grouped else [(slot, bf16)] * slots,
    )
    if grouped:
        received = [lax.all_to_all(coeff[0], "lon", 0, 0, tiled=True)]
    else:
        received = [shifted(coeff[k], "lon", k - slots // 2) for k in range(slots)]
    arrived = {mask: [] for mask in range(count)}
    block = (levels, half // HALVES)
    pieces = PARTS // HALVES
    for part in range(HALVES):
        for stage in range(count - 2, -1, -2):
            first, second = call(
                functools.partial(columns_kernel, slots, stage, part * (half // HALVES)),
                (place, right, *right_pair[part * pieces : (part + 1) * pieces], *received),
                [SMEM] + [VMEM] * (1 + pieces + len(received)),
                [(block, bf16 if stage else f32), (block, bf16)],
                flops=8 * rows * half * levels // HALVES,
                moved=2 << 20,
            )
            arrived[stage + 1].append(swapped(second, "depth", stage + 1))
            if stage:
                first = swapped(first, "depth", stage)
            arrived[stage].append(first)
    scratch = [
        pltpu.VMEM((levels, lon_cells // 2, lat_cells), f32),
        pltpu.SemaphoreType.DMA((4,)),
    ] + [pltpu.VMEM((levels * lon_cells // 2, LANES), f32)] * LANE_TILES
    whole = [((levels, lon_cells, lat_cells), f32, ANY)]
    (gradient,) = call(
        functools.partial(join_kernel, True),
        (place, *arrived[1], *arrived[3]),
        [SMEM] + [VMEM] * (2 * HALVES),
        whole,
        scratch=scratch,
        moved=2 << 20,
    )
    (gradient,) = call(
        functools.partial(join_kernel, False),
        (place, *arrived[0], *arrived[2], gradient),
        [SMEM] + [VMEM] * (2 * HALVES) + [ANY],
        whole,
        scratch=scratch,
        moved=2 << 20,
        aliases={1 + 2 * HALVES: 0},
    )
    return (lam, gradient)


def solution(mesh):
    placed = (
        P(None, "depth", "lon", None),
        P(None, "depth", "lon", None),
        P("depth", "lon", None),
        P("depth", "lon", None),
        P("lon", None),
        P("lon", None, None, "depth"),
        P("lon", None, None, "depth"),
    )
    return jax.shard_map(
        per_device,
        mesh=mesh,
        in_specs=placed,
        out_specs=(P("depth", "lon", None), P("depth", "lon", None)),
        check_vma=False,
    )
```

```python
import functools
import jax
import jax.numpy as jnp
from jax import lax
from jax.experimental import pallas as pl
from jax.experimental.pallas import tpu as pltpu
from jax.sharding import PartitionSpec as P

UNROLL = 9
LANES = 128
PARTS = 4
LOAD_GRANT = 40 << 20
WIDE_GRANT = 60 << 20
LANE_TILES = 2
HALVES = 2
GRANT = 4 << 20
VMEM = pl.BlockSpec(memory_space=pltpu.VMEM)
SMEM = pl.BlockSpec(memory_space=pltpu.SMEM)
ANY = pl.BlockSpec(memory_space=pl.ANY)


def from_behind(value, axis, steps):
    count = lax.axis_size(axis)
    initial, last = (max(0, -steps), min(count, count - steps))
    return lax.ppermute(value, axis, [(source, source + steps) for source in range(initial, last)])


def shifted(block, axis, distance):
    devices = range(lax.axis_size(axis))
    if distance % len(devices) == 0:
        return block
    route = [((i - distance) % len(devices), i) for i in devices]
    return lax.ppermute(block, axis, route)


def swapped(block, axis, mask):
    return lax.ppermute(block, axis, [(i, i ^ mask) for i in range(lax.axis_size(axis))])


def halo_table(depth):
    order, at = {}, 0
    for name, extent in (
        [(("innov", k), min(k, depth - 1)) for k in range(depth, 0, -1)]
        + [("diff", depth - 1), ("c0", depth - 1), ("c1", depth - 1), ("c2", depth - 1)]
    ):
        for distance in range(1, extent + 1):
            order[name, distance] = at
            at += 1
    order["sea"], order["flux"] = at, at + 1
    return order, at + 2


def row(ref, at):
    return ref[pl.ds(at, 1), :]


def pack_kernel(table, axes, bricks, innov_lo, innov_hi, cour_lo, cour_hi, diff_lo, diff_hi, down, up, sea, place, rows):
    me = lax.axis_index(axes[1])
    place[0], place[1], place[2] = me, lax.rem(me, 2), lax.axis_index(axes[0])
    depth = diff_lo.shape[0]
    levels, _, count = bricks.shape
    lat_cells = sea.shape[1]
    for z in range(levels):
        rows[z : z + 1] = bricks[z].astype(jnp.float32)
    brick_at = lax.broadcasted_iota(jnp.int32, (count, lat_cells), 0)
    cell_at = lax.broadcasted_iota(jnp.int32, (count, lat_cells), 1)
    inside = (brick_at == cell_at // (lat_cells // count)).astype(jnp.bfloat16)
    wide = jnp.dot(rows[...].astype(jnp.bfloat16), inside, preferred_element_type=jnp.float32)
    sea[...] = wide
    sea_lo, sea_hi = wide[:depth], wide[levels - depth :]

    def fill(out, innov, cour, diff, sea, level, sign):
        for key, at in table.items():
            if key == "sea":
                rows = [sea[level(d) : level(d) + 1] for d in range(1, depth + 1)]
                rows.append(jnp.zeros((out.shape[1] - depth, out.shape[2]), jnp.float32))
                value = jnp.concatenate(rows, 0)
            elif key == "flux":
                z = level(depth)
                gain = diff[z] + (0.5 * sign) * cour[0, z]
                value = gain * (sea[z : z + 1] * innov[innov.shape[0] - 1, z])
            else:
                name, distance = key
                z = level(distance)
                if name == "diff":
                    value = diff[z]
                elif name == "c0":
                    value = cour[0, z]
                elif name == "c1":
                    value = cour[1, z]
                elif name == "c2":
                    value = cour[2, z]
                else:
                    value = innov[name[1], z]
            out[at] = value.astype(jnp.bfloat16)

    fill(down, innov_hi, cour_hi, diff_hi, sea_hi, lambda d: depth - d, -1.0)
    fill(up, innov_lo, cour_lo, diff_lo, sea_lo, lambda d: d - 1, 1.0)


def load_kernel(*refs):
    count = len(refs) // 2
    copies = [pltpu.make_async_copy(refs[n], refs[count + n], refs[-1].at[n]) for n in range(count)]
    for copy in copies:
        copy.start()
    for copy in copies:
        copy.wait()


def halves_kernel(place, right, *rest):
    targets, (vmem, sems) = rest[:-2], rest[-2:]
    wide = targets[0].shape[2]
    start = (1 - place[1]) * wide * len(targets)
    loads, stores = [], []
    for n, target in enumerate(targets):
        window = pl.ds(pl.multiple_of(start + n * wide, wide), wide)
        loads.append(pltpu.make_async_copy(right.at[0, :, :, window], vmem.at[n], sems.at[n]))
        loads[-1].start()
        stores.append(pltpu.make_async_copy(vmem.at[n], target, sems.at[len(targets) + n]))
    for load, store in zip(loads, stores):
        load.wait()
        store.start()
    for store in stores:
        store.wait()


def first_kernel(table, innov, cour, diff, sea, before, after, sea_ext, east_gain, west_gain, to_east, to_west, east_rows, west_rows):
    steps = innov.shape[0] - 1
    levels, lon_cells, lat_cells = diff.shape
    last = lon_cells - 1

    def put(at, sea_row, diff_a, diff_b, cour_a, cour_b, innov_a, innov_b):
        here = pl.ds(at, 1)
        sea_ext[here, :] = sea_row
        low_row, high_row = sea_row * innov_a, sea_row * innov_b
        west = diff_a + 0.5 * cour_a
        east = diff_b - 0.5 * cour_b
        west_gain[here, :], east_gain[here, :] = west, east
        west_rows[here, :], east_rows[here, :] = west * low_row, east * high_row

    for halo, where in ((before, lambda d: steps - d), (after, lambda d: steps + levels + d - 1)):
        sea_rows = halo[table["sea"]].astype(jnp.float32)
        for d in range(1, steps + 1):
            sea_row = sea_rows[d - 1 : d]
            at = where(d)
            if d == steps:
                zero = jnp.zeros((1, lat_cells), jnp.float32)
                for ref in (sea_ext, west_gain, east_gain, west_rows, east_rows):
                    ref[pl.ds(at, 1), :] = zero
            else:
                dd = halo[table["diff", d]].astype(jnp.float32)
                cc = halo[table["c1", d]].astype(jnp.float32)
                ii = halo[table[("innov", steps), d]].astype(jnp.float32)
                put(at, sea_row, dd[:1], dd[last:], cc[:1], cc[last:], ii[:1], ii[last:])

    def one(z, carry):
        edge = lambda ref: (ref[z, :1], ref[z, last:])
        put(z + steps, row(sea, z), *edge(diff), *edge(cour.at[1]), *edge(innov.at[steps]))
        return carry

    lax.fori_loop(0, levels, one, 0, unroll=4)
    to_west[...] = west_rows[...].astype(jnp.bfloat16)
    to_east[...] = east_rows[...].astype(jnp.bfloat16)


def step_kernel(table, step, innov, cour, diff, sea_ext, before, after, low, high, *rest):
    steps = innov.shape[0] - 1
    levels, lon_cells, lat_cells = diff.shape
    if step > 1:
        lam, rest = rest[0], rest[1:]
    out, out_low, out_high = rest
    last = lon_cells - 1
    x_at = lax.broadcasted_iota(jnp.int32, (lon_cells, lat_cells), 0)
    y_at = lax.broadcasted_iota(jnp.int32, (lon_cells, lat_cells), 1)
    first_x, last_x = x_at == 0, x_at == last
    first_y, last_y = y_at == 0, y_at == lat_cells - 1
    reach = steps - step

    def halo_level(halo, d, name):
        return halo[table[name, d]].astype(jnp.float32)

    def state(at, innovation):
        if step == 1:
            return row(sea_ext, at) * innovation
        value = jnp.where(first_x, row(low, at), lam[at])
        return jnp.where(last_x, row(high, at), value)

    def finish(at, acc, up_flux):
        value = row(sea_ext, at) * (acc + up_flux)
        out[at] = value
        out_low[pl.ds(at, 1), :] = value[:1]
        out_high[pl.ds(at, 1), :] = value[last:]

    def depth_terms(a, d, c):
        spread, drift = d * a, c * (0.5 * a)
        return spread - drift, spread + drift

    def level(a, d, c0, c1, c2, innovation):
        half = 0.5 * a
        spread = d * a
        drift = c0 * half
        plus0, minus0 = spread - drift, spread + drift
        drift = c1 * half
        plus1, minus1 = spread - drift, spread + drift
        drift = c2 * half
        plus2, minus2 = spread - drift, spread + drift
        acc = a - 6.0 * spread + innovation
        acc = acc + jnp.where(first_x, 0.0, pltpu.roll(plus1, 1, 0))
        acc = acc + jnp.where(last_x, 0.0, pltpu.roll(minus1, lon_cells - 1, 0))
        acc = acc + jnp.where(first_y, 0.0, pltpu.roll(plus2, 1, 1))
        acc = acc + jnp.where(last_y, 0.0, pltpu.roll(minus2, lat_cells - 1, 1))
        return acc, plus0, minus0

    def halo_start(halo, d, at):
        return state(at, halo_level(halo, d, ("innov", steps)) if step == 1 else None)

    def halo_full(halo, d, at):
        a = halo_start(halo, d, at)
        return level(
            a,
            halo_level(halo, d, "diff"),
            halo_level(halo, d, "c0"),
            halo_level(halo, d, "c1"),
            halo_level(halo, d, "c2"),
            halo_level(halo, d, ("innov", steps - step)),
        )

    def halo_edge(halo, d, at):
        if step == 1:
            flux = halo[table["flux"]].astype(jnp.float32)
            return flux, flux
        a = halo_start(halo, d, at)
        return depth_terms(a, halo_level(halo, d, "diff"), halo_level(halo, d, "c0"))

    down_flux, _ = halo_edge(before, reach + 1, steps - reach - 1)
    acc = None
    for d in range(reach, 0, -1):
        at = steps - d
        value, plus0, minus0 = halo_full(before, d, at)
        if acc is not None:
            finish(at - 1, acc, minus0)
        acc, down_flux = value + down_flux, plus0

    def own(z):
        a = state(z + steps, innov[steps, z] if step == 1 else None)
        return level(a, diff[z], cour[0, z], cour[1, z], cour[2, z], innov[steps - step, z])

    value, plus0, minus0 = own(0)
    if acc is not None:
        finish(steps - 1, acc, minus0)
    carry = (value + down_flux, plus0)

    def one(z, carry):
        acc, down_flux = carry
        value, plus0, minus0 = own(z)
        finish(z + steps - 1, acc, minus0)
        return value + down_flux, plus0

    head = (levels - 1) % UNROLL
    for z in range(1, 1 + head):
        carry = one(z, carry)

    def several(i, carry):
        for u in range(UNROLL):
            carry = one(1 + head + i * UNROLL + u, carry)
        return carry

    acc, down_flux = lax.fori_loop(0, (levels - 1) // UNROLL, several, carry)
    at = steps + levels - 1
    for d in range(1, reach + 1):
        value, plus0, minus0 = halo_full(after, d, at + d)
        finish(at + d - 1, acc, minus0)
        acc, down_flux = value + down_flux, plus0
    _, up_flux = halo_edge(after, reach + 1, at + reach + 1)
    finish(at + reach, acc, up_flux)


def lay_kernel(place, lam, mine, other, *rows):
    levels = mine.shape[0]
    total, lon_cells, lat_cells = lam.shape
    steps = (total - levels) // 2

    def one(z, carry):
        value = lam[z + steps]
        for c, lanes in enumerate(rows):
            at = pl.multiple_of(z * lon_cells, lon_cells)
            lanes[pl.ds(at, lon_cells), :] = value[:, c * LANES : (c + 1) * LANES]
        return carry

    lax.fori_loop(0, levels, one, 0, unroll=4)
    half = lon_cells // 2
    for part, start in ((mine, place[1] * half), (other, (1 - place[1]) * half)):
        for x in range(half):
            for c, lanes in enumerate(rows):
                picked = lanes[pl.ds(start + x, levels, stride=lon_cells), :]
                at = x * lat_cells + c * LANES
                part[:, at : at + LANES] = picked.astype(jnp.bfloat16)


def fix_kernel(place, sea_ext, out_low, out_high, west, east, mine_in, other_in, mine, other, low, high):
    levels, half = mine.shape
    lat_cells = low.shape[1]
    steps = (sea_ext.shape[0] - levels) // 2
    low[...] = out_low[...] + sea_ext[...] * west[...].astype(jnp.float32)
    high[...] = out_high[...] + sea_ext[...] * east[...].astype(jnp.float32)
    low_rows = low[steps : steps + levels, :].astype(jnp.bfloat16)
    high_rows = high[steps : steps + levels, :].astype(jnp.bfloat16)

    @pl.when(place[1] == 0)
    def _():
        mine[:, :lat_cells] = low_rows
        other[:, half - lat_cells :] = high_rows

    @pl.when(place[1] != 0)
    def _():
        other[:, :lat_cells] = low_rows
        mine[:, half - lat_cells :] = high_rows


def emit_kernel(lam, low, high, out):
    levels, lon_cells, lat_cells = out.shape
    steps = (lam.shape[0] - levels) // 2
    x_at = lax.broadcasted_iota(jnp.int32, (lon_cells, lat_cells), 0)
    first_x, last_x = x_at == 0, x_at == lon_cells - 1

    def one(z, carry):
        at = z + steps
        out[z] = jnp.where(last_x, row(high, at), jnp.where(first_x, row(low, at), lam[at]))
        return carry

    lax.fori_loop(0, levels, one, 0, unroll=4)


def face_kernel(sea_ext, out_low, out_high, west, east, west_gain, east_gain, low, high, to_west, to_east):
    low_rows = out_low[...] + sea_ext[...] * west[...].astype(jnp.float32)
    high_rows = out_high[...] + sea_ext[...] * east[...].astype(jnp.float32)
    low[...], high[...] = low_rows, high_rows
    to_west[...] = (west_gain[...] * low_rows).astype(jnp.bfloat16)
    to_east[...] = (east_gain[...] * high_rows).astype(jnp.bfloat16)


def pack(innovations, courant, diffusivity, bricks):
    levels, lon_cells, lat_cells = diffusivity.shape
    steps = innovations.shape[0] - 1
    table, layers = halo_table(steps)
    f32, bf16 = jnp.float32, jnp.bfloat16
    end = levels // steps - 1

    def edges(shape, axis):
        block = list(shape)
        block[axis] = steps
        at = lambda index: lambda i: tuple(index if a == axis else 0 for a in range(len(shape)))
        return [pl.BlockSpec(tuple(block), at(index)) for index in (0, end)]

    message = jax.ShapeDtypeStruct((layers, lon_cells, lat_cells), bf16)
    return pl.pallas_call(
        functools.partial(pack_kernel, table, ("lon", "depth")),
        grid=(1,),
        in_specs=[VMEM]
        + edges(innovations.shape, 1)
        + edges(courant.shape, 1)
        + edges(diffusivity.shape, 0),
        out_shape=[
            message,
            message,
            jax.ShapeDtypeStruct((levels, lat_cells), f32),
            jax.ShapeDtypeStruct((3,), jnp.int32),
        ],
        out_specs=[VMEM, VMEM, VMEM, SMEM],
        scratch_shapes=[
            pltpu.VMEM((levels, bricks.shape[2]), f32),
        ],
        cost_estimate=pl.CostEstimate(flops=0, bytes_accessed=1 << 20, transcendentals=0),
    )(bricks, innovations, innovations, courant, courant, diffusivity, diffusivity)


def sweep(inputs, sea, before, after, place):
    levels, lon_cells, lat_cells = inputs[2].shape
    steps = inputs[0].shape[0] - 1
    table, _ = halo_table(steps)
    f32, bf16 = jnp.float32, jnp.bfloat16
    extended = (levels + 2 * steps, lat_cells)
    row_of = jax.ShapeDtypeStruct(extended, f32)
    sent_row = jax.ShapeDtypeStruct(extended, bf16)
    cells = jax.ShapeDtypeStruct((levels + 2 * steps, lon_cells, lat_cells), f32)
    sea_ext, east_gain, west_gain, to_east, to_west = pl.pallas_call(
        functools.partial(first_kernel, table),
        in_specs=[VMEM] * 6,
        out_shape=[row_of] * 3 + [sent_row] * 2,
        out_specs=[VMEM] * 5,
        scratch_shapes=[pltpu.VMEM(extended, f32)] * 2,
        compiler_params=pltpu.CompilerParams(vmem_limit_bytes=GRANT),
        cost_estimate=pl.CostEstimate(flops=0, bytes_accessed=1 << 20, transcendentals=0),
    )(*inputs, sea, before, after)
    lam = ()
    low = high = sea_ext
    for step in range(1, steps + 1):
        west = shifted(to_east, "lon", 1)
        east = shifted(to_west, "lon", -1)
        state = (low, high) + lam
        out, out_low, out_high = pl.pallas_call(
            functools.partial(step_kernel, table, step),
            in_specs=[VMEM] * (6 + len(state)),
            out_shape=[cells, row_of, row_of],
            out_specs=[VMEM] * 3,
            compiler_params=pltpu.CompilerParams(vmem_limit_bytes=GRANT),
            cost_estimate=pl.CostEstimate(flops=40 * levels * lon_cells * lat_cells, bytes_accessed=9 << 20, transcendentals=0),
        )(*inputs, sea_ext, before, after, *state)
        if step == steps:
            break
        low, high, to_west, to_east = pl.pallas_call(
            face_kernel,
            in_specs=[VMEM] * 7,
            out_shape=[row_of] * 2 + [sent_row] * 2,
            out_specs=[VMEM] * 4,
            compiler_params=pltpu.CompilerParams(vmem_limit_bytes=GRANT),
            cost_estimate=pl.CostEstimate(flops=0, bytes_accessed=1 << 19, transcendentals=0),
        )(sea_ext, out_low, out_high, west, east, west_gain, east_gain)
        lam = (out,)
    half = (levels, lon_cells * lat_cells // 2)
    mine, other = call(
        lay_kernel,
        (place, out),
        [SMEM, VMEM],
        [(half, bf16)] * 2,
        scratch=[pltpu.VMEM((levels * lon_cells, LANES), f32)] * (lat_cells // LANES),
        moved=3 << 20,
    )
    edge = (sea_ext, out_low, out_high, west, east)
    mine, other, low, high = call(
        fix_kernel,
        (place, *edge, mine, other),
        [SMEM] + [VMEM] * 7,
        [(half, bf16)] * 2 + [(extended, f32)] * 2,
        aliases={6: 0, 7: 1},
    )
    (lam,) = call(
        emit_kernel,
        (out, low, high),
        [VMEM] * 3,
        [((levels, lon_cells, lat_cells), f32)],
        moved=3 << 20,
    )
    return lam, mine, other


def against(a, b):
    return lax.dot_general(a, b, (((1,), (1,)), ((), ())), preferred_element_type=jnp.float32)


def rows_kernel(wide, place, left, left_pair, first, second, kept, sent):
    half = left_pair.shape[1]
    levels = first.shape[0]
    sums = [None, None]
    for at in range(0, half, wide):
        lanes = slice(at, at + wide)
        mine = left[:, pl.ds(pl.multiple_of(place[1] * half + at, LANES), wide)]
        both = jnp.concatenate([first[:, lanes], second[:, lanes]], 0)
        for c, factor in enumerate((mine, left_pair[:, lanes])):
            term = against(factor, both)
            sums[c] = term if at == 0 else sums[c] + term
    for c in range(2):
        kept[c] = sums[c]
        other_order = [sums[c][:, levels:], sums[c][:, :levels]]
        sent[1 - c] = jnp.concatenate(other_order, 1).astype(jnp.bfloat16)


def mask_kernel(slots, place, ranks, kept, arrived, *out):
    rows = kept.shape[1] // slots
    for c in range(2):
        owner = place[0] if c == 0 else place[0] + 1 - 2 * place[1]
        for k in range(slots):
            at = slice(k * rows, (k + 1) * rows)
            value = kept[c, at, :] + arrived[c, at, :].astype(jnp.float32)
            row_at = lax.broadcasted_iota(jnp.int32, value.shape, 0) + owner * rows
            value = jnp.where(row_at < ranks[0, k], value, 0.0).astype(jnp.bfloat16)
            if len(out) > 1:
                out[k][c] = value
            else:
                count = out[0].shape[0]
                out[0][lax.rem(place[2] + (k - slots // 2 + count), count), c] = value


def columns_kernel(slots, start, place, right, *rest):
    pieces = PARTS // HALVES
    right_pair, received, out = rest[:pieces], rest[pieces:-2], rest[-2:]
    count = received[0].shape[0]
    levels = out[0].shape[0]
    wide = right_pair[0].shape[1]
    half = wide * PARTS
    coeffs = []
    for c in range(2):
        for k in range(slots):
            if len(received) > 1:
                coeffs.append(received[k][c])
            else:
                source = lax.rem(place[2] + (count + slots // 2 - k), count)
                coeffs.append(received[0][source, c])
    stacked = jnp.concatenate(coeffs, 0)
    rows = right.shape[0]
    lead = (((0,), (0,)), ((), ()))
    for n, piece in enumerate(right_pair):
        lanes = slice(n * wide, (n + 1) * wide)
        mine = right[:, pl.ds(pl.multiple_of(place[1] * half + start + n * wide, LANES), wide)]
        total = lax.dot_general(stacked[:rows], mine, lead, preferred_element_type=jnp.float32)
        total = total + lax.dot_general(stacked[rows:], piece[...], lead, preferred_element_type=jnp.float32)
        out[0][:, lanes] = total[:levels].astype(out[0].dtype)
        out[1][:, lanes] = total[levels:].astype(out[1].dtype)


def join_kernel(flip, place, *rest):
    ones, twos = rest[:HALVES], rest[HALVES : 2 * HALVES]
    out, slab, sem, *rows = rest[-(3 + LANE_TILES) :]
    levels, half, lat_cells = slab.shape
    f32 = jnp.float32
    each = half // HALVES
    for x in range(half):
        for c, lanes in enumerate(rows):
            at = (x % each) * lat_cells + c * LANES
            cols = slice(at, at + LANES)
            value = ones[x // each][:, cols].astype(f32) + twos[x // each][:, cols].astype(f32)
            lanes[pl.ds(x, levels, stride=half), :] = value
    side = 1 - place[1] if flip else place[1]
    start = pl.multiple_of(side * half, half)
    parts = 4
    size = levels // parts
    copies = []
    for part in range(parts):
        for z in range(part * size, (part + 1) * size):
            for c, lanes in enumerate(rows):
                slab[z, :, c * LANES : (c + 1) * LANES] = lanes[z * half : (z + 1) * half, :]
        here = pl.ds(part * size, size)
        target = out.at[here, pl.ds(start, half)]
        copies.append(pltpu.make_async_copy(slab.at[here], target, sem.at[part]))
        copies[-1].start()
    for copy in copies:
        copy.wait()


def call(kernel, operands, in_specs, outs, grant=GRANT, flops=0, moved=1 << 20, scratch=(), aliases=None):
    return pl.pallas_call(
        kernel,
        in_specs=in_specs,
        out_shape=[jax.ShapeDtypeStruct(*o[:2]) for o in outs],
        out_specs=[o[2] if len(o) > 2 else VMEM for o in outs],
        scratch_shapes=list(scratch),
        input_output_aliases=aliases or {},
        compiler_params=pltpu.CompilerParams(vmem_limit_bytes=grant),
        cost_estimate=pl.CostEstimate(flops=flops, bytes_accessed=moved, transcendentals=0),
    )(*operands)


def per_device(
    innovations, courant, diffusivity, sea_bricks, tile_ranks, row_factors, column_factors
):
    levels, lon_cells, lat_cells = diffusivity.shape
    tile_cols = lon_cells * lat_cells
    half = tile_cols // 2
    slots = tile_ranks.shape[1]
    count = lax.axis_size("depth")
    lon_count = lax.axis_size("lon")
    f32, bf16 = jnp.float32, jnp.bfloat16
    left = row_factors.transpose(0, 1, 3, 2)
    right = column_factors.transpose(0, 1, 3, 2)
    width = left.shape[2]
    rows = slots * width

    down, up, sea, place = pack(innovations, courant, diffusivity, sea_bricks)
    (left_other,) = call(
        halves_kernel,
        (place, left),
        [SMEM, ANY],
        [((slots, width, half), bf16, ANY)],
        grant=WIDE_GRANT,
        moved=2 << 20,
        scratch=[pltpu.VMEM((1, slots, width, half), bf16), pltpu.SemaphoreType.DMA((2,))],
    )
    before = from_behind(down, "depth", 1)
    after = from_behind(up, "depth", -1)
    inputs = (innovations, courant, diffusivity)
    inputs = call(
        load_kernel,
        inputs,
        [ANY] * 3,
        [(a.shape, a.dtype) for a in inputs],
        grant=LOAD_GRANT,
        moved=18 << 20,
        scratch=[pltpu.SemaphoreType.DMA((3,))],
    )
    right_other = call(
        halves_kernel,
        (place, right),
        [SMEM, ANY],
        [((slots, width, half // PARTS), bf16, ANY)] * PARTS,
        moved=4 << 20,
        scratch=[pltpu.VMEM((PARTS, slots, width, half // PARTS), bf16), pltpu.SemaphoreType.DMA((2 * PARTS,))],
    )
    left_pair = swapped(left_other, "depth", 1)
    right_pair = []
    for part in range(PARTS):
        right_pair.append(swapped(right_other[part], "depth", 1).reshape(rows, half // PARTS))
    lam, lam_mine, lam_other = sweep(inputs, sea, before, after, place)
    left_pair = left_pair.reshape(rows, half)
    left, right = left.reshape(rows, tile_cols), right.reshape(rows, tile_cols)
    blocks = {0: lam_mine}
    for mask in range(count - 1, 0, -1):
        blocks[mask] = swapped(lam_other if mask % 2 else lam_mine, "depth", mask)
    sums = {}
    for stage in range(0, count, 2):
        pair = (2, rows, 2 * levels)
        kept, sent = call(
            functools.partial(rows_kernel, 4 * LANES),
            (place, left, left_pair, blocks[stage], blocks[stage + 1]),
            [SMEM] + [VMEM] * 4,
            [(pair, f32), (pair, bf16)],
            flops=8 * rows * half * levels,
            moved=3 << 20,
        )
        sums[stage] = (kept, swapped(sent, "depth", 1))
    grouped = lon_count == slots
    slot = (2, width, 2 * levels)
    arrived = {mask: [] for mask in range(count)}
    block = (levels, half // HALVES)
    pieces = PARTS // HALVES
    for stage in range(count - 2, -1, -2):
        coeff = call(
            functools.partial(mask_kernel, slots),
            (place, tile_ranks, *sums[stage]),
            [SMEM, SMEM, VMEM, VMEM],
            [((lon_count,) + slot, bf16)] if grouped else [(slot, bf16)] * slots,
        )
        if grouped:
            received = [lax.all_to_all(coeff[0], "lon", 0, 0, tiled=True)]
        else:
            received = [shifted(coeff[k], "lon", k - slots // 2) for k in range(slots)]
        for part in range(HALVES):
            first, second = call(
                functools.partial(columns_kernel, slots, part * (half // HALVES)),
                (place, right, *right_pair[part * pieces : (part + 1) * pieces], *received),
                [SMEM] + [VMEM] * (1 + pieces + len(received)),
                [(block, bf16 if stage else f32), (block, bf16)],
                flops=8 * rows * half * levels // HALVES,
                moved=2 << 20,
            )
            arrived[stage + 1].append(swapped(second, "depth", stage + 1))
            if stage:
                first = swapped(first, "depth", stage)
            arrived[stage].append(first)
    scratch = [
        pltpu.VMEM((levels, lon_cells // 2, lat_cells), f32),
        pltpu.SemaphoreType.DMA((4,)),
    ] + [pltpu.VMEM((levels * lon_cells // 2, LANES), f32)] * LANE_TILES
    whole = [((levels, lon_cells, lat_cells), f32, ANY)]
    (gradient,) = call(
        functools.partial(join_kernel, True),
        (place, *arrived[1], *arrived[3]),
        [SMEM] + [VMEM] * (2 * HALVES),
        whole,
        scratch=scratch,
        moved=2 << 20,
    )
    (gradient,) = call(
        functools.partial(join_kernel, False),
        (place, *arrived[0], *arrived[2], gradient),
        [SMEM] + [VMEM] * (2 * HALVES) + [ANY],
        whole,
        scratch=scratch,
        moved=2 << 20,
        aliases={1 + 2 * HALVES: 0},
    )
    return (lam, gradient)


def solution(mesh):
    placed = (
        P(None, "depth", "lon", None),
        P(None, "depth", "lon", None),
        P("depth", "lon", None),
        P("depth", "lon", None),
        P("lon", None),
        P("lon", None, None, "depth"),
        P("lon", None, None, "depth"),
    )
    return jax.shard_map(
        per_device,
        mesh=mesh,
        in_specs=placed,
        out_specs=(P("depth", "lon", None), P("depth", "lon", None)),
        check_vma=False,
    )
```

```python
import functools
import jax
import jax.numpy as jnp
from jax import lax
from jax.experimental import pallas as pl
from jax.experimental.pallas import tpu as pltpu
from jax.sharding import PartitionSpec as P

UNROLL = 9
LANES = 128
PARTS = 4
LOAD_GRANT = 40 << 20
WIDE_GRANT = 60 << 20
STAGES = 2
LANE_TILES = 2
HALVES = 2
GRANT = 4 << 20
VMEM = pl.BlockSpec(memory_space=pltpu.VMEM)
SMEM = pl.BlockSpec(memory_space=pltpu.SMEM)
ANY = pl.BlockSpec(memory_space=pl.ANY)


def from_behind(value, axis, steps):
    count = lax.axis_size(axis)
    initial, last = (max(0, -steps), min(count, count - steps))
    return lax.ppermute(value, axis, [(source, source + steps) for source in range(initial, last)])


def shifted(block, axis, distance):
    devices = range(lax.axis_size(axis))
    if distance % len(devices) == 0:
        return block
    route = [((i - distance) % len(devices), i) for i in devices]
    return lax.ppermute(block, axis, route)


def swapped(block, axis, mask):
    return lax.ppermute(block, axis, [(i, i ^ mask) for i in range(lax.axis_size(axis))])


def halo_table(depth):
    order, at = {}, 0
    for name, extent in (
        [(("innov", k), min(k, depth - 1)) for k in range(depth, 0, -1)]
        + [("diff", depth - 1), ("c0", depth - 1), ("c1", depth - 1), ("c2", depth - 1)]
    ):
        for distance in range(1, extent + 1):
            order[name, distance] = at
            at += 1
    order["sea"], order["flux"] = at, at + 1
    return order, at + 2


def row(ref, at):
    return ref[pl.ds(at, 1), :]


def pack_kernel(table, axes, bricks, innov_lo, innov_hi, cour_lo, cour_hi, diff_lo, diff_hi, down, up, sea, place, rows):
    me = lax.axis_index(axes[1])
    place[0], place[1], place[2] = me, lax.rem(me, 2), lax.axis_index(axes[0])
    depth = diff_lo.shape[0]
    levels, _, count = bricks.shape
    lat_cells = sea.shape[1]
    for z in range(levels):
        rows[z : z + 1] = bricks[z].astype(jnp.float32)
    brick_at = lax.broadcasted_iota(jnp.int32, (count, lat_cells), 0)
    cell_at = lax.broadcasted_iota(jnp.int32, (count, lat_cells), 1)
    inside = (brick_at == cell_at // (lat_cells // count)).astype(jnp.bfloat16)
    wide = jnp.dot(rows[...].astype(jnp.bfloat16), inside, preferred_element_type=jnp.float32)
    sea[...] = wide
    sea_lo, sea_hi = wide[:depth], wide[levels - depth :]

    def fill(out, innov, cour, diff, sea, level, sign):
        for key, at in table.items():
            if key == "sea":
                rows = [sea[level(d) : level(d) + 1] for d in range(1, depth + 1)]
                rows.append(jnp.zeros((out.shape[1] - depth, out.shape[2]), jnp.float32))
                value = jnp.concatenate(rows, 0)
            elif key == "flux":
                z = level(depth)
                gain = diff[z] + (0.5 * sign) * cour[0, z]
                value = gain * (sea[z : z + 1] * innov[innov.shape[0] - 1, z])
            else:
                name, distance = key
                z = level(distance)
                if name == "diff":
                    value = diff[z]
                elif name == "c0":
                    value = cour[0, z]
                elif name == "c1":
                    value = cour[1, z]
                elif name == "c2":
                    value = cour[2, z]
                else:
                    value = innov[name[1], z]
            out[at] = value.astype(jnp.bfloat16)

    fill(down, innov_hi, cour_hi, diff_hi, sea_hi, lambda d: depth - d, -1.0)
    fill(up, innov_lo, cour_lo, diff_lo, sea_lo, lambda d: d - 1, 1.0)


def load_kernel(*refs):
    count = len(refs) // 2
    copies = [pltpu.make_async_copy(refs[n], refs[count + n], refs[-1].at[n]) for n in range(count)]
    for copy in copies:
        copy.start()
    for copy in copies:
        copy.wait()


def halves_kernel(place, right, *rest):
    targets, (vmem, sems) = rest[:-2], rest[-2:]
    wide = targets[0].shape[2]
    start = (1 - place[1]) * wide * len(targets)
    loads, stores = [], []
    for n, target in enumerate(targets):
        window = pl.ds(pl.multiple_of(start + n * wide, wide), wide)
        loads.append(pltpu.make_async_copy(right.at[0, :, :, window], vmem.at[n], sems.at[n]))
        loads[-1].start()
        stores.append(pltpu.make_async_copy(vmem.at[n], target, sems.at[len(targets) + n]))
    for load, store in zip(loads, stores):
        load.wait()
        store.start()
    for store in stores:
        store.wait()


def first_kernel(table, innov, cour, diff, sea, before, after, sea_ext, east_gain, west_gain, to_east, to_west, east_rows, west_rows):
    steps = innov.shape[0] - 1
    levels, lon_cells, lat_cells = diff.shape
    last = lon_cells - 1

    def put(at, sea_row, diff_a, diff_b, cour_a, cour_b, innov_a, innov_b):
        here = pl.ds(at, 1)
        sea_ext[here, :] = sea_row
        low_row, high_row = sea_row * innov_a, sea_row * innov_b
        west = diff_a + 0.5 * cour_a
        east = diff_b - 0.5 * cour_b
        west_gain[here, :], east_gain[here, :] = west, east
        west_rows[here, :], east_rows[here, :] = west * low_row, east * high_row

    for halo, where in ((before, lambda d: steps - d), (after, lambda d: steps + levels + d - 1)):
        sea_rows = halo[table["sea"]].astype(jnp.float32)
        for d in range(1, steps + 1):
            sea_row = sea_rows[d - 1 : d]
            at = where(d)
            if d == steps:
                zero = jnp.zeros((1, lat_cells), jnp.float32)
                for ref in (sea_ext, west_gain, east_gain, west_rows, east_rows):
                    ref[pl.ds(at, 1), :] = zero
            else:
                dd = halo[table["diff", d]].astype(jnp.float32)
                cc = halo[table["c1", d]].astype(jnp.float32)
                ii = halo[table[("innov", steps), d]].astype(jnp.float32)
                put(at, sea_row, dd[:1], dd[last:], cc[:1], cc[last:], ii[:1], ii[last:])

    def one(z, carry):
        edge = lambda ref: (ref[z, :1], ref[z, last:])
        put(z + steps, row(sea, z), *edge(diff), *edge(cour.at[1]), *edge(innov.at[steps]))
        return carry

    lax.fori_loop(0, levels, one, 0, unroll=4)
    to_west[...] = west_rows[...].astype(jnp.bfloat16)
    to_east[...] = east_rows[...].astype(jnp.bfloat16)


def step_kernel(table, step, innov, cour, diff, sea_ext, before, after, low, high, *rest):
    steps = innov.shape[0] - 1
    levels, lon_cells, lat_cells = diff.shape
    if step > 1:
        lam, rest = rest[0], rest[1:]
    out, out_low, out_high = rest
    last = lon_cells - 1
    x_at = lax.broadcasted_iota(jnp.int32, (lon_cells, lat_cells), 0)
    y_at = lax.broadcasted_iota(jnp.int32, (lon_cells, lat_cells), 1)
    first_x, last_x = x_at == 0, x_at == last
    first_y, last_y = y_at == 0, y_at == lat_cells - 1
    reach = steps - step

    def halo_level(halo, d, name):
        return halo[table[name, d]].astype(jnp.float32)

    def state(at, innovation):
        if step == 1:
            return row(sea_ext, at) * innovation
        value = jnp.where(first_x, row(low, at), lam[at])
        return jnp.where(last_x, row(high, at), value)

    def finish(at, acc, up_flux):
        value = row(sea_ext, at) * (acc + up_flux)
        out[at] = value
        out_low[pl.ds(at, 1), :] = value[:1]
        out_high[pl.ds(at, 1), :] = value[last:]

    def depth_terms(a, d, c):
        spread, drift = d * a, c * (0.5 * a)
        return spread - drift, spread + drift

    def level(a, d, c0, c1, c2, innovation):
        half = 0.5 * a
        spread = d * a
        drift = c0 * half
        plus0, minus0 = spread - drift, spread + drift
        drift = c1 * half
        plus1, minus1 = spread - drift, spread + drift
        drift = c2 * half
        plus2, minus2 = spread - drift, spread + drift
        acc = a - 6.0 * spread + innovation
        acc = acc + jnp.where(first_x, 0.0, pltpu.roll(plus1, 1, 0))
        acc = acc + jnp.where(last_x, 0.0, pltpu.roll(minus1, lon_cells - 1, 0))
        acc = acc + jnp.where(first_y, 0.0, pltpu.roll(plus2, 1, 1))
        acc = acc + jnp.where(last_y, 0.0, pltpu.roll(minus2, lat_cells - 1, 1))
        return acc, plus0, minus0

    def halo_start(halo, d, at):
        return state(at, halo_level(halo, d, ("innov", steps)) if step == 1 else None)

    def halo_full(halo, d, at):
        a = halo_start(halo, d, at)
        return level(
            a,
            halo_level(halo, d, "diff"),
            halo_level(halo, d, "c0"),
            halo_level(halo, d, "c1"),
            halo_level(halo, d, "c2"),
            halo_level(halo, d, ("innov", steps - step)),
        )

    def halo_edge(halo, d, at):
        if step == 1:
            flux = halo[table["flux"]].astype(jnp.float32)
            return flux, flux
        a = halo_start(halo, d, at)
        return depth_terms(a, halo_level(halo, d, "diff"), halo_level(halo, d, "c0"))

    down_flux, _ = halo_edge(before, reach + 1, steps - reach - 1)
    acc = None
    for d in range(reach, 0, -1):
        at = steps - d
        value, plus0, minus0 = halo_full(before, d, at)
        if acc is not None:
            finish(at - 1, acc, minus0)
        acc, down_flux = value + down_flux, plus0

    def own(z):
        a = state(z + steps, innov[steps, z] if step == 1 else None)
        return level(a, diff[z], cour[0, z], cour[1, z], cour[2, z], innov[steps - step, z])

    value, plus0, minus0 = own(0)
    if acc is not None:
        finish(steps - 1, acc, minus0)
    carry = (value + down_flux, plus0)

    def one(z, carry):
        acc, down_flux = carry
        value, plus0, minus0 = own(z)
        finish(z + steps - 1, acc, minus0)
        return value + down_flux, plus0

    head = (levels - 1) % UNROLL
    for z in range(1, 1 + head):
        carry = one(z, carry)

    def several(i, carry):
        for u in range(UNROLL):
            carry = one(1 + head + i * UNROLL + u, carry)
        return carry

    acc, down_flux = lax.fori_loop(0, (levels - 1) // UNROLL, several, carry)
    at = steps + levels - 1
    for d in range(1, reach + 1):
        value, plus0, minus0 = halo_full(after, d, at + d)
        finish(at + d - 1, acc, minus0)
        acc, down_flux = value + down_flux, plus0
    _, up_flux = halo_edge(after, reach + 1, at + reach + 1)
    finish(at + reach, acc, up_flux)


def lay_kernel(place, lam, mine, other, *rows):
    levels = mine.shape[0]
    total, lon_cells, lat_cells = lam.shape
    steps = (total - levels) // 2

    def one(z, carry):
        value = lam[z + steps]
        for c, lanes in enumerate(rows):
            at = pl.multiple_of(z * lon_cells, lon_cells)
            lanes[pl.ds(at, lon_cells), :] = value[:, c * LANES : (c + 1) * LANES]
        return carry

    lax.fori_loop(0, levels, one, 0, unroll=4)
    half = lon_cells // 2
    for part, start in ((mine, place[1] * half), (other, (1 - place[1]) * half)):
        for x in range(half):
            for c, lanes in enumerate(rows):
                picked = lanes[pl.ds(start + x, levels, stride=lon_cells), :]
                at = x * lat_cells + c * LANES
                part[:, at : at + LANES] = picked.astype(jnp.bfloat16)


def fix_kernel(place, sea_ext, out_low, out_high, west, east, mine_in, other_in, mine, other, low, high):
    levels, half = mine.shape
    lat_cells = low.shape[1]
    steps = (sea_ext.shape[0] - levels) // 2
    low[...] = out_low[...] + sea_ext[...] * west[...].astype(jnp.float32)
    high[...] = out_high[...] + sea_ext[...] * east[...].astype(jnp.float32)
    low_rows = low[steps : steps + levels, :].astype(jnp.bfloat16)
    high_rows = high[steps : steps + levels, :].astype(jnp.bfloat16)

    @pl.when(place[1] == 0)
    def _():
        mine[:, :lat_cells] = low_rows
        other[:, half - lat_cells :] = high_rows

    @pl.when(place[1] != 0)
    def _():
        other[:, :lat_cells] = low_rows
        mine[:, half - lat_cells :] = high_rows


def emit_kernel(lam, low, high, out):
    levels, lon_cells, lat_cells = out.shape
    steps = (lam.shape[0] - levels) // 2
    x_at = lax.broadcasted_iota(jnp.int32, (lon_cells, lat_cells), 0)
    first_x, last_x = x_at == 0, x_at == lon_cells - 1

    def one(z, carry):
        at = z + steps
        out[z] = jnp.where(last_x, row(high, at), jnp.where(first_x, row(low, at), lam[at]))
        return carry

    lax.fori_loop(0, levels, one, 0, unroll=4)


def face_kernel(sea_ext, out_low, out_high, west, east, west_gain, east_gain, low, high, to_west, to_east):
    low_rows = out_low[...] + sea_ext[...] * west[...].astype(jnp.float32)
    high_rows = out_high[...] + sea_ext[...] * east[...].astype(jnp.float32)
    low[...], high[...] = low_rows, high_rows
    to_west[...] = (west_gain[...] * low_rows).astype(jnp.bfloat16)
    to_east[...] = (east_gain[...] * high_rows).astype(jnp.bfloat16)


def pack(innovations, courant, diffusivity, bricks):
    levels, lon_cells, lat_cells = diffusivity.shape
    steps = innovations.shape[0] - 1
    table, layers = halo_table(steps)
    f32, bf16 = jnp.float32, jnp.bfloat16
    end = levels // steps - 1

    def edges(shape, axis):
        block = list(shape)
        block[axis] = steps
        at = lambda index: lambda i: tuple(index if a == axis else 0 for a in range(len(shape)))
        return [pl.BlockSpec(tuple(block), at(index)) for index in (0, end)]

    message = jax.ShapeDtypeStruct((layers, lon_cells, lat_cells), bf16)
    return pl.pallas_call(
        functools.partial(pack_kernel, table, ("lon", "depth")),
        grid=(1,),
        in_specs=[VMEM]
        + edges(innovations.shape, 1)
        + edges(courant.shape, 1)
        + edges(diffusivity.shape, 0),
        out_shape=[
            message,
            message,
            jax.ShapeDtypeStruct((levels, lat_cells), f32),
            jax.ShapeDtypeStruct((3,), jnp.int32),
        ],
        out_specs=[VMEM, VMEM, VMEM, SMEM],
        scratch_shapes=[
            pltpu.VMEM((levels, bricks.shape[2]), f32),
        ],
        cost_estimate=pl.CostEstimate(flops=0, bytes_accessed=1 << 20, transcendentals=0),
    )(bricks, innovations, innovations, courant, courant, diffusivity, diffusivity)


def sweep(inputs, sea, before, after, place):
    levels, lon_cells, lat_cells = inputs[2].shape
    steps = inputs[0].shape[0] - 1
    table, _ = halo_table(steps)
    f32, bf16 = jnp.float32, jnp.bfloat16
    extended = (levels + 2 * steps, lat_cells)
    row_of = jax.ShapeDtypeStruct(extended, f32)
    sent_row = jax.ShapeDtypeStruct(extended, bf16)
    cells = jax.ShapeDtypeStruct((levels + 2 * steps, lon_cells, lat_cells), f32)
    sea_ext, east_gain, west_gain, to_east, to_west = pl.pallas_call(
        functools.partial(first_kernel, table),
        in_specs=[VMEM] * 6,
        out_shape=[row_of] * 3 + [sent_row] * 2,
        out_specs=[VMEM] * 5,
        scratch_shapes=[pltpu.VMEM(extended, f32)] * 2,
        compiler_params=pltpu.CompilerParams(vmem_limit_bytes=GRANT),
        cost_estimate=pl.CostEstimate(flops=0, bytes_accessed=1 << 20, transcendentals=0),
    )(*inputs, sea, before, after)
    lam = ()
    low = high = sea_ext
    for step in range(1, steps + 1):
        west = shifted(to_east, "lon", 1)
        east = shifted(to_west, "lon", -1)
        state = (low, high) + lam
        out, out_low, out_high = pl.pallas_call(
            functools.partial(step_kernel, table, step),
            in_specs=[VMEM] * (6 + len(state)),
            out_shape=[cells, row_of, row_of],
            out_specs=[VMEM] * 3,
            compiler_params=pltpu.CompilerParams(vmem_limit_bytes=GRANT),
            cost_estimate=pl.CostEstimate(flops=40 * levels * lon_cells * lat_cells, bytes_accessed=9 << 20, transcendentals=0),
        )(*inputs, sea_ext, before, after, *state)
        if step == steps:
            break
        low, high, to_west, to_east = pl.pallas_call(
            face_kernel,
            in_specs=[VMEM] * 7,
            out_shape=[row_of] * 2 + [sent_row] * 2,
            out_specs=[VMEM] * 4,
            compiler_params=pltpu.CompilerParams(vmem_limit_bytes=GRANT),
            cost_estimate=pl.CostEstimate(flops=0, bytes_accessed=1 << 19, transcendentals=0),
        )(sea_ext, out_low, out_high, west, east, west_gain, east_gain)
        lam = (out,)
    half = (levels, lon_cells * lat_cells // 2)
    mine, other = call(
        lay_kernel,
        (place, out),
        [SMEM, VMEM],
        [(half, bf16)] * 2,
        scratch=[pltpu.VMEM((levels * lon_cells, LANES), f32)] * (lat_cells // LANES),
        moved=3 << 20,
    )
    edge = (sea_ext, out_low, out_high, west, east)
    mine, other, low, high = call(
        fix_kernel,
        (place, *edge, mine, other),
        [SMEM] + [VMEM] * 7,
        [(half, bf16)] * 2 + [(extended, f32)] * 2,
        aliases={6: 0, 7: 1},
    )
    (lam,) = call(
        emit_kernel,
        (out, low, high),
        [VMEM] * 3,
        [((levels, lon_cells, lat_cells), f32)],
        moved=3 << 20,
    )
    return lam, mine, other


def against(a, b):
    return lax.dot_general(a, b, (((1,), (1,)), ((), ())), preferred_element_type=jnp.float32)


def rows_kernel(wide, place, left, left_pair, first, second, kept, sent):
    half = left_pair.shape[1]
    levels = first.shape[0]
    sums = [None, None]
    for at in range(0, half, wide):
        lanes = slice(at, at + wide)
        mine = left[:, pl.ds(pl.multiple_of(place[1] * half + at, LANES), wide)]
        both = jnp.concatenate([first[:, lanes], second[:, lanes]], 0)
        for c, factor in enumerate((mine, left_pair[:, lanes])):
            term = against(factor, both)
            sums[c] = term if at == 0 else sums[c] + term
    for c in range(2):
        kept[c] = sums[c]
        other_order = [sums[c][:, levels:], sums[c][:, :levels]]
        sent[1 - c] = jnp.concatenate(other_order, 1).astype(jnp.bfloat16)


def mask_kernel(slots, place, ranks, *rest):
    stages = [rest[n : n + 2] for n in range(0, STAGES * 2, 2)]
    out = rest[STAGES * 2 :]
    rows = stages[0][0].shape[1] // slots
    for c in range(2):
        owner = place[0] if c == 0 else place[0] + 1 - 2 * place[1]
        for k in range(slots):
            at = slice(k * rows, (k + 1) * rows)
            value = jnp.concatenate(
                [kept[c, at, :] + arrived[c, at, :].astype(jnp.float32) for kept, arrived in stages], 1
            )
            row = lax.broadcasted_iota(jnp.int32, value.shape, 0) + owner * rows
            value = jnp.where(row < ranks[0, k], value, 0.0).astype(jnp.bfloat16)
            if len(out) > 1:
                out[k][c] = value
            else:
                count = out[0].shape[0]
                out[0][lax.rem(place[2] + (k - slots // 2 + count), count), c] = value


def columns_kernel(slots, stage, start, place, right, *rest):
    pieces = PARTS // HALVES
    right_pair, received, out = rest[:pieces], rest[pieces:-2], rest[-2:]
    count = received[0].shape[0]
    levels = out[0].shape[0]
    wide = right_pair[0].shape[1]
    half = wide * PARTS
    picked = slice(stage * levels, (stage + 2) * levels)
    coeffs = []
    for c in range(2):
        for k in range(slots):
            if len(received) > 1:
                coeffs.append(received[k][c, :, picked])
            else:
                source = lax.rem(place[2] + (count + slots // 2 - k), count)
                coeffs.append(received[0][source, c, :, picked])
    stacked = jnp.concatenate(coeffs, 0)
    rows = right.shape[0]
    lead = (((0,), (0,)), ((), ()))
    for n, piece in enumerate(right_pair):
        lanes = slice(n * wide, (n + 1) * wide)
        mine = right[:, pl.ds(pl.multiple_of(place[1] * half + start + n * wide, LANES), wide)]
        total = lax.dot_general(stacked[:rows], mine, lead, preferred_element_type=jnp.float32)
        total = total + lax.dot_general(stacked[rows:], piece[...], lead, preferred_element_type=jnp.float32)
        out[0][:, lanes] = total[:levels].astype(out[0].dtype)
        out[1][:, lanes] = total[levels:].astype(out[1].dtype)


def add_rows(place, own, arrived1, arrived2, arrived3, rows):
    levels = own.shape[0]
    each = rows[0].shape[0] // levels // 2
    f32 = jnp.float32
    wide = own.shape[1] // each
    for x in range(each):
        for c, lanes in enumerate(rows):
            cols = slice(x * wide + c * LANES, x * wide + (c + 1) * LANES)
            mine = own[:, cols] + arrived2[:, cols].astype(f32)
            other = arrived1[:, cols].astype(f32) + arrived3[:, cols].astype(f32)
            lanes[pl.ds(place[1] * each + x, levels, stride=2 * each), :] = mine
            lanes[pl.ds((1 - place[1]) * each + x, levels, stride=2 * each), :] = other


def early_kernel(place, own, arrived1, arrived2, arrived3, *rows):
    add_rows(place, own, arrived1, arrived2, arrived3, rows)


def join_kernel(place, own, arrived1, arrived2, arrived3, *rest):
    early = rest[:LANE_TILES]
    out, slab, sem, *rows = rest[LANE_TILES:]
    add_rows(place, own, arrived1, arrived2, arrived3, rows)
    levels, lon_cells, _ = slab.shape
    half = lon_cells // 2
    each = half // 2
    lower = lax.broadcasted_iota(jnp.int32, (half, LANES), 0) < each
    parts = 4
    size = levels // parts
    copies = []
    for part in range(parts):
        for z in range(part * size, (part + 1) * size):
            for c in range(LANE_TILES):
                a = early[c][z * half : (z + 1) * half, :]
                b = rows[c][z * half : (z + 1) * half, :]
                lanes = slice(c * LANES, (c + 1) * LANES)
                slab[z, :half, lanes] = jnp.where(lower, a, pltpu.roll(b, each, 0))
                slab[z, half:, lanes] = jnp.where(lower, pltpu.roll(a, each, 0), b)
        here = pl.ds(part * size, size)
        copies.append(pltpu.make_async_copy(slab.at[here], out.at[here], sem.at[part]))
        copies[-1].start()
    for copy in copies:
        copy.wait()


def call(kernel, operands, in_specs, outs, grant=GRANT, flops=0, moved=1 << 20, scratch=(), aliases=None):
    return pl.pallas_call(
        kernel,
        in_specs=in_specs,
        out_shape=[jax.ShapeDtypeStruct(*o[:2]) for o in outs],
        out_specs=[o[2] if len(o) > 2 else VMEM for o in outs],
        scratch_shapes=list(scratch),
        input_output_aliases=aliases or {},
        compiler_params=pltpu.CompilerParams(vmem_limit_bytes=grant),
        cost_estimate=pl.CostEstimate(flops=flops, bytes_accessed=moved, transcendentals=0),
    )(*operands)


def per_device(
    innovations, courant, diffusivity, sea_bricks, tile_ranks, row_factors, column_factors
):
    levels, lon_cells, lat_cells = diffusivity.shape
    tile_cols = lon_cells * lat_cells
    half = tile_cols // 2
    slots = tile_ranks.shape[1]
    count = lax.axis_size("depth")
    lon_count = lax.axis_size("lon")
    f32, bf16 = jnp.float32, jnp.bfloat16
    left = row_factors.transpose(0, 1, 3, 2)
    right = column_factors.transpose(0, 1, 3, 2)
    width = left.shape[2]
    rows = slots * width

    down, up, sea, place = pack(innovations, courant, diffusivity, sea_bricks)
    (left_other,) = call(
        halves_kernel,
        (place, left),
        [SMEM, ANY],
        [((slots, width, half), bf16, ANY)],
        grant=WIDE_GRANT,
        moved=2 << 20,
        scratch=[pltpu.VMEM((1, slots, width, half), bf16), pltpu.SemaphoreType.DMA((2,))],
    )
    before = from_behind(down, "depth", 1)
    after = from_behind(up, "depth", -1)
    inputs = (innovations, courant, diffusivity)
    inputs = call(
        load_kernel,
        inputs,
        [ANY] * 3,
        [(a.shape, a.dtype) for a in inputs],
        grant=LOAD_GRANT,
        moved=18 << 20,
        scratch=[pltpu.SemaphoreType.DMA((3,))],
    )
    right_other = call(
        halves_kernel,
        (place, right),
        [SMEM, ANY],
        [((slots, width, half // PARTS), bf16, ANY)] * PARTS,
        moved=4 << 20,
        scratch=[pltpu.VMEM((PARTS, slots, width, half // PARTS), bf16), pltpu.SemaphoreType.DMA((2 * PARTS,))],
    )
    left_pair = swapped(left_other, "depth", 1)
    right_pair = []
    for part in range(PARTS):
        right_pair.append(swapped(right_other[part], "depth", 1).reshape(rows, half // PARTS))
    lam, lam_mine, lam_other = sweep(inputs, sea, before, after, place)
    left_pair = left_pair.reshape(rows, half)
    left, right = left.reshape(rows, tile_cols), right.reshape(rows, tile_cols)
    blocks = {0: lam_mine}
    for mask in range(count - 1, 0, -1):
        blocks[mask] = swapped(lam_other if mask % 2 else lam_mine, "depth", mask)
    sums = []
    for stage in range(0, count, 2):
        pair = (2, rows, 2 * levels)
        kept, sent = call(
            functools.partial(rows_kernel, 4 * LANES),
            (place, left, left_pair, blocks[stage], blocks[stage + 1]),
            [SMEM] + [VMEM] * 4,
            [(pair, f32), (pair, bf16)],
            flops=8 * rows * half * levels,
            moved=3 << 20,
        )
        sums += [kept, swapped(sent, "depth", 1)]
    grouped = lon_count == slots
    slot = (2, width, count * levels)
    coeff = call(
        functools.partial(mask_kernel, slots),
        (place, tile_ranks, *sums),
        [SMEM, SMEM] + [VMEM] * len(sums),
        [((lon_count,) + slot, bf16)] if grouped else [(slot, bf16)] * slots,
    )
    if grouped:
        received = [lax.all_to_all(coeff[0], "lon", 0, 0, tiled=True)]
    else:
        received = [shifted(coeff[k], "lon", k - slots // 2) for k in range(slots)]
    arrived = {mask: [] for mask in range(count)}
    block = (levels, half // HALVES)
    pieces = PARTS // HALVES
    for part in range(HALVES):
        for stage in range(count - 2, -1, -2):
            first, second = call(
                functools.partial(columns_kernel, slots, stage, part * (half // HALVES)),
                (place, right, *right_pair[part * pieces : (part + 1) * pieces], *received),
                [SMEM] + [VMEM] * (1 + pieces + len(received)),
                [(block, bf16 if stage else f32), (block, bf16)],
                flops=8 * rows * half * levels // HALVES,
                moved=2 << 20,
            )
            arrived[stage + 1].append(swapped(second, "depth", stage + 1))
            if stage:
                first = swapped(first, "depth", stage)
            arrived[stage].append(first)
    rows_of = (levels * lon_cells // 2, LANES)
    pieces = [[arrived[mask][part] for mask in range(count)] for part in range(HALVES)]
    early = call(
        early_kernel,
        (place, *pieces[0]),
        [SMEM] + [VMEM] * count,
        [(rows_of, f32)] * LANE_TILES,
        moved=2 << 20,
    )
    (gradient,) = call(
        join_kernel,
        (place, *pieces[1], *early),
        [SMEM] + [VMEM] * (count + LANE_TILES),
        [((levels, lon_cells, lat_cells), f32, ANY)],
        scratch=[pltpu.VMEM((levels, lon_cells, lat_cells), f32), pltpu.SemaphoreType.DMA((4,))]
        + [pltpu.VMEM(rows_of, f32)] * LANE_TILES,
        moved=3 << 20,
    )
    return (lam, gradient)


def solution(mesh):
    placed = (
        P(None, "depth", "lon", None),
        P(None, "depth", "lon", None),
        P("depth", "lon", None),
        P("depth", "lon", None),
        P("lon", None),
        P("lon", None, None, "depth"),
        P("lon", None, None, "depth"),
    )
    return jax.shard_map(
        per_device,
        mesh=mesh,
        in_specs=placed,
        out_specs=(P("depth", "lon", None), P("depth", "lon", None)),
        check_vma=False,
    )
```

```python
import functools
import jax
import jax.numpy as jnp
from jax import lax
from jax.experimental import pallas as pl
from jax.experimental.pallas import tpu as pltpu
from jax.sharding import PartitionSpec as P

UNROLL = 9
LANES = 128
PARTS = 4
LOAD_GRANT = 40 << 20
WIDE_GRANT = 60 << 20
STAGES = 2
LANE_TILES = 2
HALVES = 2
GRANT = 4 << 20
VMEM = pl.BlockSpec(memory_space=pltpu.VMEM)
SMEM = pl.BlockSpec(memory_space=pltpu.SMEM)
ANY = pl.BlockSpec(memory_space=pl.ANY)


def from_behind(value, axis, steps):
    count = lax.axis_size(axis)
    initial, last = (max(0, -steps), min(count, count - steps))
    return lax.ppermute(value, axis, [(source, source + steps) for source in range(initial, last)])


def shifted(block, axis, distance):
    devices = range(lax.axis_size(axis))
    if distance % len(devices) == 0:
        return block
    route = [((i - distance) % len(devices), i) for i in devices]
    return lax.ppermute(block, axis, route)


def swapped(block, axis, mask):
    return lax.ppermute(block, axis, [(i, i ^ mask) for i in range(lax.axis_size(axis))])


def halo_table(depth):
    order, at = {}, 0
    for name, extent in (
        [(("innov", k), min(k, depth - 1)) for k in range(depth, 0, -1)]
        + [("diff", depth - 1), ("c0", depth - 1), ("c1", depth - 1), ("c2", depth - 1)]
    ):
        for distance in range(1, extent + 1):
            order[name, distance] = at
            at += 1
    order["sea"], order["flux"] = at, at + 1
    return order, at + 2


def row(ref, at):
    return ref[pl.ds(at, 1), :]


def pack_kernel(table, bricks, innov_lo, innov_hi, cour_lo, cour_hi, diff_lo, diff_hi, down, up, sea, rows):
    depth = diff_lo.shape[0]
    levels, _, count = bricks.shape
    lat_cells = sea.shape[1]
    for z in range(levels):
        rows[z : z + 1] = bricks[z].astype(jnp.float32)
    brick_at = lax.broadcasted_iota(jnp.int32, (count, lat_cells), 0)
    cell_at = lax.broadcasted_iota(jnp.int32, (count, lat_cells), 1)
    inside = (brick_at == cell_at // (lat_cells // count)).astype(jnp.bfloat16)
    wide = jnp.dot(rows[...].astype(jnp.bfloat16), inside, preferred_element_type=jnp.float32)
    sea[...] = wide
    sea_lo, sea_hi = wide[:depth], wide[levels - depth :]

    def fill(out, innov, cour, diff, sea, level, sign):
        for key, at in table.items():
            if key == "sea":
                rows = [sea[level(d) : level(d) + 1] for d in range(1, depth + 1)]
                rows.append(jnp.zeros((out.shape[1] - depth, out.shape[2]), jnp.float32))
                value = jnp.concatenate(rows, 0)
            elif key == "flux":
                z = level(depth)
                gain = diff[z] + (0.5 * sign) * cour[0, z]
                value = gain * (sea[z : z + 1] * innov[innov.shape[0] - 1, z])
            else:
                name, distance = key
                z = level(distance)
                if name == "diff":
                    value = diff[z]
                elif name == "c0":
                    value = cour[0, z]
                elif name == "c1":
                    value = cour[1, z]
                elif name == "c2":
                    value = cour[2, z]
                else:
                    value = innov[name[1], z]
            out[at] = value.astype(jnp.bfloat16)

    fill(down, innov_hi, cour_hi, diff_hi, sea_hi, lambda d: depth - d, -1.0)
    fill(up, innov_lo, cour_lo, diff_lo, sea_lo, lambda d: d - 1, 1.0)


def load_kernel(*refs):
    count = len(refs) // 2
    copies = [pltpu.make_async_copy(refs[n], refs[count + n], refs[-1].at[n]) for n in range(count)]
    for copy in copies:
        copy.start()
    for copy in copies:
        copy.wait()


def halves_kernel(place, right, *rest):
    targets, (vmem, sems) = rest[:-2], rest[-2:]
    wide = targets[0].shape[2]
    start = (1 - place[1]) * wide * len(targets)
    loads, stores = [], []
    for n, target in enumerate(targets):
        window = pl.ds(pl.multiple_of(start + n * wide, wide), wide)
        loads.append(pltpu.make_async_copy(right.at[0, :, :, window], vmem.at[n], sems.at[n]))
        loads[-1].start()
        stores.append(pltpu.make_async_copy(vmem.at[n], target, sems.at[len(targets) + n]))
    for load, store in zip(loads, stores):
        load.wait()
        store.start()
    for store in stores:
        store.wait()


def first_kernel(table, innov, cour, diff, sea, before, after, sea_ext, east_gain, west_gain, to_east, to_west, east_rows, west_rows):
    steps = innov.shape[0] - 1
    levels, lon_cells, lat_cells = diff.shape
    last = lon_cells - 1

    def put(at, sea_row, diff_a, diff_b, cour_a, cour_b, innov_a, innov_b):
        here = pl.ds(at, 1)
        sea_ext[here, :] = sea_row
        low_row, high_row = sea_row * innov_a, sea_row * innov_b
        west = diff_a + 0.5 * cour_a
        east = diff_b - 0.5 * cour_b
        west_gain[here, :], east_gain[here, :] = west, east
        west_rows[here, :], east_rows[here, :] = west * low_row, east * high_row

    for halo, where in ((before, lambda d: steps - d), (after, lambda d: steps + levels + d - 1)):
        sea_rows = halo[table["sea"]].astype(jnp.float32)
        for d in range(1, steps + 1):
            sea_row = sea_rows[d - 1 : d]
            at = where(d)
            if d == steps:
                zero = jnp.zeros((1, lat_cells), jnp.float32)
                for ref in (sea_ext, west_gain, east_gain, west_rows, east_rows):
                    ref[pl.ds(at, 1), :] = zero
            else:
                dd = halo[table["diff", d]].astype(jnp.float32)
                cc = halo[table["c1", d]].astype(jnp.float32)
                ii = halo[table[("innov", steps), d]].astype(jnp.float32)
                put(at, sea_row, dd[:1], dd[last:], cc[:1], cc[last:], ii[:1], ii[last:])

    def one(z, carry):
        edge = lambda ref: (ref[z, :1], ref[z, last:])
        put(z + steps, row(sea, z), *edge(diff), *edge(cour.at[1]), *edge(innov.at[steps]))
        return carry

    lax.fori_loop(0, levels, one, 0, unroll=4)
    to_west[...] = west_rows[...].astype(jnp.bfloat16)
    to_east[...] = east_rows[...].astype(jnp.bfloat16)


def step_kernel(table, step, innov, cour, diff, sea_ext, before, after, low, high, *rest):
    steps = innov.shape[0] - 1
    levels, lon_cells, lat_cells = diff.shape
    if step > 1:
        lam, rest = rest[0], rest[1:]
    out, out_low, out_high = rest
    last = lon_cells - 1
    x_at = lax.broadcasted_iota(jnp.int32, (lon_cells, lat_cells), 0)
    y_at = lax.broadcasted_iota(jnp.int32, (lon_cells, lat_cells), 1)
    first_x, last_x = x_at == 0, x_at == last
    first_y, last_y = y_at == 0, y_at == lat_cells - 1
    reach = steps - step

    def halo_level(halo, d, name):
        return halo[table[name, d]].astype(jnp.float32)

    def state(at, innovation):
        if step == 1:
            return row(sea_ext, at) * innovation
        value = jnp.where(first_x, row(low, at), lam[at])
        return jnp.where(last_x, row(high, at), value)

    def finish(at, acc, up_flux):
        value = row(sea_ext, at) * (acc + up_flux)
        out[at] = value
        out_low[pl.ds(at, 1), :] = value[:1]
        out_high[pl.ds(at, 1), :] = value[last:]

    def depth_terms(a, d, c):
        spread, drift = d * a, c * (0.5 * a)
        return spread - drift, spread + drift

    def level(a, d, c0, c1, c2, innovation):
        half = 0.5 * a
        spread = d * a
        drift = c0 * half
        plus0, minus0 = spread - drift, spread + drift
        drift = c1 * half
        plus1, minus1 = spread - drift, spread + drift
        drift = c2 * half
        plus2, minus2 = spread - drift, spread + drift
        acc = a - 6.0 * spread + innovation
        acc = acc + jnp.where(first_x, 0.0, pltpu.roll(plus1, 1, 0))
        acc = acc + jnp.where(last_x, 0.0, pltpu.roll(minus1, lon_cells - 1, 0))
        acc = acc + jnp.where(first_y, 0.0, pltpu.roll(plus2, 1, 1))
        acc = acc + jnp.where(last_y, 0.0, pltpu.roll(minus2, lat_cells - 1, 1))
        return acc, plus0, minus0

    def halo_start(halo, d, at):
        return state(at, halo_level(halo, d, ("innov", steps)) if step == 1 else None)

    def halo_full(halo, d, at):
        a = halo_start(halo, d, at)
        return level(
            a,
            halo_level(halo, d, "diff"),
            halo_level(halo, d, "c0"),
            halo_level(halo, d, "c1"),
            halo_level(halo, d, "c2"),
            halo_level(halo, d, ("innov", steps - step)),
        )

    def halo_edge(halo, d, at):
        if step == 1:
            flux = halo[table["flux"]].astype(jnp.float32)
            return flux, flux
        a = halo_start(halo, d, at)
        return depth_terms(a, halo_level(halo, d, "diff"), halo_level(halo, d, "c0"))

    down_flux, _ = halo_edge(before, reach + 1, steps - reach - 1)
    acc = None
    for d in range(reach, 0, -1):
        at = steps - d
        value, plus0, minus0 = halo_full(before, d, at)
        if acc is not None:
            finish(at - 1, acc, minus0)
        acc, down_flux = value + down_flux, plus0

    def own(z):
        a = state(z + steps, innov[steps, z] if step == 1 else None)
        return level(a, diff[z], cour[0, z], cour[1, z], cour[2, z], innov[steps - step, z])

    value, plus0, minus0 = own(0)
    if acc is not None:
        finish(steps - 1, acc, minus0)
    carry = (value + down_flux, plus0)

    def one(z, carry):
        acc, down_flux = carry
        value, plus0, minus0 = own(z)
        finish(z + steps - 1, acc, minus0)
        return value + down_flux, plus0

    head = (levels - 1) % UNROLL
    for z in range(1, 1 + head):
        carry = one(z, carry)

    def several(i, carry):
        for u in range(UNROLL):
            carry = one(1 + head + i * UNROLL + u, carry)
        return carry

    acc, down_flux = lax.fori_loop(0, (levels - 1) // UNROLL, several, carry)
    at = steps + levels - 1
    for d in range(1, reach + 1):
        value, plus0, minus0 = halo_full(after, d, at + d)
        finish(at + d - 1, acc, minus0)
        acc, down_flux = value + down_flux, plus0
    _, up_flux = halo_edge(after, reach + 1, at + reach + 1)
    finish(at + reach, acc, up_flux)


def lay_kernel(place, lam, mine, other, *rows):
    levels = mine.shape[0]
    total, lon_cells, lat_cells = lam.shape
    steps = (total - levels) // 2

    def one(z, carry):
        value = lam[z + steps]
        for c, lanes in enumerate(rows):
            at = pl.multiple_of(z * lon_cells, lon_cells)
            lanes[pl.ds(at, lon_cells), :] = value[:, c * LANES : (c + 1) * LANES]
        return carry

    lax.fori_loop(0, levels, one, 0, unroll=4)
    half = lon_cells // 2
    for part, start in ((mine, place[1] * half), (other, (1 - place[1]) * half)):
        for x in range(half):
            for c, lanes in enumerate(rows):
                picked = lanes[pl.ds(start + x, levels, stride=lon_cells), :]
                at = x * lat_cells + c * LANES
                part[:, at : at + LANES] = picked.astype(jnp.bfloat16)


def fix_kernel(place, sea_ext, out_low, out_high, west, east, mine_in, other_in, mine, other, low, high):
    levels, half = mine.shape
    lat_cells = low.shape[1]
    steps = (sea_ext.shape[0] - levels) // 2
    low[...] = out_low[...] + sea_ext[...] * west[...].astype(jnp.float32)
    high[...] = out_high[...] + sea_ext[...] * east[...].astype(jnp.float32)
    low_rows = low[steps : steps + levels, :].astype(jnp.bfloat16)
    high_rows = high[steps : steps + levels, :].astype(jnp.bfloat16)

    @pl.when(place[1] == 0)
    def _():
        mine[:, :lat_cells] = low_rows
        other[:, half - lat_cells :] = high_rows

    @pl.when(place[1] != 0)
    def _():
        other[:, :lat_cells] = low_rows
        mine[:, half - lat_cells :] = high_rows


def emit_kernel(lam, low, high, out):
    levels, lon_cells, lat_cells = out.shape
    steps = (lam.shape[0] - levels) // 2
    x_at = lax.broadcasted_iota(jnp.int32, (lon_cells, lat_cells), 0)
    first_x, last_x = x_at == 0, x_at == lon_cells - 1

    def one(z, carry):
        at = z + steps
        out[z] = jnp.where(last_x, row(high, at), jnp.where(first_x, row(low, at), lam[at]))
        return carry

    lax.fori_loop(0, levels, one, 0, unroll=4)


def face_kernel(sea_ext, out_low, out_high, west, east, west_gain, east_gain, low, high, to_west, to_east):
    low_rows = out_low[...] + sea_ext[...] * west[...].astype(jnp.float32)
    high_rows = out_high[...] + sea_ext[...] * east[...].astype(jnp.float32)
    low[...], high[...] = low_rows, high_rows
    to_west[...] = (west_gain[...] * low_rows).astype(jnp.bfloat16)
    to_east[...] = (east_gain[...] * high_rows).astype(jnp.bfloat16)


def pack(innovations, courant, diffusivity, bricks):
    levels, lon_cells, lat_cells = diffusivity.shape
    steps = innovations.shape[0] - 1
    table, layers = halo_table(steps)
    f32, bf16 = jnp.float32, jnp.bfloat16
    end = levels // steps - 1

    def edges(shape, axis):
        block = list(shape)
        block[axis] = steps
        at = lambda index: lambda i: tuple(index if a == axis else 0 for a in range(len(shape)))
        return [pl.BlockSpec(tuple(block), at(index)) for index in (0, end)]

    message = jax.ShapeDtypeStruct((layers, lon_cells, lat_cells), bf16)
    return pl.pallas_call(
        functools.partial(pack_kernel, table),
        grid=(1,),
        in_specs=[VMEM]
        + edges(innovations.shape, 1)
        + edges(courant.shape, 1)
        + edges(diffusivity.shape, 0),
        out_shape=[
            message,
            message,
            jax.ShapeDtypeStruct((levels, lat_cells), f32),
        ],
        out_specs=[VMEM, VMEM, VMEM],
        scratch_shapes=[
            pltpu.VMEM((levels, bricks.shape[2]), f32),
        ],
        cost_estimate=pl.CostEstimate(flops=0, bytes_accessed=1 << 20, transcendentals=0),
    )(bricks, innovations, innovations, courant, courant, diffusivity, diffusivity)


def sweep(inputs, sea, before, after, place):
    levels, lon_cells, lat_cells = inputs[2].shape
    steps = inputs[0].shape[0] - 1
    table, _ = halo_table(steps)
    f32, bf16 = jnp.float32, jnp.bfloat16
    extended = (levels + 2 * steps, lat_cells)
    row_of = jax.ShapeDtypeStruct(extended, f32)
    sent_row = jax.ShapeDtypeStruct(extended, bf16)
    cells = jax.ShapeDtypeStruct((levels + 2 * steps, lon_cells, lat_cells), f32)
    sea_ext, east_gain, west_gain, to_east, to_west = pl.pallas_call(
        functools.partial(first_kernel, table),
        in_specs=[VMEM] * 6,
        out_shape=[row_of] * 3 + [sent_row] * 2,
        out_specs=[VMEM] * 5,
        scratch_shapes=[pltpu.VMEM(extended, f32)] * 2,
        compiler_params=pltpu.CompilerParams(vmem_limit_bytes=GRANT),
        cost_estimate=pl.CostEstimate(flops=0, bytes_accessed=1 << 20, transcendentals=0),
    )(*inputs, sea, before, after)
    lam = ()
    low = high = sea_ext
    for step in range(1, steps + 1):
        west = shifted(to_east, "lon", 1)
        east = shifted(to_west, "lon", -1)
        state = (low, high) + lam
        out, out_low, out_high = pl.pallas_call(
            functools.partial(step_kernel, table, step),
            in_specs=[VMEM] * (6 + len(state)),
            out_shape=[cells, row_of, row_of],
            out_specs=[VMEM] * 3,
            compiler_params=pltpu.CompilerParams(vmem_limit_bytes=GRANT),
            cost_estimate=pl.CostEstimate(flops=40 * levels * lon_cells * lat_cells, bytes_accessed=9 << 20, transcendentals=0),
        )(*inputs, sea_ext, before, after, *state)
        if step == steps:
            break
        low, high, to_west, to_east = pl.pallas_call(
            face_kernel,
            in_specs=[VMEM] * 7,
            out_shape=[row_of] * 2 + [sent_row] * 2,
            out_specs=[VMEM] * 4,
            compiler_params=pltpu.CompilerParams(vmem_limit_bytes=GRANT),
            cost_estimate=pl.CostEstimate(flops=0, bytes_accessed=1 << 19, transcendentals=0),
        )(sea_ext, out_low, out_high, west, east, west_gain, east_gain)
        lam = (out,)
    half = (levels, lon_cells * lat_cells // 2)
    mine, other = call(
        lay_kernel,
        (place, out),
        [SMEM, VMEM],
        [(half, bf16)] * 2,
        scratch=[pltpu.VMEM((levels * lon_cells, LANES), f32)] * (lat_cells // LANES),
        moved=3 << 20,
    )
    edge = (sea_ext, out_low, out_high, west, east)
    mine, other, low, high = call(
        fix_kernel,
        (place, *edge, mine, other),
        [SMEM] + [VMEM] * 7,
        [(half, bf16)] * 2 + [(extended, f32)] * 2,
        aliases={5: 0, 6: 1},
    )
    (lam,) = call(
        emit_kernel,
        (out, low, high),
        [VMEM] * 3,
        [((levels, lon_cells, lat_cells), f32)],
        moved=3 << 20,
    )
    return lam, mine, other


def against(a, b):
    return lax.dot_general(a, b, (((1,), (1,)), ((), ())), preferred_element_type=jnp.float32)


def rows_kernel(wide, place, left, left_pair, first, second, kept, sent):
    half = left_pair.shape[1]
    levels = first.shape[0]
    sums = [None, None]
    for at in range(0, half, wide):
        lanes = slice(at, at + wide)
        mine = left[:, pl.ds(pl.multiple_of(place[1] * half + at, LANES), wide)]
        both = jnp.concatenate([first[:, lanes], second[:, lanes]], 0)
        for c, factor in enumerate((mine, left_pair[:, lanes])):
            term = against(factor, both)
            sums[c] = term if at == 0 else sums[c] + term
    for c in range(2):
        kept[c] = sums[c]
        other_order = [sums[c][:, levels:], sums[c][:, :levels]]
        sent[1 - c] = jnp.concatenate(other_order, 1).astype(jnp.bfloat16)


def mask_kernel(slots, place, ranks, *rest):
    stages = [rest[n : n + 2] for n in range(0, STAGES * 2, 2)]
    out = rest[STAGES * 2 :]
    rows = stages[0][0].shape[1] // slots
    for c in range(2):
        owner = place[0] if c == 0 else place[0] + 1 - 2 * place[1]
        for k in range(slots):
            at = slice(k * rows, (k + 1) * rows)
            value = jnp.concatenate(
                [kept[c, at, :] + arrived[c, at, :].astype(jnp.float32) for kept, arrived in stages], 1
            )
            row = lax.broadcasted_iota(jnp.int32, value.shape, 0) + owner * rows
            value = jnp.where(row < ranks[:1, k : k + 1], value, 0.0).astype(jnp.bfloat16)
            if len(out) > 1:
                out[k][c] = value
            else:
                count = out[0].shape[0]
                out[0][lax.rem(place[2] + (k - slots // 2 + count), count), c] = value


def columns_kernel(slots, stage, start, place, right, *rest):
    pieces = PARTS // HALVES
    right_pair, received, out = rest[:pieces], rest[pieces:-2], rest[-2:]
    count = received[0].shape[0]
    levels = out[0].shape[0]
    wide = right_pair[0].shape[1]
    half = wide * PARTS
    picked = slice(stage * levels, (stage + 2) * levels)
    coeffs = []
    for c in range(2):
        for k in range(slots):
            if len(received) > 1:
                coeffs.append(received[k][c, :, picked])
            else:
                source = lax.rem(place[2] + (count + slots // 2 - k), count)
                coeffs.append(received[0][source, c, :, picked])
    stacked = jnp.concatenate(coeffs, 0)
    rows = right.shape[0]
    lead = (((0,), (0,)), ((), ()))
    for n, piece in enumerate(right_pair):
        lanes = slice(n * wide, (n + 1) * wide)
        mine = right[:, pl.ds(pl.multiple_of(place[1] * half + start + n * wide, LANES), wide)]
        total = lax.dot_general(stacked[:rows], mine, lead, preferred_element_type=jnp.float32)
        total = total + lax.dot_general(stacked[rows:], piece[...], lead, preferred_element_type=jnp.float32)
        out[0][:, lanes] = total[:levels].astype(out[0].dtype)
        out[1][:, lanes] = total[levels:].astype(out[1].dtype)


def add_rows(place, own, arrived1, arrived2, arrived3, rows):
    levels = own.shape[0]
    each = rows[0].shape[0] // levels // 2
    f32 = jnp.float32
    wide = own.shape[1] // each
    for x in range(each):
        for c, lanes in enumerate(rows):
            cols = slice(x * wide + c * LANES, x * wide + (c + 1) * LANES)
            mine = own[:, cols] + arrived2[:, cols].astype(f32)
            other = arrived1[:, cols].astype(f32) + arrived3[:, cols].astype(f32)
            lanes[pl.ds(place[1] * each + x, levels, stride=2 * each), :] = mine
            lanes[pl.ds((1 - place[1]) * each + x, levels, stride=2 * each), :] = other


def early_kernel(place, own, arrived1, arrived2, arrived3, *rows):
    add_rows(place, own, arrived1, arrived2, arrived3, rows)


def join_kernel(place, own, arrived1, arrived2, arrived3, *rest):
    early = rest[:LANE_TILES]
    out, slab, sem, *rows = rest[LANE_TILES:]
    add_rows(place, own, arrived1, arrived2, arrived3, rows)
    levels, lon_cells, _ = slab.shape
    half = lon_cells // 2
    each = half // 2
    lower = lax.broadcasted_iota(jnp.int32, (half, LANES), 0) < each
    parts = 4
    size = levels // parts
    copies = []
    for part in range(parts):
        for z in range(part * size, (part + 1) * size):
            for c in range(LANE_TILES):
                a = early[c][z * half : (z + 1) * half, :]
                b = rows[c][z * half : (z + 1) * half, :]
                lanes = slice(c * LANES, (c + 1) * LANES)
                slab[z, :half, lanes] = jnp.where(lower, a, pltpu.roll(b, each, 0))
                slab[z, half:, lanes] = jnp.where(lower, pltpu.roll(a, each, 0), b)
        here = pl.ds(part * size, size)
        copies.append(pltpu.make_async_copy(slab.at[here], out.at[here], sem.at[part]))
        copies[-1].start()
    for copy in copies:
        copy.wait()


HERE = object()


def located(kernel):
    def run(*refs):
        me = lax.axis_index("depth")
        return kernel((me, lax.rem(me, 2), lax.axis_index("lon")), *refs)

    return run


def call(kernel, operands, in_specs, outs, grant=GRANT, flops=0, moved=1 << 20, scratch=(), aliases=None):
    if operands[0] is HERE:
        kernel, operands, in_specs = located(kernel), operands[1:], in_specs[1:]
    return pl.pallas_call(
        kernel,
        in_specs=in_specs,
        out_shape=[jax.ShapeDtypeStruct(*o[:2]) for o in outs],
        out_specs=[o[2] if len(o) > 2 else VMEM for o in outs],
        scratch_shapes=list(scratch),
        input_output_aliases=aliases or {},
        compiler_params=pltpu.CompilerParams(vmem_limit_bytes=grant),
        cost_estimate=pl.CostEstimate(flops=flops, bytes_accessed=moved, transcendentals=0),
    )(*operands)


def per_device(
    innovations, courant, diffusivity, sea_bricks, tile_ranks, row_factors, column_factors
):
    levels, lon_cells, lat_cells = diffusivity.shape
    tile_cols = lon_cells * lat_cells
    half = tile_cols // 2
    slots = tile_ranks.shape[1]
    count = lax.axis_size("depth")
    lon_count = lax.axis_size("lon")
    f32, bf16 = jnp.float32, jnp.bfloat16
    left = row_factors.transpose(0, 1, 3, 2)
    right = column_factors.transpose(0, 1, 3, 2)
    width = left.shape[2]
    rows = slots * width

    down, up, sea = pack(innovations, courant, diffusivity, sea_bricks)
    place = HERE
    (left_other,) = call(
        halves_kernel,
        (place, left),
        [SMEM, ANY],
        [((slots, width, half), bf16, ANY)],
        grant=WIDE_GRANT,
        moved=2 << 20,
        scratch=[pltpu.VMEM((1, slots, width, half), bf16), pltpu.SemaphoreType.DMA((2,))],
    )
    before = from_behind(down, "depth", 1)
    after = from_behind(up, "depth", -1)
    inputs = (innovations, courant, diffusivity)
    inputs = call(
        load_kernel,
        inputs,
        [ANY] * 3,
        [(a.shape, a.dtype) for a in inputs],
        grant=LOAD_GRANT,
        moved=18 << 20,
        scratch=[pltpu.SemaphoreType.DMA((3,))],
    )
    right_other = call(
        halves_kernel,
        (place, right),
        [SMEM, ANY],
        [((slots, width, half // PARTS), bf16, ANY)] * PARTS,
        moved=4 << 20,
        scratch=[pltpu.VMEM((PARTS, slots, width, half // PARTS), bf16), pltpu.SemaphoreType.DMA((2 * PARTS,))],
    )
    left_pair = swapped(left_other, "depth", 1)
    right_pair = []
    for part in range(PARTS):
        right_pair.append(swapped(right_other[part], "depth", 1).reshape(rows, half // PARTS))
    lam, lam_mine, lam_other = sweep(inputs, sea, before, after, place)
    left_pair = left_pair.reshape(rows, half)
    left, right = left.reshape(rows, tile_cols), right.reshape(rows, tile_cols)
    blocks = {0: lam_mine}
    for mask in range(count - 1, 0, -1):
        blocks[mask] = swapped(lam_other if mask % 2 else lam_mine, "depth", mask)
    sums = []
    for stage in range(0, count, 2):
        pair = (2, rows, 2 * levels)
        kept, sent = call(
            functools.partial(rows_kernel, 4 * LANES),
            (place, left, left_pair, blocks[stage], blocks[stage + 1]),
            [SMEM] + [VMEM] * 4,
            [(pair, f32), (pair, bf16)],
            flops=8 * rows * half * levels,
            moved=3 << 20,
        )
        sums += [kept, swapped(sent, "depth", 1)]
    grouped = False
    slot = (2, width, count * levels)
    coeff = call(
        functools.partial(mask_kernel, slots),
        (place, tile_ranks, *sums),
        [SMEM, VMEM] + [VMEM] * len(sums),
        [((lon_count,) + slot, bf16)] if grouped else [(slot, bf16)] * slots,
    )
    if grouped:
        received = [lax.all_to_all(coeff[0], "lon", 0, 0, tiled=True)]
    else:
        received = [shifted(coeff[k], "lon", k - slots // 2) for k in range(slots)]
    arrived = {mask: [] for mask in range(count)}
    block = (levels, half // HALVES)
    pieces = PARTS // HALVES
    for part in range(HALVES):
        for stage in range(count - 2, -1, -2):
            first, second = call(
                functools.partial(columns_kernel, slots, stage, part * (half // HALVES)),
                (place, right, *right_pair[part * pieces : (part + 1) * pieces], *received),
                [SMEM] + [VMEM] * (1 + pieces + len(received)),
                [(block, bf16 if stage else f32), (block, bf16)],
                flops=8 * rows * half * levels // HALVES,
                moved=2 << 20,
            )
            arrived[stage + 1].append(swapped(second, "depth", stage + 1))
            if stage:
                first = swapped(first, "depth", stage)
            arrived[stage].append(first)
    rows_of = (levels * lon_cells // 2, LANES)
    pieces = [[arrived[mask][part] for mask in range(count)] for part in range(HALVES)]
    early = call(
        early_kernel,
        (place, *pieces[0]),
        [SMEM] + [VMEM] * count,
        [(rows_of, f32)] * LANE_TILES,
        moved=2 << 20,
    )
    (gradient,) = call(
        join_kernel,
        (place, *pieces[1], *early),
        [SMEM] + [VMEM] * (count + LANE_TILES),
        [((levels, lon_cells, lat_cells), f32, ANY)],
        scratch=[pltpu.VMEM((levels, lon_cells, lat_cells), f32), pltpu.SemaphoreType.DMA((4,))]
        + [pltpu.VMEM(rows_of, f32)] * LANE_TILES,
        moved=3 << 20,
    )
    return (lam, gradient)


def solution(mesh):
    placed = (
        P(None, "depth", "lon", None),
        P(None, "depth", "lon", None),
        P("depth", "lon", None),
        P("depth", "lon", None),
        P("lon", None),
        P("lon", None, None, "depth"),
        P("lon", None, None, "depth"),
    )
    return jax.shard_map(
        per_device,
        mesh=mesh,
        in_specs=placed,
        out_specs=(P("depth", "lon", None), P("depth", "lon", None)),
        check_vma=False,
    )
```

```python
import functools
import jax
import jax.numpy as jnp
from jax import lax
from jax.experimental import pallas as pl
from jax.experimental.pallas import tpu as pltpu
from jax.sharding import PartitionSpec as P

UNROLL = 9
LANES = 128
PARTS = 4
LOAD_GRANT = 40 << 20
WIDE_GRANT = 60 << 20
STAGES = 2
LANE_TILES = 2
HALVES = 2
GRANT = 4 << 20
VMEM = pl.BlockSpec(memory_space=pltpu.VMEM)
SMEM = pl.BlockSpec(memory_space=pltpu.SMEM)
ANY = pl.BlockSpec(memory_space=pl.ANY)


def from_behind(value, axis, steps):
    count = lax.axis_size(axis)
    initial, last = (max(0, -steps), min(count, count - steps))
    return lax.ppermute(value, axis, [(source, source + steps) for source in range(initial, last)])


def shifted(block, axis, distance):
    devices = range(lax.axis_size(axis))
    if distance % len(devices) == 0:
        return block
    route = [((i - distance) % len(devices), i) for i in devices]
    return lax.ppermute(block, axis, route)


def swapped(block, axis, mask):
    return lax.ppermute(block, axis, [(i, i ^ mask) for i in range(lax.axis_size(axis))])


def halo_table(depth):
    order, at = {}, 0
    for name, extent in (
        [(("innov", k), min(k, depth - 1)) for k in range(depth, 0, -1)]
        + [("diff", depth - 1), ("c0", depth - 1), ("c1", depth - 1), ("c2", depth - 1)]
    ):
        for distance in range(1, extent + 1):
            order[name, distance] = at
            at += 1
    order["sea"], order["flux"] = at, at + 1
    return order, at + 2


def row(ref, at):
    return ref[pl.ds(at, 1), :]


def pack_kernel(table, bricks, innov_lo, innov_hi, cour_lo, cour_hi, diff_lo, diff_hi, down, up, sea, rows):
    depth = diff_lo.shape[0]
    levels, _, count = bricks.shape
    lat_cells = sea.shape[1]
    for z in range(levels):
        rows[z : z + 1] = bricks[z].astype(jnp.float32)
    brick_at = lax.broadcasted_iota(jnp.int32, (count, lat_cells), 0)
    cell_at = lax.broadcasted_iota(jnp.int32, (count, lat_cells), 1)
    inside = (brick_at == cell_at // (lat_cells // count)).astype(jnp.bfloat16)
    wide = jnp.dot(rows[...].astype(jnp.bfloat16), inside, preferred_element_type=jnp.float32)
    sea[...] = wide
    sea_lo, sea_hi = wide[:depth], wide[levels - depth :]

    def fill(out, innov, cour, diff, sea, level, sign):
        for key, at in table.items():
            if key == "sea":
                rows = [sea[level(d) : level(d) + 1] for d in range(1, depth + 1)]
                rows.append(jnp.zeros((out.shape[1] - depth, out.shape[2]), jnp.float32))
                value = jnp.concatenate(rows, 0)
            elif key == "flux":
                z = level(depth)
                gain = diff[z] + (0.5 * sign) * cour[0, z]
                value = gain * (sea[z : z + 1] * innov[innov.shape[0] - 1, z])
            else:
                name, distance = key
                z = level(distance)
                if name == "diff":
                    value = diff[z]
                elif name == "c0":
                    value = cour[0, z]
                elif name == "c1":
                    value = cour[1, z]
                elif name == "c2":
                    value = cour[2, z]
                else:
                    value = innov[name[1], z]
            out[at] = value.astype(jnp.bfloat16)

    fill(down, innov_hi, cour_hi, diff_hi, sea_hi, lambda d: depth - d, -1.0)
    fill(up, innov_lo, cour_lo, diff_lo, sea_lo, lambda d: d - 1, 1.0)


def load_kernel(*refs):
    count = len(refs) // 2
    copies = []
    for source, target in zip(refs[:count], refs[count : 2 * count]):
        leading = range(source.shape[0]) if len(source.shape) > 3 else (pl.ds(0, source.shape[0]),)
        for n in leading:
            copies.append(pltpu.make_async_copy(source.at[n], target.at[n], refs[-1].at[len(copies)]))
            copies[-1].start()
    for copy in copies:
        copy.wait()


def halves_kernel(place, right, *rest):
    targets, (vmem, sems) = rest[:-2], rest[-2:]
    wide = targets[0].shape[2]
    start = (1 - place[1]) * wide * len(targets)
    loads, stores = [], []
    for n, target in enumerate(targets):
        window = pl.ds(pl.multiple_of(start + n * wide, wide), wide)
        loads.append(pltpu.make_async_copy(right.at[0, :, :, window], vmem.at[n], sems.at[n]))
        loads[-1].start()
        stores.append(pltpu.make_async_copy(vmem.at[n], target, sems.at[len(targets) + n]))
    for load, store in zip(loads, stores):
        load.wait()
        store.start()
    for store in stores:
        store.wait()


def left_kernel(place, right, *rest):
    targets, (vmem, sems) = rest[:-2], rest[-2:]
    wide = targets[0].shape[2]
    start = (1 - place[1]) * wide * len(targets)
    loads, stores = [], []
    for n, target in enumerate(targets):
        window = pl.ds(pl.multiple_of(start + n * wide, wide), wide)
        for k in range(target.shape[0]):
            at = len(loads)
            loads.append(pltpu.make_async_copy(right.at[0, k, :, window], vmem.at[n, k], sems.at[0, at]))
            loads[-1].start()
            stores.append(pltpu.make_async_copy(vmem.at[n, k], target.at[k], sems.at[1, at]))
    for load, store in zip(loads, stores):
        load.wait()
        store.start()
    for store in stores:
        store.wait()


def first_kernel(table, innov, cour, diff, sea, before, after, sea_ext, east_gain, west_gain, to_east, to_west, east_rows, west_rows):
    steps = innov.shape[0] - 1
    levels, lon_cells, lat_cells = diff.shape
    last = lon_cells - 1

    def put(at, sea_row, diff_a, diff_b, cour_a, cour_b, innov_a, innov_b):
        here = pl.ds(at, 1)
        sea_ext[here, :] = sea_row
        low_row, high_row = sea_row * innov_a, sea_row * innov_b
        west = diff_a + 0.5 * cour_a
        east = diff_b - 0.5 * cour_b
        west_gain[here, :], east_gain[here, :] = west, east
        west_rows[here, :], east_rows[here, :] = west * low_row, east * high_row

    for halo, where in ((before, lambda d: steps - d), (after, lambda d: steps + levels + d - 1)):
        sea_rows = halo[table["sea"]].astype(jnp.float32)
        for d in range(1, steps + 1):
            sea_row = sea_rows[d - 1 : d]
            at = where(d)
            if d == steps:
                zero = jnp.zeros((1, lat_cells), jnp.float32)
                for ref in (sea_ext, west_gain, east_gain, west_rows, east_rows):
                    ref[pl.ds(at, 1), :] = zero
            else:
                dd = halo[table["diff", d]].astype(jnp.float32)
                cc = halo[table["c1", d]].astype(jnp.float32)
                ii = halo[table[("innov", steps), d]].astype(jnp.float32)
                put(at, sea_row, dd[:1], dd[last:], cc[:1], cc[last:], ii[:1], ii[last:])

    def one(z, carry):
        edge = lambda ref: (ref[z, :1], ref[z, last:])
        put(z + steps, row(sea, z), *edge(diff), *edge(cour.at[1]), *edge(innov.at[steps]))
        return carry

    lax.fori_loop(0, levels, one, 0, unroll=4)
    to_west[...] = west_rows[...].astype(jnp.bfloat16)
    to_east[...] = east_rows[...].astype(jnp.bfloat16)


def step_kernel(table, step, innov, cour, diff, sea_ext, before, after, low, high, *rest):
    steps = innov.shape[0] - 1
    levels, lon_cells, lat_cells = diff.shape
    if step > 1:
        lam, rest = rest[0], rest[1:]
    out, out_low, out_high = rest
    last = lon_cells - 1
    x_at = lax.broadcasted_iota(jnp.int32, (lon_cells, lat_cells), 0)
    y_at = lax.broadcasted_iota(jnp.int32, (lon_cells, lat_cells), 1)
    first_x, last_x = x_at == 0, x_at == last
    first_y, last_y = y_at == 0, y_at == lat_cells - 1
    reach = steps - step

    def halo_level(halo, d, name):
        return halo[table[name, d]].astype(jnp.float32)

    def state(at, innovation):
        if step == 1:
            return row(sea_ext, at) * innovation
        value = jnp.where(first_x, row(low, at), lam[at])
        return jnp.where(last_x, row(high, at), value)

    def finish(at, acc, up_flux):
        value = row(sea_ext, at) * (acc + up_flux)
        out[at] = value
        out_low[pl.ds(at, 1), :] = value[:1]
        out_high[pl.ds(at, 1), :] = value[last:]

    def depth_terms(a, d, c):
        spread, drift = d * a, c * (0.5 * a)
        return spread - drift, spread + drift

    def level(a, d, c0, c1, c2, innovation):
        half = 0.5 * a
        spread = d * a
        drift = c0 * half
        plus0, minus0 = spread - drift, spread + drift
        drift = c1 * half
        plus1, minus1 = spread - drift, spread + drift
        drift = c2 * half
        plus2, minus2 = spread - drift, spread + drift
        acc = a - 6.0 * spread + innovation
        acc = acc + jnp.where(first_x, 0.0, pltpu.roll(plus1, 1, 0))
        acc = acc + jnp.where(last_x, 0.0, pltpu.roll(minus1, lon_cells - 1, 0))
        acc = acc + jnp.where(first_y, 0.0, pltpu.roll(plus2, 1, 1))
        acc = acc + jnp.where(last_y, 0.0, pltpu.roll(minus2, lat_cells - 1, 1))
        return acc, plus0, minus0

    def halo_start(halo, d, at):
        return state(at, halo_level(halo, d, ("innov", steps)) if step == 1 else None)

    def halo_full(halo, d, at):
        a = halo_start(halo, d, at)
        return level(
            a,
            halo_level(halo, d, "diff"),
            halo_level(halo, d, "c0"),
            halo_level(halo, d, "c1"),
            halo_level(halo, d, "c2"),
            halo_level(halo, d, ("innov", steps - step)),
        )

    def halo_edge(halo, d, at):
        if step == 1:
            flux = halo[table["flux"]].astype(jnp.float32)
            return flux, flux
        a = halo_start(halo, d, at)
        return depth_terms(a, halo_level(halo, d, "diff"), halo_level(halo, d, "c0"))

    down_flux, _ = halo_edge(before, reach + 1, steps - reach - 1)
    acc = None
    for d in range(reach, 0, -1):
        at = steps - d
        value, plus0, minus0 = halo_full(before, d, at)
        if acc is not None:
            finish(at - 1, acc, minus0)
        acc, down_flux = value + down_flux, plus0

    def own(z):
        a = state(z + steps, innov[steps, z] if step == 1 else None)
        return level(a, diff[z], cour[0, z], cour[1, z], cour[2, z], innov[steps - step, z])

    value, plus0, minus0 = own(0)
    if acc is not None:
        finish(steps - 1, acc, minus0)
    carry = (value + down_flux, plus0)

    def one(z, carry):
        acc, down_flux = carry
        value, plus0, minus0 = own(z)
        finish(z + steps - 1, acc, minus0)
        return value + down_flux, plus0

    head = (levels - 1) % UNROLL
    for z in range(1, 1 + head):
        carry = one(z, carry)

    def several(i, carry):
        for u in range(UNROLL):
            carry = one(1 + head + i * UNROLL + u, carry)
        return carry

    acc, down_flux = lax.fori_loop(0, (levels - 1) // UNROLL, several, carry)
    at = steps + levels - 1
    for d in range(1, reach + 1):
        value, plus0, minus0 = halo_full(after, d, at + d)
        finish(at + d - 1, acc, minus0)
        acc, down_flux = value + down_flux, plus0
    _, up_flux = halo_edge(after, reach + 1, at + reach + 1)
    finish(at + reach, acc, up_flux)


def lay_kernel(place, lam, mine, other, *rows):
    levels = mine.shape[0]
    total, lon_cells, lat_cells = lam.shape
    steps = (total - levels) // 2

    def one(z, carry):
        value = lam[z + steps]
        for c, lanes in enumerate(rows):
            at = pl.multiple_of(z * lon_cells, lon_cells)
            lanes[pl.ds(at, lon_cells), :] = value[:, c * LANES : (c + 1) * LANES]
        return carry

    lax.fori_loop(0, levels, one, 0, unroll=4)
    half = lon_cells // 2
    for part, start in ((mine, place[1] * half), (other, (1 - place[1]) * half)):
        for x in range(half):
            for c, lanes in enumerate(rows):
                picked = lanes[pl.ds(start + x, levels, stride=lon_cells), :]
                at = x * lat_cells + c * LANES
                part[:, at : at + LANES] = picked.astype(jnp.bfloat16)


def fix_kernel(place, sea_ext, out_low, out_high, west, east, mine_in, other_in, mine, other, low, high):
    levels, half = mine.shape
    lat_cells = low.shape[1]
    steps = (sea_ext.shape[0] - levels) // 2
    low[...] = out_low[...] + sea_ext[...] * west[...].astype(jnp.float32)
    high[...] = out_high[...] + sea_ext[...] * east[...].astype(jnp.float32)
    low_rows = low[steps : steps + levels, :].astype(jnp.bfloat16)
    high_rows = high[steps : steps + levels, :].astype(jnp.bfloat16)

    @pl.when(place[1] == 0)
    def _():
        mine[:, :lat_cells] = low_rows
        other[:, half - lat_cells :] = high_rows

    @pl.when(place[1] != 0)
    def _():
        other[:, :lat_cells] = low_rows
        mine[:, half - lat_cells :] = high_rows


def emit_kernel(lam, low, high, out):
    levels, lon_cells, lat_cells = out.shape
    steps = (lam.shape[0] - levels) // 2
    x_at = lax.broadcasted_iota(jnp.int32, (lon_cells, lat_cells), 0)
    first_x, last_x = x_at == 0, x_at == lon_cells - 1

    def one(z, carry):
        at = z + steps
        out[z] = jnp.where(last_x, row(high, at), jnp.where(first_x, row(low, at), lam[at]))
        return carry

    lax.fori_loop(0, levels, one, 0, unroll=4)


def face_kernel(sea_ext, out_low, out_high, west, east, west_gain, east_gain, low, high, to_west, to_east):
    low_rows = out_low[...] + sea_ext[...] * west[...].astype(jnp.float32)
    high_rows = out_high[...] + sea_ext[...] * east[...].astype(jnp.float32)
    low[...], high[...] = low_rows, high_rows
    to_west[...] = (west_gain[...] * low_rows).astype(jnp.bfloat16)
    to_east[...] = (east_gain[...] * high_rows).astype(jnp.bfloat16)


def pack(innovations, courant, diffusivity, bricks):
    levels, lon_cells, lat_cells = diffusivity.shape
    steps = innovations.shape[0] - 1
    table, layers = halo_table(steps)
    f32, bf16 = jnp.float32, jnp.bfloat16
    end = levels // steps - 1

    def edges(shape, axis):
        block = list(shape)
        block[axis] = steps
        at = lambda index: lambda i: tuple(index if a == axis else 0 for a in range(len(shape)))
        return [pl.BlockSpec(tuple(block), at(index)) for index in (0, end)]

    message = jax.ShapeDtypeStruct((layers, lon_cells, lat_cells), bf16)
    return pl.pallas_call(
        functools.partial(pack_kernel, table),
        grid=(1,),
        in_specs=[VMEM]
        + edges(innovations.shape, 1)
        + edges(courant.shape, 1)
        + edges(diffusivity.shape, 0),
        out_shape=[
            message,
            message,
            jax.ShapeDtypeStruct((levels, lat_cells), f32),
        ],
        out_specs=[VMEM, VMEM, VMEM],
        scratch_shapes=[
            pltpu.VMEM((levels, bricks.shape[2]), f32),
        ],
        cost_estimate=pl.CostEstimate(flops=0, bytes_accessed=1 << 20, transcendentals=0),
    )(bricks, innovations, innovations, courant, courant, diffusivity, diffusivity)


def sweep(inputs, sea, before, after, place):
    levels, lon_cells, lat_cells = inputs[2].shape
    steps = inputs[0].shape[0] - 1
    table, _ = halo_table(steps)
    f32, bf16 = jnp.float32, jnp.bfloat16
    extended = (levels + 2 * steps, lat_cells)
    row_of = jax.ShapeDtypeStruct(extended, f32)
    sent_row = jax.ShapeDtypeStruct(extended, bf16)
    cells = jax.ShapeDtypeStruct((levels + 2 * steps, lon_cells, lat_cells), f32)
    sea_ext, east_gain, west_gain, to_east, to_west = pl.pallas_call(
        functools.partial(first_kernel, table),
        in_specs=[VMEM] * 6,
        out_shape=[row_of] * 3 + [sent_row] * 2,
        out_specs=[VMEM] * 5,
        scratch_shapes=[pltpu.VMEM(extended, f32)] * 2,
        compiler_params=pltpu.CompilerParams(vmem_limit_bytes=GRANT),
        cost_estimate=pl.CostEstimate(flops=0, bytes_accessed=1 << 20, transcendentals=0),
    )(*inputs, sea, before, after)
    lam = ()
    low = high = sea_ext
    for step in range(1, steps + 1):
        west = shifted(to_east, "lon", 1)
        east = shifted(to_west, "lon", -1)
        state = (low, high) + lam
        out, out_low, out_high = pl.pallas_call(
            functools.partial(step_kernel, table, step),
            in_specs=[VMEM] * (6 + len(state)),
            out_shape=[cells, row_of, row_of],
            out_specs=[VMEM] * 3,
            compiler_params=pltpu.CompilerParams(vmem_limit_bytes=GRANT),
            cost_estimate=pl.CostEstimate(flops=40 * levels * lon_cells * lat_cells, bytes_accessed=9 << 20, transcendentals=0),
        )(*inputs, sea_ext, before, after, *state)
        if step == steps:
            break
        low, high, to_west, to_east = pl.pallas_call(
            face_kernel,
            in_specs=[VMEM] * 7,
            out_shape=[row_of] * 2 + [sent_row] * 2,
            out_specs=[VMEM] * 4,
            compiler_params=pltpu.CompilerParams(vmem_limit_bytes=GRANT),
            cost_estimate=pl.CostEstimate(flops=0, bytes_accessed=1 << 19, transcendentals=0),
        )(sea_ext, out_low, out_high, west, east, west_gain, east_gain)
        lam = (out,)
    half = (levels, lon_cells * lat_cells // 2)
    mine, other = call(
        lay_kernel,
        (place, out),
        [SMEM, VMEM],
        [(half, bf16)] * 2,
        scratch=[pltpu.VMEM((levels * lon_cells, LANES), f32)] * (lat_cells // LANES),
        moved=3 << 20,
    )
    edge = (sea_ext, out_low, out_high, west, east)
    mine, other, low, high = call(
        fix_kernel,
        (place, *edge, mine, other),
        [SMEM] + [VMEM] * 7,
        [(half, bf16)] * 2 + [(extended, f32)] * 2,
        aliases={5: 0, 6: 1},
    )
    (lam,) = call(
        emit_kernel,
        (out, low, high),
        [VMEM] * 3,
        [((levels, lon_cells, lat_cells), f32)],
        moved=3 << 20,
    )
    return lam, mine, other


def against(a, b):
    return lax.dot_general(a, b, (((1,), (1,)), ((), ())), preferred_element_type=jnp.float32)


def rows_kernel(wide, place, left, left_pair, first, second, kept, sent):
    half = left_pair.shape[1]
    levels = first.shape[0]
    sums = [None, None]
    for at in range(0, half, wide):
        lanes = slice(at, at + wide)
        mine = left[:, pl.ds(pl.multiple_of(place[1] * half + at, LANES), wide)]
        both = jnp.concatenate([first[:, lanes], second[:, lanes]], 0)
        for c, factor in enumerate((mine, left_pair[:, lanes])):
            term = against(factor, both)
            sums[c] = term if at == 0 else sums[c] + term
    for c in range(2):
        kept[c] = sums[c]
        other_order = [sums[c][:, levels:], sums[c][:, :levels]]
        sent[1 - c] = jnp.concatenate(other_order, 1).astype(jnp.bfloat16)


def mask_kernel(slots, place, ranks, *rest):
    stages = [rest[n : n + 2] for n in range(0, STAGES * 2, 2)]
    out = rest[STAGES * 2 :]
    rows = stages[0][0].shape[1] // slots
    for c in range(2):
        owner = place[0] if c == 0 else place[0] + 1 - 2 * place[1]
        for k in range(slots):
            at = slice(k * rows, (k + 1) * rows)
            value = jnp.concatenate(
                [kept[c, at, :] + arrived[c, at, :].astype(jnp.float32) for kept, arrived in stages], 1
            )
            row = lax.broadcasted_iota(jnp.int32, value.shape, 0) + owner * rows
            value = jnp.where(row < ranks[:1, k : k + 1], value, 0.0).astype(jnp.bfloat16)
            if len(out) > 1:
                out[k][c] = value
            else:
                count = out[0].shape[0]
                out[0][lax.rem(place[2] + (k - slots // 2 + count), count), c] = value


def columns_kernel(slots, stage, start, place, right, *rest):
    pieces = PARTS // HALVES
    right_pair, received, out = rest[:pieces], rest[pieces:-2], rest[-2:]
    count = received[0].shape[0]
    levels = out[0].shape[0]
    wide = right_pair[0].shape[1]
    half = wide * PARTS
    picked = slice(stage * levels, (stage + 2) * levels)
    coeffs = []
    for c in range(2):
        for k in range(slots):
            if len(received) > 1:
                coeffs.append(received[k][c, :, picked])
            else:
                source = lax.rem(place[2] + (count + slots // 2 - k), count)
                coeffs.append(received[0][source, c, :, picked])
    stacked = jnp.concatenate(coeffs, 0)
    rows = right.shape[0]
    lead = (((0,), (0,)), ((), ()))
    for n, piece in enumerate(right_pair):
        lanes = slice(n * wide, (n + 1) * wide)
        mine = right[:, pl.ds(pl.multiple_of(place[1] * half + start + n * wide, LANES), wide)]
        total = lax.dot_general(stacked[:rows], mine, lead, preferred_element_type=jnp.float32)
        total = total + lax.dot_general(stacked[rows:], piece[...], lead, preferred_element_type=jnp.float32)
        out[0][:, lanes] = total[:levels].astype(out[0].dtype)
        out[1][:, lanes] = total[levels:].astype(out[1].dtype)


def add_rows(place, own, arrived1, arrived2, arrived3, rows):
    levels = own.shape[0]
    each = rows[0].shape[0] // levels // 2
    f32 = jnp.float32
    wide = own.shape[1] // each
    for x in range(each):
        for c, lanes in enumerate(rows):
            cols = slice(x * wide + c * LANES, x * wide + (c + 1) * LANES)
            mine = own[:, cols] + arrived2[:, cols].astype(f32)
            other = arrived1[:, cols].astype(f32) + arrived3[:, cols].astype(f32)
            lanes[pl.ds(place[1] * each + x, levels, stride=2 * each), :] = mine
            lanes[pl.ds((1 - place[1]) * each + x, levels, stride=2 * each), :] = other


def early_kernel(place, own, arrived1, arrived2, arrived3, *rows):
    add_rows(place, own, arrived1, arrived2, arrived3, rows)


def join_kernel(place, own, arrived1, arrived2, arrived3, *rest):
    early = rest[:LANE_TILES]
    out, slab, sem, *rows = rest[LANE_TILES:]
    add_rows(place, own, arrived1, arrived2, arrived3, rows)
    levels, lon_cells, _ = slab.shape
    half = lon_cells // 2
    each = half // 2
    lower = lax.broadcasted_iota(jnp.int32, (half, LANES), 0) < each
    parts = 4
    size = levels // parts
    copies = []
    for part in range(parts):
        for z in range(part * size, (part + 1) * size):
            for c in range(LANE_TILES):
                a = early[c][z * half : (z + 1) * half, :]
                b = rows[c][z * half : (z + 1) * half, :]
                lanes = slice(c * LANES, (c + 1) * LANES)
                slab[z, :half, lanes] = jnp.where(lower, a, pltpu.roll(b, each, 0))
                slab[z, half:, lanes] = jnp.where(lower, pltpu.roll(a, each, 0), b)
        here = pl.ds(part * size, size)
        copies.append(pltpu.make_async_copy(slab.at[here], out.at[here], sem.at[part]))
        copies[-1].start()
    for copy in copies:
        copy.wait()


HERE = object()


def located(kernel):
    def run(*refs):
        me = lax.axis_index("depth")
        return kernel((me, lax.rem(me, 2), lax.axis_index("lon")), *refs)

    return run


def call(kernel, operands, in_specs, outs, grant=GRANT, flops=0, moved=1 << 20, scratch=(), aliases=None):
    if operands[0] is HERE:
        kernel, operands, in_specs = located(kernel), operands[1:], in_specs[1:]
    return pl.pallas_call(
        kernel,
        in_specs=in_specs,
        out_shape=[jax.ShapeDtypeStruct(*o[:2]) for o in outs],
        out_specs=[o[2] if len(o) > 2 else VMEM for o in outs],
        scratch_shapes=list(scratch),
        input_output_aliases=aliases or {},
        compiler_params=pltpu.CompilerParams(vmem_limit_bytes=grant),
        cost_estimate=pl.CostEstimate(flops=flops, bytes_accessed=moved, transcendentals=0),
    )(*operands)


def per_device(
    innovations, courant, diffusivity, sea_bricks, tile_ranks, row_factors, column_factors
):
    levels, lon_cells, lat_cells = diffusivity.shape
    tile_cols = lon_cells * lat_cells
    half = tile_cols // 2
    slots = tile_ranks.shape[1]
    count = lax.axis_size("depth")
    lon_count = lax.axis_size("lon")
    f32, bf16 = jnp.float32, jnp.bfloat16
    left = row_factors.transpose(0, 1, 3, 2)
    right = column_factors.transpose(0, 1, 3, 2)
    width = left.shape[2]
    rows = slots * width

    down, up, sea = pack(innovations, courant, diffusivity, sea_bricks)
    place = HERE
    (left_other,) = call(
        left_kernel,
        (place, left),
        [SMEM, ANY],
        [((slots, width, half), bf16, ANY)],
        grant=WIDE_GRANT,
        moved=2 << 20,
        scratch=[pltpu.VMEM((1, slots, width, half), bf16), pltpu.SemaphoreType.DMA((2, slots))],
    )
    before = from_behind(down, "depth", 1)
    after = from_behind(up, "depth", -1)
    inputs = (innovations, courant, diffusivity)
    inputs = call(
        load_kernel,
        inputs,
        [ANY] * 3,
        [(a.shape, a.dtype) for a in inputs],
        grant=LOAD_GRANT,
        moved=18 << 20,
        scratch=[pltpu.SemaphoreType.DMA((sum(a.shape[0] if a.ndim > 3 else 1 for a in inputs),))],
    )
    right_other = call(
        halves_kernel,
        (place, right),
        [SMEM, ANY],
        [((slots, width, half // PARTS), bf16, ANY)] * PARTS,
        moved=4 << 20,
        scratch=[pltpu.VMEM((PARTS, slots, width, half // PARTS), bf16), pltpu.SemaphoreType.DMA((2 * PARTS,))],
    )
    left_pair = swapped(left_other, "depth", 1)
    right_pair = []
    for part in range(PARTS):
        right_pair.append(swapped(right_other[part], "depth", 1).reshape(rows, half // PARTS))
    lam, lam_mine, lam_other = sweep(inputs, sea, before, after, place)
    left_pair = left_pair.reshape(rows, half)
    left, right = left.reshape(rows, tile_cols), right.reshape(rows, tile_cols)
    blocks = {0: lam_mine}
    for mask in range(count - 1, 0, -1):
        blocks[mask] = swapped(lam_other if mask % 2 else lam_mine, "depth", mask)
    sums = []
    for stage in range(0, count, 2):
        pair = (2, rows, 2 * levels)
        kept, sent = call(
            functools.partial(rows_kernel, 4 * LANES),
            (place, left, left_pair, blocks[stage], blocks[stage + 1]),
            [SMEM] + [VMEM] * 4,
            [(pair, f32), (pair, bf16)],
            flops=8 * rows * half * levels,
            moved=3 << 20,
        )
        sums += [kept, swapped(sent, "depth", 1)]
    grouped = False
    slot = (2, width, count * levels)
    coeff = call(
        functools.partial(mask_kernel, slots),
        (place, tile_ranks, *sums),
        [SMEM, VMEM] + [VMEM] * len(sums),
        [((lon_count,) + slot, bf16)] if grouped else [(slot, bf16)] * slots,
    )
    if grouped:
        received = [lax.all_to_all(coeff[0], "lon", 0, 0, tiled=True)]
    else:
        received = [shifted(coeff[k], "lon", k - slots // 2) for k in range(slots)]
    arrived = {mask: [] for mask in range(count)}
    block = (levels, half // HALVES)
    pieces = PARTS // HALVES
    for part in range(HALVES):
        for stage in range(count - 2, -1, -2):
            first, second = call(
                functools.partial(columns_kernel, slots, stage, part * (half // HALVES)),
                (place, right, *right_pair[part * pieces : (part + 1) * pieces], *received),
                [SMEM] + [VMEM] * (1 + pieces + len(received)),
                [(block, bf16 if stage else f32), (block, bf16)],
                flops=8 * rows * half * levels // HALVES,
                moved=2 << 20,
            )
            arrived[stage + 1].append(swapped(second, "depth", stage + 1))
            if stage:
                first = swapped(first, "depth", stage)
            arrived[stage].append(first)
    rows_of = (levels * lon_cells // 2, LANES)
    pieces = [[arrived[mask][part] for mask in range(count)] for part in range(HALVES)]
    early = call(
        early_kernel,
        (place, *pieces[0]),
        [SMEM] + [VMEM] * count,
        [(rows_of, f32)] * LANE_TILES,
        moved=2 << 20,
    )
    (gradient,) = call(
        join_kernel,
        (place, *pieces[1], *early),
        [SMEM] + [VMEM] * (count + LANE_TILES),
        [((levels, lon_cells, lat_cells), f32, ANY)],
        scratch=[pltpu.VMEM((levels, lon_cells, lat_cells), f32), pltpu.SemaphoreType.DMA((4,))]
        + [pltpu.VMEM(rows_of, f32)] * LANE_TILES,
        moved=3 << 20,
    )
    return (lam, gradient)


def solution(mesh):
    placed = (
        P(None, "depth", "lon", None),
        P(None, "depth", "lon", None),
        P("depth", "lon", None),
        P("depth", "lon", None),
        P("lon", None),
        P("lon", None, None, "depth"),
        P("lon", None, None, "depth"),
    )
    return jax.shard_map(
        per_device,
        mesh=mesh,
        in_specs=placed,
        out_specs=(P("depth", "lon", None), P("depth", "lon", None)),
        check_vma=False,
    )
```
